32 devices in a mesh: groups: 2 (over y), seq: 4 (over z), head: 2 (over x), sub: 2 (over core).
Axes of the slice: x: 2, y: 2, z: 4, core: 2. Of those that a mesh axis runs over, the one named last changes fastest.
Arguments:
- x_raw: bfloat16 [4096, 16384], P(('groups', 'seq'), ('head', 'sub')), parts along dimension 0, may hold values from -6 to 6
- bc_raw: bfloat16 [4096, 2, 1024], P(('groups', 'seq'), None, ('head', 'sub')), parts along dimension 0, may hold values from -6 to 6
- dt_raw: float32 [128, 4096], P(('head', 'sub'), ('groups', 'seq')), parts along dimension 1, may hold values from -3 to 3
- dt_bias: float32 [128], P(('head', 'sub')), may hold values from -3.8 to -3.2
- a_log: float32 [128], P(('head', 'sub')), may hold values from -12 to 1
- d_skip: float32 [128], P(('head', 'sub')), may hold values from 0 to 2.5
- conv_x: float32 [4, 16384], P(None, ('head', 'sub')), may hold values from -3 to 3
- conv_x_bias: float32 [16384], P(('head', 'sub')), may hold values from -0.8 to -0.3
- conv_bc: float32 [4, 2, 1024], P(None, None, ('head', 'sub')), may hold values from -1.5 to 1.5
- conv_bc_bias: float32 [2, 1024], P(None, ('head', 'sub')), may hold values from -0.35 to 0.05
- doc_starts: int32 [8], P('groups'), parts along dimension 0, may hold values from 0 to 1792, as said below
Outputs:
- scan_output: bfloat16 [4096, 16384], P(('groups', 'seq'), ('head', 'sub')), parts along dimension 0
The draws below stay inside these ranges and needn't reach their ends.
There are 2 independent parts, one for each index of `groups`. The reference program is written for one: setup_inputs(seed, part) draws one part's arguments, and reference() takes and returns one part's arrays. A program takes and returns all parts, laid end to end along the dimension named above; an argument that names none is the same for every part. Nothing has to cross between parts.
Inputs may be any that keep to these rules, and one draw needn't show every extreme that they name: doc_starts[0] is 0 and the entries rise strictly; the last entry is 1792; document j runs from doc_starts[j] up to the next entry, the last one up to 2048.
All inputs are finite; a program needn't handle non-finite values.
Results may differ from the reference program's by a relative error of at most 0.0048.
Values may be sent and summed in bfloat16 or wider, within the bound.
No kernel may reach another device: no remote copies, remote signals or barrier semaphores. Data moves between devices by JAX's collectives and lax.ppermute only.
A program may use at most 128 MiB of HBM per device.

```python
import math
import jax
import jax.numpy as jnp
from jax import lax

STATE_HEADS = 128
P_SIZE = 128
N = 128
G = 8
K = 4
BLK = 512
NDOCS = 4
TOK_DEV = 512
SEQUENCE_TOKENS = 2048


def draw_dt_raw(key, part):
    noise_random_key, shift_random_key = jax.random.split(key, 2)
    jitter = jnp.clip(0.4 * jax.random.normal(noise_random_key, (STATE_HEADS, SEQUENCE_TOKENS), jnp.float32), -1.6, 1.6)
    offsets = jax.random.uniform(shift_random_key, (STATE_HEADS, SEQUENCE_TOKENS // TOK_DEV), jnp.float32, -0.7, 0.7)
    return jitter + jnp.repeat(offsets, TOK_DEV, axis=1)


def draw_a_log(key, part):
    pick_key, fast_key, slow_key = jax.random.split(key, 3)
    fast_share = 50
    chosen = jax.random.randint(pick_key, (STATE_HEADS,), 0, 100) < fast_share
    fast_log = jax.random.uniform(fast_key, (STATE_HEADS,), jnp.float32, math.log(0.003), math.log(1.5))
    slow_log = jax.random.uniform(slow_key, (STATE_HEADS,), jnp.float32, math.log(0.1), math.log(0.5)) - math.log(0.035 * SEQUENCE_TOKENS)
    return jnp.where(chosen, fast_log, slow_log)


def draw_doc_starts(key, part):
    early_key, late_key = jax.random.split(key, 2)
    last_start = SEQUENCE_TOKENS - TOK_DEV // 2
    early = jax.random.randint(early_key, (1,), 1, TOK_DEV).astype(jnp.int32)
    late = jax.random.permutation(late_key, 3 * TOK_DEV // 2)[:NDOCS - 3].astype(jnp.int32) + (SEQUENCE_TOKENS - 2 * TOK_DEV)
    return jnp.concatenate([jnp.zeros((1,), jnp.int32), early, jnp.sort(late).astype(jnp.int32), jnp.full((1,), last_start, jnp.int32)])


def block_scale(own_key, dims, cuts, smallest, high):
    level, own = 1.0, jax.random.fold_in(own_key, 6)
    for dim, shards_of in cuts:
        steps = jnp.exp(jax.random.uniform(jax.random.fold_in(own, dim), (shards_of,), jnp.float32, smallest / len(cuts), high / len(cuts)))
        level = level * jnp.repeat(steps, dims[dim] // shards_of).reshape([-1 if axis == dim else 1 for axis in range(len(dims))])
    return level


def scatter_about(rng, dims, deviation, most, cuts=(), kind=jnp.bfloat16):
    factor_of = block_scale(rng, dims, cuts, -0.22, 0.18) if cuts else 1.0
    result = jax.random.normal(rng, dims, jnp.float32) * deviation * factor_of
    return jnp.minimum(jnp.maximum(result, -most), most).astype(kind)


def setup_inputs(seed: int = 0, part: int = 0) -> dict:
    seeds = jax.random.split(jax.random.key(seed), 12)
    own_keys = jax.random.split(jax.random.fold_in(seeds[11], part), 12)
    x_raw = scatter_about(own_keys[0], (SEQUENCE_TOKENS, STATE_HEADS * P_SIZE), 1.0, 6.0, ((0, 4), (1, 4)))
    bc_raw = scatter_about(own_keys[1], (SEQUENCE_TOKENS, 2, G * N), 1.0, 6.0, ((0, 4), (2, 4)))
    dt_raw = draw_dt_raw(jax.random.fold_in(jax.random.fold_in(seeds[11], part), 71), part)
    dt_bias = jnp.clip(-3.8 + 0.5999999 * jax.random.uniform(seeds[3], (STATE_HEADS,), jnp.float32) ** block_scale(seeds[3], (STATE_HEADS,), ((0, 4),), -0.2, 0.2), -3.8, -3.2)
    a_log = draw_a_log(jax.random.fold_in(seeds[11], 71), part)
    d_skip = jnp.clip(2.5 * jax.random.uniform(seeds[5], (STATE_HEADS,), jnp.float32) ** block_scale(seeds[5], (STATE_HEADS,), ((0, 4),), -0.2, 0.2), 0.0, 2.5)
    conv_x = scatter_about(seeds[6], (K, STATE_HEADS * P_SIZE), 0.5, 3.0, ((1, 4),), jnp.float32)
    conv_x_bias = jnp.clip(-0.8 + 0.5 * jax.random.uniform(seeds[7], (STATE_HEADS * P_SIZE,), jnp.float32) ** block_scale(seeds[7], (STATE_HEADS * P_SIZE,), ((0, 4),), -0.2, 0.2), -0.8, -0.3)
    conv_bc = scatter_about(seeds[8], (K, 2, G * N), 0.25, 1.5, ((2, 4),), jnp.float32)
    conv_bc_bias = jnp.clip(-0.35 + 0.4 * jax.random.uniform(seeds[9], (2, G * N), jnp.float32) ** block_scale(seeds[9], (2, G * N), ((1, 4),), -0.2, 0.2), -0.35, 0.05)
    doc_starts = draw_doc_starts(jax.random.fold_in(jax.random.fold_in(seeds[11], part), 71), part)
    return {"x_raw": x_raw, "bc_raw": bc_raw, "dt_raw": dt_raw, "dt_bias": dt_bias, "a_log": a_log, "d_skip": d_skip, "conv_x": conv_x, "conv_x_bias": conv_x_bias, "conv_bc": conv_bc, "conv_bc_bias": conv_bc_bias, "doc_starts": doc_starts}


def segment_ids(positions, doc_starts):
    counted = jnp.sum((doc_starts[None, :] <= positions[:, None]).astype(jnp.int32), axis=1)
    return (counted - 1).astype(jnp.int32)


def convolve(extended, weight, bias_row, same_doc):
    row_count = same_doc.shape[1]
    mask_shape = (row_count,) + (1,) * (extended.ndim - 1)
    summed = jnp.where(same_doc[0].reshape(mask_shape), weight[0] * extended[0:row_count].astype(jnp.float32), 0.0)
    for tap_index in range(1, weight.shape[0]):
        tap_term = weight[tap_index] * extended[tap_index:tap_index + row_count].astype(jnp.float32)
        summed = summed + jnp.where(same_doc[tap_index].reshape(mask_shape), tap_term, 0.0)
    return jax.nn.silu(summed + bias_row)


def block_terms(mixed_x, mixed_bc, rate_block, step_block, doc_block, doc_before):
    row_count = mixed_x.shape[0]
    group_count = rate_block.shape[0]
    per_group = rate_block.shape[1]
    x_four = mixed_x.reshape(row_count, group_count, per_group, P_SIZE).astype(jnp.float32)
    b_groups = mixed_bc[:, 0, :].reshape(row_count, group_count, N).astype(jnp.float32)
    c_groups = mixed_bc[:, 1, :].reshape(row_count, group_count, N).astype(jnp.float32)
    cum_rates = jnp.cumsum(rate_block, axis=2)
    row_order = jnp.arange(row_count)
    causal_mask = (row_order[:, None] >= row_order[None, :]) & (doc_block[:, None] == doc_block[None, :])
    scores = jnp.einsum("tgn,sgn->gts", c_groups, b_groups)
    log_gaps = jnp.where(causal_mask, cum_rates[:, :, :, None] - cum_rates[:, :, None, :], -jnp.inf)
    weights = (scores[:, None] * jnp.exp(log_gaps) * step_block[:, :, None, :]).astype(jnp.bfloat16)
    inner_terms = jnp.einsum("gits,sgip->tgip", weights.astype(jnp.float32), x_four)
    last_cum = cum_rates[:, :, row_count - 1:]
    tail_factor = jnp.exp(jnp.where(doc_block == doc_block[row_count - 1], last_cum - cum_rates, -jnp.inf)) * step_block
    b_moved = jnp.transpose(b_groups, (1, 0, 2))
    tail_weights = (b_moved[:, None] * tail_factor[..., None]).astype(jnp.bfloat16)
    block_state = jnp.einsum("gisn,sgip->gipn", tail_weights.astype(jnp.float32), x_four)
    block_decay = jnp.where(doc_block[row_count - 1] == doc_before, jnp.exp(last_cum[:, :, 0]), 0.0)
    entry_factor = jnp.where(doc_block == doc_before, jnp.exp(cum_rates), 0.0)
    return inner_terms, block_state, block_decay, entry_factor


def block_output(inner_terms, entry_factor, mixed_bc, carried, mixed_x, skip_four):
    row_count = mixed_x.shape[0]
    group_count = carried.shape[0]
    c_float = mixed_bc[:, 1, :].reshape(row_count, group_count, N).astype(jnp.float32)
    from_before = jnp.einsum("tgn,gipn->tgip", c_float, carried, precision=lax.Precision.HIGHEST)
    x_four = mixed_x.reshape(row_count, group_count, -1, P_SIZE)
    summed = inner_terms + from_before * jnp.transpose(entry_factor, (2, 0, 1))[..., None] + skip_four[None, :, :, None] * x_four.astype(jnp.float32)
    return summed.astype(jnp.bfloat16).reshape(row_count, -1)


def reference(x_raw, bc_raw, dt_raw, dt_bias, a_log, d_skip, conv_x, conv_x_bias, conv_bc, conv_bc_bias, doc_starts):
    tap_count = conv_x.shape[0]
    per_group = STATE_HEADS // G
    block_count = SEQUENCE_TOKENS // BLK
    positions = jnp.arange(SEQUENCE_TOKENS, dtype=jnp.int32)
    doc_rows = segment_ids(positions, doc_starts)
    step_sizes = jax.nn.softplus(dt_raw + dt_bias[:, None])
    log_rates = -jnp.exp(a_log)[:, None] * step_sizes
    skip_four = d_skip.reshape(G, per_group)

    def by_block(values):
        return jnp.transpose(values.reshape(G, per_group, block_count, BLK), (2, 0, 1, 3))

    def step_block_fn(carry, packed):
        carried, x_rim, bc_rim, doc_rim = carry
        x_block, bc_block, rate_block, dt_block, doc_block = packed
        doc_ext = jnp.concatenate([doc_rim, doc_block])
        same_doc = jnp.stack([doc_ext[tap_index:tap_index + BLK] == doc_block for tap_index in range(tap_count)])
        mixed_x = convolve(jnp.concatenate([x_rim, x_block], axis=0), conv_x, conv_x_bias, same_doc).astype(jnp.bfloat16)
        mixed_bc = convolve(jnp.concatenate([bc_rim, bc_block], axis=0), conv_bc, conv_bc_bias, same_doc).astype(jnp.bfloat16)
        doc_before = doc_rim[tap_count - 2]
        inner_terms, block_state, block_decay, entry_factor = block_terms(mixed_x, mixed_bc, rate_block, dt_block, doc_block, doc_before)
        rows_out = block_output(inner_terms, entry_factor, mixed_bc, carried, mixed_x, skip_four)
        next_carried = block_decay[:, :, None, None] * carried + block_state
        keep_from = BLK - tap_count + 1
        return (next_carried, x_block[keep_from:], bc_block[keep_from:], doc_block[keep_from:]), rows_out

    start_carry = (jnp.zeros((G, per_group, P_SIZE, N), jnp.float32),
                   jnp.zeros((tap_count - 1, STATE_HEADS * P_SIZE), jnp.bfloat16),
                   jnp.zeros((tap_count - 1, 2, G * N), jnp.bfloat16),
                   jnp.full((tap_count - 1,), -1, jnp.int32))
    packed_inputs = (x_raw.reshape(block_count, BLK, STATE_HEADS * P_SIZE), bc_raw.reshape(block_count, BLK, 2, G * N),
                     by_block(log_rates), by_block(step_sizes), doc_rows.reshape(block_count, BLK))
    unused, outputs = lax.scan(step_block_fn, start_carry, packed_inputs)
    return outputs.reshape(SEQUENCE_TOKENS, STATE_HEADS * P_SIZE)
```

```python
import functools
import math

import jax
import jax.numpy as jnp
from jax import lax
from jax.experimental import pallas as pl
from jax.experimental.pallas import tpu as pltpu
from jax.sharding import PartitionSpec as P

D = 128
Q = 128
BLK = 512
NQ = BLK // Q
HC = 4
CW = HC * D
RIM = 8
LOG2E = math.log2(math.e)
F32 = jnp.float32
BF16 = jnp.bfloat16


def doc_of(pos, starts_ref):
    count = jnp.zeros_like(pos)
    for j in range(starts_ref.shape[0]):
        count = count + (pos >= starts_ref[j]).astype(jnp.int32)
    return count - 1


def silu_half(u):
    return u + u * jnp.tanh(u)


def params_kernel(row_ref, starts_ref, dt_ref, bias_ref, alog_ref, cols_ref, rows_ref, dec_ref, mask_ref):
    first = row_ref[0]
    heads = dt_ref.shape[0]
    v = dt_ref[...] + bias_ref[...]
    step = jnp.maximum(v, 0.0) + jnp.log(1.0 + jnp.exp(-jnp.abs(v)))
    rate = -jnp.exp(alog_ref[...]) * step
    tri = (
        lax.broadcasted_iota(jnp.int32, (Q, Q), 0) <= lax.broadcasted_iota(jnp.int32, (Q, Q), 1)
    ).astype(F32)
    doc_before = doc_of(first - 1, starts_ref)
    base = jnp.zeros((heads, 1), F32)
    for q in range(NQ):
        span = slice(q * Q, (q + 1) * Q)
        cum = jnp.dot(rate[:, span], tri, precision=lax.Precision.HIGHEST, preferred_element_type=F32)
        last = cum[:, Q - 1 : Q]
        step_q = step[:, span]
        pos = first + q * Q + lax.broadcasted_iota(jnp.int32, (1, Q), 1)
        doc = doc_of(pos, starts_ref)
        doc_prev = doc_of(first + q * Q - 1, starts_ref)
        doc_end = doc_of(first + (q + 1) * Q - 1, starts_ref)
        tail = jnp.where(doc == doc_end, jnp.exp(last - cum) * step_q, 0.0)
        entry = jnp.where(doc == doc_prev, jnp.exp(cum), 0.0)
        far = jnp.where(doc == doc_before, jnp.exp(cum + base), 0.0)
        packed = [tail, cum * LOG2E, entry, far]
        if 4 * heads < D:
            packed.append(jnp.zeros((D - 4 * heads, Q), F32))
        cols_ref[span, :] = jnp.transpose(jnp.concatenate(packed, axis=0), (1, 0))
        rows_ref[:, span] = (cum - jnp.log(step_q)) * LOG2E
        keep = jnp.where(doc_end == doc_prev, 1.0, 0.0)
        dec_ref[:, q : q + 1] = jnp.exp(last) * keep
        base = base + last
    doc_last = doc_of(first + BLK - 1, starts_ref)
    dec_ref[:, NQ : NQ + 1] = jnp.exp(base) * jnp.where(doc_last == doc_before, 1.0, 0.0)
    dec_ref[:, NQ + 1 :] = jnp.zeros((heads, dec_ref.shape[1] - NQ - 1), F32)
    for k in range(3):
        pos = first + lax.broadcasted_iota(jnp.int32, (BLK, D), 0)
        same = doc_of(pos, starts_ref) == doc_of(pos - (3 - k), starts_ref)
        mask_ref[k] = same.astype(F32)


def fill(buf_ref, rim_ref, x_ref):
    buf_ref[0:RIM, :] = rim_ref[...].astype(F32)
    for r in range(0, BLK, Q):
        buf_ref[RIM + r : RIM + r + Q, :] = x_ref[r : r + Q, :].astype(F32)


def conv_tile(buf_ref, w_ref, b_ref, mask_ref, r, lanes):
    total = 0.5 * w_ref[3:4, lanes] * buf_ref[pl.ds(RIM + r, Q), lanes] + 0.5 * b_ref[0:1, lanes]
    for k in range(3):
        term = 0.5 * w_ref[k : k + 1, lanes] * buf_ref[pl.ds(RIM - 3 + k + r, Q), lanes]
        total = total + mask_ref[k, r : r + Q, :] * term
    return silu_half(total).astype(BF16)


def state_kernel(
    row_ref, starts_ref, dec_ref, x_ref, rim_ref, wx_ref, bx_ref, mask_ref, cols_ref,
    bc_ref, rimbc_ref, wbc_ref, bbc_ref,
    mx_ref, enter_ref, end_ref, c_ref, score_ref,
    buf_ref, scaled_ref, bt_ref, *, groups, per_group,
):
    c = pl.program_id(0)
    heads = groups * per_group * HC

    @pl.when(c == 0)
    def first():
        first_row = row_ref[0]
        for part in range(2):
            for g in range(groups):
                lo = (part * groups + g) * D
                lanes = slice(lo, lo + D)
                buf_ref[0:RIM, 0:D] = rimbc_ref[:, lanes].astype(F32)
                buf_ref[RIM : RIM + BLK, 0:D] = bc_ref[:, lanes].astype(F32)
                for r in range(0, BLK, Q):
                    total = 0.5 * wbc_ref[3:4, lanes] * buf_ref[pl.ds(RIM + r, Q), 0:D]
                    total = total + 0.5 * bbc_ref[0:1, lanes]
                    for k in range(3):
                        term = 0.5 * wbc_ref[k : k + 1, lanes] * buf_ref[pl.ds(RIM - 3 + k + r, Q), 0:D]
                        total = total + mask_ref[k, r : r + Q, :] * term
                    mixed = silu_half(total)
                    if part == 0:
                        bt_ref[g, :, r : r + Q] = jnp.transpose(mixed, (1, 0)).astype(BF16)
                    else:
                        c_ref[r : r + Q, g * D : (g + 1) * D] = mixed.astype(BF16)
        for q in range(NQ):
            at = first_row + q * Q
            row = at + lax.broadcasted_iota(jnp.int32, (Q, Q), 0)
            col = at + lax.broadcasted_iota(jnp.int32, (Q, Q), 1)
            keep = (row >= col) & (doc_of(row, starts_ref) == doc_of(col, starts_ref))
            for g in range(groups):
                score = jnp.dot(
                    c_ref[q * Q : (q + 1) * Q, g * D : (g + 1) * D],
                    bt_ref[g, :, q * Q : (q + 1) * Q],
                    preferred_element_type=F32,
                )
                score_ref[q * Q : (q + 1) * Q, g * D : (g + 1) * D] = jnp.where(keep, score, 0.0)

    fill(buf_ref, rim_ref, x_ref)
    shift = lax.rem(D - HC * c, D)
    for q in range(NQ):
        r = q * Q
        cols = pltpu.roll(cols_ref[r : r + Q, :], shift, 1)
        for i in range(HC):
            lanes = slice(i * D, (i + 1) * D)
            mixed = conv_tile(buf_ref, wx_ref, bx_ref, mask_ref, r, lanes)
            mx_ref[r : r + Q, lanes] = mixed
            scaled_ref[r : r + Q, lanes] = (mixed.astype(F32) * cols[:, i : i + 1]).astype(BF16)
    g = lax.div(c, per_group)
    for q in range(NQ):
        part = jnp.dot(
            bt_ref[g, :, q * Q : (q + 1) * Q],
            scaled_ref[q * Q : (q + 1) * Q, :],
            preferred_element_type=F32,
        )
        for i in range(HC):
            lanes = slice(i * D, (i + 1) * D)
            if q == 0:
                end_ref[:, lanes] = part[:, lanes]
            else:
                before = end_ref[:, lanes]
                enter_ref[q - 1, :, lanes] = before.astype(BF16)
                end_ref[:, lanes] = dec_ref[c * HC + i, q] * before + part[:, lanes]


def intra_kernel(skip_ref, mx_ref, enter_ref, c_ref, score_ref, cols_ref, rows_ref, y_ref, *, heads):
    c = pl.program_id(0)
    shift = lax.rem(D - HC * c, D)
    for q in range(NQ):
        r = q * Q
        cols = pltpu.roll(cols_ref[r : r + Q, :], shift, 1)
        score = score_ref[r : r + Q, :]
        both = rows_ref[pl.ds(pl.multiple_of(2 * HC * lax.div(c, 2), 2 * HC), 2 * HC), r : r + Q]
        terms = jnp.where(lax.rem(c, 2) == 0, both[:HC], both[HC:])
        if q:
            far = jnp.dot(c_ref[r : r + Q, :], enter_ref[q - 1], preferred_element_type=F32)
        for i in range(HC):
            lanes = slice(i * D, (i + 1) * D)
            head = c * HC + i
            gap = cols[:, heads + i : heads + i + 1] - terms[i : i + 1]
            weight = (score * jnp.exp2(jnp.minimum(gap, 100.0))).astype(BF16)
            x = mx_ref[r : r + Q, lanes]
            y = jnp.dot(weight, x, preferred_element_type=F32) + skip_ref[head] * x.astype(F32)
            if q:
                y = y + cols[:, 2 * heads + i : 2 * heads + i + 1] * far[:, lanes]
            y_ref[r : r + Q, lanes] = y.astype(BF16)


def start_kernel(table_ref, end_ref, send_ref):
    send_ref[...] = end_ref[...].astype(BF16)


def pass_kernel(table_ref, dec_ref, recv_ref, end_ref, held_ref, send_ref, keep_ref, *, turn, stream, per_stream):
    chunk = stream * per_stream + table_ref[2 * turn]
    for i in range(HC):
        lanes = slice(i * D, (i + 1) * D)
        got = recv_ref[:, lanes]
        keep_ref[:, lanes] = got
        send_ref[:, lanes] = (
            dec_ref[chunk * HC + i, NQ] * got.astype(F32) + end_ref[:, lanes]
        ).astype(BF16)


def keep_kernel(table_ref, recv_ref, held_ref, keep_ref):
    keep_ref[...] = recv_ref[...]


def final_kernel(y_ref, c_ref, cols_ref, held0_ref, held1_ref, out_ref, *, heads, per_stream):
    c = pl.program_id(0)
    held = jnp.where(c < per_stream, held0_ref[...], held1_ref[...])
    shift = lax.rem(D - HC * c, D)
    for q in range(NQ):
        r = q * Q
        cols = pltpu.roll(cols_ref[r : r + Q, :], shift, 1)
        far = jnp.dot(c_ref[r : r + Q, :], held, preferred_element_type=F32)
        for i in range(HC):
            lanes = slice(i * D, (i + 1) * D)
            y = y_ref[r : r + Q, lanes].astype(F32)
            out_ref[r : r + Q, lanes] = (
                y + cols[:, 3 * heads + i : 3 * heads + i + 1] * far[:, lanes]
            ).astype(BF16)


SMEM = pl.BlockSpec(memory_space=pltpu.SMEM)
ANY = pl.BlockSpec(memory_space=pl.ANY)


def whole(shape):
    return pl.BlockSpec(shape, lambda c: (0,) * len(shape))


def shape_of(shape, dtype):
    return jax.ShapeDtypeStruct(shape, dtype)


def per_device(
    x_raw, bc_raw, dt_raw, dt_bias, a_log, d_skip, conv_x, conv_x_bias, conv_bc, conv_bc_bias, doc_starts
):
    rows, width = x_raw.shape
    groups = bc_raw.shape[2] // D
    heads = dt_raw.shape[0]
    chunks = heads // HC
    per_group = chunks // groups
    seq = lax.axis_size("seq")
    place = lax.axis_index("seq")
    first_row = (place * rows).astype(jnp.int32).reshape(1)
    ring = [(i, (i + 1) % seq) for i in range(seq)]

    bc = bc_raw.reshape(rows, -1)
    tail = jnp.concatenate([x_raw[rows - RIM :], bc_raw[rows - RIM :].reshape(RIM, -1)], axis=1)
    rim = lax.ppermute(tail, "seq", ring)

    cols, row_terms, dec, mask = pl.pallas_call(
        params_kernel,
        in_specs=[SMEM, SMEM] + [pl.BlockSpec(memory_space=pltpu.VMEM)] * 3,
        out_specs=[pl.BlockSpec(memory_space=pltpu.VMEM)] * 4,
        out_shape=[
            shape_of((BLK, D), F32),
            shape_of((heads, BLK), F32),
            shape_of((heads, 8), F32),
            shape_of((3, BLK, D), F32),
        ],
        name="params",
    )(first_row, doc_starts, dt_raw, dt_bias[:, None], a_log[:, None])

    mixed_x, enter, end, mixed_c, score = pl.pallas_call(
        functools.partial(state_kernel, groups=groups, per_group=per_group),
        grid=(chunks,),
        in_specs=[
            SMEM, SMEM, SMEM,
            pl.BlockSpec((BLK, CW), lambda c: (0, c)),
            pl.BlockSpec((RIM, CW), lambda c: (0, c)),
            pl.BlockSpec((4, CW), lambda c: (0, c)),
            pl.BlockSpec((1, CW), lambda c: (0, c)),
            whole((3, BLK, D)),
            whole((BLK, D)),
            whole((BLK, 2 * groups * D)),
            whole((RIM, 2 * groups * D)),
            whole((4, 2 * groups * D)),
            whole((1, 2 * groups * D)),
        ],
        out_specs=[
            pl.BlockSpec((BLK, CW), lambda c: (0, c)),
            pl.BlockSpec((NQ - 1, D, CW), lambda c: (0, 0, c)),
            pl.BlockSpec((D, CW), lambda c: (0, c)),
            whole((BLK, groups * D)),
            whole((BLK, groups * D)),
        ],
        out_shape=[
            shape_of((BLK, width), BF16),
            shape_of((NQ - 1, D, width), BF16),
            shape_of((D, width), F32),
            shape_of((BLK, groups * D), BF16),
            shape_of((BLK, groups * D), F32),
        ],
        scratch_shapes=[
            pltpu.VMEM((RIM + BLK, CW), F32),
            pltpu.VMEM((BLK, CW), BF16),
            pltpu.VMEM((groups, D, BLK), BF16),
        ],
        name="states",
    )(
        first_row, doc_starts, dec, x_raw, rim[:, :width], conv_x, conv_x_bias[None], mask, cols,
        bc, rim[:, width:], conv_bc.reshape(4, -1), conv_bc_bias.reshape(1, -1),
    )

    streams = 2
    per_stream = chunks // streams
    slots = per_stream + seq - 2
    turn_no = jnp.arange(slots + 1, dtype=jnp.int32) - place
    valid = (turn_no >= 0) & (turn_no < per_stream) & (place > 0)
    table = jnp.stack(
        [jnp.clip(turn_no, 0, per_stream - 1), jnp.where(valid, turn_no, per_stream)], axis=1
    ).astype(jnp.int32).reshape(-1)

    chunk_shape = shape_of((D, CW), BF16)
    held_shape = shape_of((D, (per_stream + 1) * CW), BF16)
    held = [jnp.zeros(held_shape.shape, BF16) for _ in range(streams)]
    flying = [None] * streams
    for s in range(streams):
        send = pl.pallas_call(
            start_kernel,
            grid_spec=pltpu.PrefetchScalarGridSpec(
                num_scalar_prefetch=1,
                grid=(1,),
                in_specs=[pl.BlockSpec((D, CW), lambda i, tab, s=s: (0, s * per_stream + tab[0]))],
                out_specs=pl.BlockSpec((D, CW), lambda i, tab: (0, 0)),
            ),
            out_shape=chunk_shape,
            name="start",
        )(table, end)
        flying[s] = lax.ppermute(send, "seq", ring)

    y = pl.pallas_call(
        functools.partial(intra_kernel, heads=heads),
        grid=(chunks,),
        in_specs=[
            SMEM,
            pl.BlockSpec((BLK, CW), lambda c: (0, c)),
            pl.BlockSpec((NQ - 1, D, CW), lambda c: (0, 0, c)),
            pl.BlockSpec((BLK, D), lambda c: (0, c // per_group)),
            pl.BlockSpec((BLK, D), lambda c: (0, c // per_group)),
            whole((BLK, D)),
            whole((heads, BLK)),
        ],
        out_specs=pl.BlockSpec((BLK, CW), lambda c: (0, c)),
        out_shape=shape_of((BLK, width), BF16),
        cost_estimate=pl.CostEstimate(flops=4 * BLK * Q * width, bytes_accessed=8 * BLK * width, transcendentals=0),
        name="intra",
    )(d_skip, mixed_x, enter, mixed_c, score, cols, row_terms)

    for turn in range(1, slots + 1):
        for s in range(streams):
            if turn == slots:
                held[s] = pl.pallas_call(
                    keep_kernel,
                    grid_spec=pltpu.PrefetchScalarGridSpec(
                        num_scalar_prefetch=1,
                        grid=(1,),
                        in_specs=[pl.BlockSpec((D, CW), lambda i, tab: (0, 0)), ANY],
                        out_specs=pl.BlockSpec((D, CW), lambda i, tab, t=turn: (0, tab[2 * t + 1])),
                    ),
                    out_shape=held_shape,
                    input_output_aliases={2: 0},
                    name="keep",
                )(table, flying[s], held[s])
                continue
            send, held[s] = pl.pallas_call(
                functools.partial(pass_kernel, turn=turn, stream=s, per_stream=per_stream),
                grid_spec=pltpu.PrefetchScalarGridSpec(
                    num_scalar_prefetch=1,
                    grid=(1,),
                    in_specs=[
                        SMEM,
                        pl.BlockSpec((D, CW), lambda i, tab: (0, 0)),
                        pl.BlockSpec((D, CW), lambda i, tab, t=turn, s=s: (0, s * per_stream + tab[2 * t])),
                        ANY,
                    ],
                    out_specs=[
                        pl.BlockSpec((D, CW), lambda i, tab: (0, 0)),
                        pl.BlockSpec((D, CW), lambda i, tab, t=turn: (0, tab[2 * t + 1])),
                    ],
                ),
                out_shape=[chunk_shape, held_shape],
                input_output_aliases={4: 1},
                name="pass",
            )(table, dec, flying[s], end, held[s])
            flying[s] = lax.ppermute(send, "seq", ring)

    return pl.pallas_call(
        functools.partial(final_kernel, heads=heads, per_stream=per_stream),
        grid=(chunks,),
        in_specs=[
            pl.BlockSpec((BLK, CW), lambda c: (0, c)),
            pl.BlockSpec((BLK, D), lambda c: (0, c // per_group)),
            whole((BLK, D)),
            pl.BlockSpec((D, CW), lambda c: (0, jnp.minimum(c, per_stream - 1))),
            pl.BlockSpec((D, CW), lambda c: (0, jnp.maximum(c - per_stream, 0))),
        ],
        out_specs=pl.BlockSpec((BLK, CW), lambda c: (0, c)),
        out_shape=shape_of((BLK, width), BF16),
        name="final",
    )(y, mixed_c, cols, held[0], held[1])


def solution(mesh):
    return jax.shard_map(
        per_device,
        mesh=mesh,
        in_specs=(
            P(("groups", "seq"), ("head", "sub")),
            P(("groups", "seq"), None, ("head", "sub")),
            P(("head", "sub"), ("groups", "seq")),
            P(("head", "sub")),
            P(("head", "sub")),
            P(("head", "sub")),
            P(None, ("head", "sub")),
            P(("head", "sub")),
            P(None, None, ("head", "sub")),
            P(None, ("head", "sub")),
            P("groups"),
        ),
        out_specs=P(("groups", "seq"), ("head", "sub")),
        check_vma=False,
    )
```

```python
import functools
import math

import jax
import jax.numpy as jnp
from jax import lax
from jax.experimental import pallas as pl
from jax.experimental.pallas import tpu as pltpu
from jax.sharding import PartitionSpec as P

D = 128
Q = 128
BLK = 512
NQ = BLK // Q
HC = 4
CW = HC * D
RIM = 8
LOG2E = math.log2(math.e)
F32 = jnp.float32
BF16 = jnp.bfloat16


def doc_of(pos, starts_ref):
    count = jnp.zeros_like(pos)
    for j in range(starts_ref.shape[0]):
        count = count + (pos >= starts_ref[j]).astype(jnp.int32)
    return count - 1


def silu_half(u):
    return u + u * jnp.tanh(u)


def doc_at(pos, starts_ref):
    count = jnp.int32(-1)
    for j in range(starts_ref.shape[0]):
        count = count + (pos >= starts_ref[j]).astype(jnp.int32)
    return count


def column_of(ref):
    heads = ref.shape[0]
    index = lax.broadcasted_iota(jnp.int32, (heads, 1), 0)
    column = jnp.zeros((heads, 1), F32)
    for h in range(heads):
        column = jnp.where(index == h, ref[h], column)
    return column


def split(value, parts):
    pieces = []
    for _ in range(parts - 1):
        piece = value.astype(BF16).astype(F32)
        pieces.append(piece)
        value = value - piece
    return pieces + [value]


def doc_at(pos, starts_ref):
    count = jnp.int32(-1)
    for j in range(starts_ref.shape[0]):
        count = count + (pos >= starts_ref[j]).astype(jnp.int32)
    return count


def column_of(ref):
    heads = ref.shape[0]
    index = lax.broadcasted_iota(jnp.int32, (heads, 1), 0)
    column = jnp.zeros((heads, 1), F32)
    for h in range(heads):
        column = jnp.where(index == h, ref[h], column)
    return column


def split(value, parts):
    pieces = []
    for _ in range(parts - 1):
        piece = value.astype(BF16).astype(F32)
        pieces.append(piece)
        value = value - piece
    return pieces + [value]


def doc_at(pos, starts_ref):
    count = jnp.int32(-1)
    for j in range(starts_ref.shape[0]):
        count = count + (pos >= starts_ref[j]).astype(jnp.int32)
    return count


def column_of(ref):
    heads = ref.shape[0]
    index = lax.broadcasted_iota(jnp.int32, (heads, 1), 0)
    column = jnp.zeros((heads, 1), F32)
    for h in range(heads):
        column = jnp.where(index == h, ref[h], column)
    return column


def split(value, parts):
    pieces = []
    for _ in range(parts - 1):
        piece = value.astype(BF16).astype(F32)
        pieces.append(piece)
        value = value - piece
    return pieces + [value]


def params_kernel(
    place_ref, starts_ref, bias_ref, alog_ref, skip_ref, dt_ref, scale_ref, cum_ref, rows_ref, dec_ref, shift_ref
):
    first = place_ref[0] * BLK
    heads = dt_ref.shape[0]
    v = dt_ref[...] + column_of(bias_ref)
    step = jnp.maximum(v, 0.0) + jnp.log(1.0 + jnp.exp(-jnp.abs(v)))
    rate = -jnp.exp(column_of(alog_ref)) * step
    tri = (
        lax.broadcasted_iota(jnp.int32, (Q, Q), 0) <= lax.broadcasted_iota(jnp.int32, (Q, Q), 1)
    ).astype(F32)
    doc_before = doc_at(first - 1, starts_ref)
    base = jnp.zeros((heads, 1), F32)
    dec_ref[...] = jnp.zeros_like(dec_ref)
    dec_ref[:, 2 * NQ : 2 * NQ + 1] = column_of(skip_ref)
    for q in range(NQ):
        span = slice(q * Q, (q + 1) * Q)
        cum = jnp.dot(rate[:, span], tri, precision=lax.Precision.HIGHEST, preferred_element_type=F32)
        last = cum[:, Q - 1 : Q]
        step_q = step[:, span]
        pos = first + q * Q + lax.broadcasted_iota(jnp.int32, (1, Q), 1)
        doc = doc_of(pos, starts_ref)
        doc_prev = doc_at(first + q * Q - 1, starts_ref)
        doc_end = doc_at(first + (q + 1) * Q - 1, starts_ref)
        tail = jnp.where(doc == doc_end, jnp.exp(last - cum) * step_q, 0.0)
        entry = jnp.where(doc == doc_prev, jnp.exp(cum), 0.0)
        packed = split(tail, 2) + split(entry, 2)
        if 4 * heads < D:
            packed.append(jnp.zeros((D - 4 * heads, Q), F32))
        scale_ref[span, :] = jnp.transpose(jnp.concatenate(packed, axis=0), (1, 0)).astype(BF16)
        packed = split(cum * LOG2E, 3) + [jnp.zeros((D - 3 * heads, Q), F32)]
        cum_ref[span, :] = jnp.transpose(jnp.concatenate(packed, axis=0), (1, 0)).astype(BF16)
        rows_ref[:, span] = (cum - jnp.log(step_q)) * LOG2E
        dec_ref[:, q : q + 1] = jnp.exp(last) * jnp.where(doc_end == doc_prev, 1.0, 0.0)
        if q:
            dec_ref[:, NQ + q : NQ + q + 1] = jnp.exp(base) * jnp.where(doc_prev == doc_before, 1.0, 0.0)
        base = base + last
    doc_last = doc_at(first + BLK - 1, starts_ref)
    dec_ref[:, NQ : NQ + 1] = jnp.exp(base) * jnp.where(doc_last == doc_before, 1.0, 0.0)
    for q in range(NQ):
        row = lax.broadcasted_iota(jnp.int32, (Q, 2 * Q), 0)
        col = lax.broadcasted_iota(jnp.int32, (Q, 2 * Q), 1) - Q
        at = first + q * Q
        same = doc_of(at + row, starts_ref) == doc_of(at + col, starts_ref)
        for k in range(3):
            hit = same & (col == row - (3 - k))
            shift_ref[q, k * Q : (k + 1) * Q, :] = jnp.where(hit, 1.0, 0.0).astype(BF16)


def chooser(heads, chunk, lo, hi, width):
    k = lax.broadcasted_iota(jnp.int32, (D, width), 0)
    head = HC * chunk + lax.broadcasted_iota(jnp.int32, (D, width), 1) // D
    hit = ((k & (heads - 1)) == head) & (k >= lo * heads) & (k < hi * heads)
    return jnp.where(hit, 1.0, 0.0).astype(BF16)


def convolved(q, window, now, shift_ref, taps, bias):
    moved = jnp.dot(shift_ref[q], window, preferred_element_type=F32)
    total = (0.5 * taps[3]) * now.astype(F32) + 0.5 * bias
    for k in range(3):
        total = total + (0.5 * taps[k]) * moved[k * Q : (k + 1) * Q]
    return silu_half(total)


def window_of(q, edge_ref, x_ref):
    return edge_ref[...] if q == 0 else x_ref[(q - 1) * Q : (q + 1) * Q, :]


def edge(edge_ref, rim_ref, x_ref):
    width = x_ref.shape[1]
    rim = jnp.concatenate([jnp.zeros((Q - RIM, width), F32), rim_ref[...].astype(F32)], axis=0)
    edge_ref[0:Q, 0:width] = rim.astype(BF16)
    edge_ref[Q : 2 * Q, 0:width] = x_ref[0:Q, :]


def state_body(
    chunk, per_group, dec_ref, x_ref, rim_ref, wx_ref, bx_ref, shift_ref, scale_ref, bt_ref,
    mx_ref, enter_ref, end_ref, edge_ref, send_ref=None,
):
    heads = dec_ref.shape[0]
    edge(edge_ref, rim_ref, x_ref)
    pick = chooser(heads, chunk, 0, 2, CW)
    g = lax.div(chunk, per_group)
    taps = [wx_ref[k : k + 1, :] for k in range(4)]
    state = None
    for q in range(NQ):
        span = slice(q * Q, (q + 1) * Q)
        mixed = convolved(q, window_of(q, edge_ref, x_ref), x_ref[span, :], shift_ref, taps, bx_ref[...])
        mx_ref[span, :] = mixed.astype(BF16)
        scale = jnp.dot(scale_ref[span, :], pick, preferred_element_type=F32)
        part = jnp.dot(bt_ref[g, :, span], (mixed * scale).astype(BF16), preferred_element_type=F32)
        for i in range(HC):
            lanes = slice(i * D, (i + 1) * D)
            if q == 0:
                end_ref[0, :, lanes] = part[:, lanes]
            else:
                before = end_ref[0, :, lanes]
                enter_ref[q - 1, :, lanes] = before.astype(BF16)
                end_ref[0, :, lanes] = dec_ref[chunk * HC + i, q] * before + part[:, lanes]
    if send_ref is not None:
        send_ref[...] = end_ref[0].astype(BF16)


def first_kernel(
    place_ref, starts_ref, dec_ref, x_ref, rim_ref, wx_ref, bx_ref, shift_ref, scale_ref,
    bc_ref, rimbc_ref, wbc_ref, bbc_ref,
    mx_ref, enter_ref, end_ref, send_ref, bt_ref, c_ref, score_ref,
    edge_ref, *, per_group,
):
    groups = bt_ref.shape[0]
    wide = 2 * groups * D
    edge(edge_ref, rimbc_ref, bc_ref)

    def joined(rows):
        return jnp.concatenate(rows, axis=1)

    taps = [joined([wbc_ref[k, p : p + 1, :] for p in range(2)]) for k in range(4)]
    bias = joined([bbc_ref[p : p + 1, :] for p in range(2)])
    for q in range(NQ):
        span = slice(q * Q, (q + 1) * Q)
        window = edge_ref[:, 0:wide] if q == 0 else bc_ref[(q - 1) * Q : (q + 1) * Q, :]
        mixed = convolved(q, window, bc_ref[span, :], shift_ref, taps, bias)
        c_ref[span, :] = mixed[:, groups * D :].astype(BF16)
        at = place_ref[0] * BLK + q * Q
        row = at + lax.broadcasted_iota(jnp.int32, (Q, Q), 0)
        col = at + lax.broadcasted_iota(jnp.int32, (Q, Q), 1)
        keep = (row >= col) & (doc_of(row, starts_ref) == doc_of(col, starts_ref))
        for g in range(groups):
            lanes = slice(g * D, (g + 1) * D)
            bt = jnp.transpose(mixed[:, lanes], (1, 0)).astype(BF16)
            bt_ref[g, :, span] = bt
            score = jnp.dot(c_ref[span, lanes], bt, preferred_element_type=F32)
            score_ref[span, lanes] = jnp.where(keep, score, 0.0)
    state_body(
        0, per_group, dec_ref, x_ref, rim_ref, wx_ref, bx_ref, shift_ref, scale_ref, bt_ref,
        mx_ref, enter_ref, end_ref, edge_ref, send_ref,
    )


def more_kernel(
    dec_ref, x_ref, rim_ref, wx_ref, bx_ref, shift_ref, scale_ref, bt_ref, old1, old2, old3,
    mx_ref, enter_ref, end_ref, *rest, per_group, chunk_of, sends,
):
    send_ref, edge_ref = rest if sends else (None, rest[0])
    state_body(
        chunk_of(pl.program_id(0)), per_group, dec_ref, x_ref, rim_ref, wx_ref, bx_ref, shift_ref, scale_ref,
        bt_ref, mx_ref, enter_ref, end_ref, edge_ref, send_ref,
    )


def join_kernel(place_ref, dec_ref, recv_ref, end_ref, token_ref, send_ref, *, turn, stream, per_stream):
    chunk = stream * per_stream + jnp.clip(turn - place_ref[0], 0, per_stream - 1)
    for i in range(HC):
        lanes = slice(i * D, (i + 1) * D)
        fade = dec_ref[chunk * HC + i, NQ]
        send_ref[:, lanes] = (fade * recv_ref[:, lanes].astype(F32) + end_ref[0, :, lanes]).astype(BF16)


def out_kernel(
    place_ref, dec_ref, mx_ref, enter_ref, c_ref, score_ref, scale_ref, cum_ref, rows_ref, recv_ref,
    *rest, turn, stream, per_stream,
):
    out_ref, token_ref = rest[-2:]
    token_ref[...] = jnp.zeros_like(token_ref)
    heads = rows_ref.shape[0]
    rank = turn - place_ref[0]
    chunk = stream * per_stream + jnp.clip(rank, 0, per_stream - 1)

    @pl.when((rank >= 0) & (rank < per_stream))
    def compute():
        pick_cum = chooser(heads, chunk, 0, 3, CW)
        pick_entry = chooser(heads, chunk, 2, 4, CW)
        for q in range(NQ):
            span = slice(q * Q, (q + 1) * Q)
            both = rows_ref[pl.ds(pl.multiple_of(2 * HC * lax.div(chunk, 2), 2 * HC), 2 * HC), span]
            terms = jnp.where(lax.rem(chunk, 2) == 0, both[:HC], both[HC:])
            cums = jnp.dot(cum_ref[span, :], pick_cum, preferred_element_type=F32)
            entry = jnp.dot(scale_ref[span, :], pick_entry, preferred_element_type=F32)
            if q:
                parts = []
                for i in range(HC):
                    lanes = slice(i * D, (i + 1) * D)
                    reach = dec_ref[chunk * HC + i, NQ + q]
                    parts.append(
                        (enter_ref[q - 1, :, lanes].astype(F32) + reach * recv_ref[:, lanes].astype(F32)).astype(BF16)
                    )
                state = jnp.concatenate(parts, axis=1)
            else:
                state = recv_ref[...]
            far = jnp.dot(c_ref[span, :], state, preferred_element_type=F32)
            score = score_ref[span, :]
            for i in range(HC):
                lanes = slice(i * D, (i + 1) * D)
                gap = cums[:, lanes] - terms[i : i + 1]
                weight = (score * jnp.exp2(jnp.minimum(gap, 100.0))).astype(BF16)
                x = mx_ref[span, lanes]
                y = jnp.dot(weight, x, preferred_element_type=F32)
                y = y + entry[:, lanes] * far[:, lanes] + dec_ref[chunk * HC + i, 2 * NQ] * x.astype(F32)
                out_ref[span, lanes] = y.astype(BF16)

    if turn >= per_stream:
        @pl.when(rank >= per_stream)
        def again():
            out_ref[...] = rest[0][...]


SMEM = pl.BlockSpec(memory_space=pltpu.SMEM)
ROOM = pltpu.CompilerParams(vmem_limit_bytes=16 * 2**20)
ANY = pl.BlockSpec(memory_space=pl.ANY)


def whole(shape):
    return pl.BlockSpec(shape, lambda *_: (0,) * len(shape))


def shape_of(shape, dtype):
    return jax.ShapeDtypeStruct(shape, dtype)


def per_device(
    x_raw, bc_raw, dt_raw, dt_bias, a_log, d_skip, conv_x, conv_x_bias, conv_bc, conv_bc_bias, doc_starts
):
    rows, width = x_raw.shape
    held = [x_raw, dt_raw, dt_bias, a_log, d_skip, conv_x, conv_bc, conv_bc_bias, doc_starts]
    held = [pltpu.with_memory_space_constraint(a, pltpu.HBM) for a in held]
    x_pin, dt_raw, dt_bias, a_log, d_skip, conv_x, conv_bc, conv_bc_bias, doc_starts = held
    groups = bc_raw.shape[2] // D
    heads = dt_raw.shape[0]
    chunks = heads // HC
    per_group = chunks // groups
    wide = 2 * groups * D
    seq = lax.axis_size("seq")
    place = lax.axis_index("seq").astype(jnp.int32)
    place_row = place.reshape(1)
    ring = [(i, (i + 1) % seq) for i in range(seq)]
    streams = 2
    per_stream = chunks // streams
    slots = per_stream + seq - 2

    tail = jnp.concatenate([x_raw[rows - RIM :], bc_raw[rows - RIM :].reshape(RIM, -1)], axis=1)
    rim = lax.ppermute(tail, "seq", ring)
    bc = bc_raw.reshape(rows, -1)
    bias_x = pltpu.with_memory_space_constraint(conv_x_bias[None], pltpu.HBM)

    scale, cums, row_terms, dec, shift = pl.pallas_call(
        params_kernel,
        in_specs=[SMEM] * 5 + [pl.BlockSpec(memory_space=pltpu.VMEM)],
        out_specs=[pl.BlockSpec(memory_space=pltpu.VMEM)] * 5,
        out_shape=[
            shape_of((BLK, D), BF16),
            shape_of((BLK, D), BF16),
            shape_of((heads, BLK), F32),
            shape_of((heads, 16), F32),
            shape_of((NQ, 3 * Q, 2 * Q), BF16),
        ],
        compiler_params=ROOM,
        name="params",
    )(place_row, doc_starts, dt_bias, a_log, d_skip, dt_raw)

    def chunk_specs(chunk_of):
        ins = [
            pl.BlockSpec((BLK, CW), lambda i: (0, chunk_of(i))),
            pl.BlockSpec((RIM, CW), lambda i: (0, chunk_of(i))),
            pl.BlockSpec((4, CW), lambda i: (0, chunk_of(i))),
            pl.BlockSpec((1, CW), lambda i: (0, chunk_of(i))),
            whole((NQ, 3 * Q, 2 * Q)),
            whole((BLK, D)),
        ]
        outs = [
            pl.BlockSpec((BLK, CW), lambda i: (0, chunk_of(i))),
            pl.BlockSpec((NQ - 1, D, CW), lambda i: (0, 0, chunk_of(i))),
            pl.BlockSpec((1, D, CW), lambda i: (chunk_of(i), 0, 0)),
        ]
        return ins, outs

    big = [
        shape_of((BLK, width), BF16),
        shape_of((NQ - 1, D, width), BF16),
        shape_of((chunks, D, CW), F32),
    ]
    chunk_shape = shape_of((D, CW), BF16)
    edge_scratch = [pltpu.VMEM((2 * Q, CW), BF16)]
    ins, outs = chunk_specs(lambda i: 0)
    mixed_x, enter, end, send_a, bt, mixed_c, score = pl.pallas_call(
        functools.partial(first_kernel, per_group=per_group),
        grid=(1,),
        in_specs=[
            SMEM, SMEM, SMEM, *ins,
            whole((BLK, wide)),
            pl.BlockSpec((RIM, wide), lambda i: (0, width // wide)),
            whole((4, 2, groups * D)),
            whole((2, groups * D)),
        ],
        out_specs=[
            *outs,
            whole((D, CW)),
            whole((groups, D, BLK)),
            whole((BLK, groups * D)),
            whole((BLK, groups * D)),
        ],
        out_shape=[
            *big,
            chunk_shape,
            shape_of((groups, D, BLK), BF16),
            shape_of((BLK, groups * D), BF16),
            shape_of((BLK, groups * D), F32),
        ],
        scratch_shapes=edge_scratch,
        compiler_params=ROOM,
        name="first",
    )(
        place_row, doc_starts, dec, x_pin, rim, conv_x, bias_x, shift, scale,
        bc, rim, conv_bc, conv_bc_bias,
    )

    def more(count, chunk_of, sends, mixed_x, enter, end):
        ins, outs = chunk_specs(chunk_of)
        return pl.pallas_call(
            functools.partial(more_kernel, per_group=per_group, chunk_of=chunk_of, sends=sends),
            grid=(count,),
            in_specs=[SMEM, *ins, whole((groups, D, BLK)), ANY, ANY, ANY],
            out_specs=outs + [whole((D, CW))] * sends,
            out_shape=big + [chunk_shape] * sends,
            input_output_aliases={8: 0, 9: 1, 10: 2},
            scratch_shapes=edge_scratch,
            cost_estimate=pl.CostEstimate(
                flops=4 * count * BLK * D * CW, bytes_accessed=4 * count * BLK * CW, transcendentals=0
            ),
            compiler_params=ROOM,
        name="more",
        )(dec, x_pin, rim, conv_x, bias_x, shift, scale, bt, mixed_x, enter, end)

    flying = [lax.ppermute(send_a, "seq", ring), None]
    mixed_x, enter, end, send_b = more(1, lambda i: per_stream, 1, mixed_x, enter, end)
    flying[1] = lax.ppermute(send_b, "seq", ring)
    rest = (per_stream - 1) * streams
    mixed_x, enter, end = more(
        rest, lambda i: 1 + i // 2 + (i % 2) * per_stream, 0, mixed_x, enter, end
    )

    def join(turn, s, recv, token):
        def chunk(at):
            return s * per_stream + jnp.clip(turn - at[0], 0, per_stream - 1)

        return pl.pallas_call(
            functools.partial(join_kernel, turn=turn, stream=s, per_stream=per_stream),
            grid_spec=pltpu.PrefetchScalarGridSpec(
                num_scalar_prefetch=1,
                grid=(1,),
                in_specs=[
                    SMEM,
                    whole((D, CW)),
                    pl.BlockSpec((1, D, CW), lambda i, at: (chunk(at), 0, 0)),
                    whole((8, D)),
                ],
                out_specs=whole((D, CW)),
            ),
            out_shape=chunk_shape,
            compiler_params=ROOM,
            name="join",
        )(place_row, dec, recv, end, token)

    def output(turn, s, recv, out):
        def chunk(place_ref):
            return s * per_stream + jnp.clip(turn - place_ref[0], 0, per_stream - 1)

        block = pl.BlockSpec((BLK, CW), lambda i, at: (0, chunk(at)))
        old = [] if out is None else [out]
        return pl.pallas_call(
            functools.partial(out_kernel, turn=turn, stream=s, per_stream=per_stream),
            grid_spec=pltpu.PrefetchScalarGridSpec(
                num_scalar_prefetch=1,
                grid=(1,),
                in_specs=[
                    SMEM,
                    block,
                    pl.BlockSpec((NQ - 1, D, CW), lambda i, at: (0, 0, chunk(at))),
                    pl.BlockSpec((BLK, D), lambda i, at: (0, chunk(at) // per_group)),
                    pl.BlockSpec((BLK, D), lambda i, at: (0, chunk(at) // per_group)),
                    whole((BLK, D)),
                    whole((BLK, D)),
                    whole((heads, BLK)),
                    whole((D, CW)),
                ]
                + [block if turn >= per_stream else ANY] * len(old),
                out_specs=[block, whole((8, D))],
            ),
            out_shape=[shape_of((BLK, width), BF16), shape_of((8, D), F32)],
            input_output_aliases={10: 0} if old else {},
            cost_estimate=pl.CostEstimate(
                flops=8 * BLK * Q * CW, bytes_accessed=6 * BLK * CW, transcendentals=0
            ),
            compiler_params=ROOM,
        name="out",
        )(place_row, dec, mixed_x, enter, mixed_c, score, scale, cums, row_terms, recv, *old)

    out, token = None, None
    carried = [send_a, send_b]
    for turn in range(slots + 1):
        for s in range(streams):
            if turn:
                recv = flying[s]
                if turn < slots:
                    flying[s] = lax.ppermute(join(turn, s, recv, token), "seq", ring)
                carried[s] = recv
            out, token = output(turn, s, carried[s], out)
    return out


def solution(mesh):
    return jax.shard_map(
        per_device,
        mesh=mesh,
        in_specs=(
            P(("groups", "seq"), ("head", "sub")),
            P(("groups", "seq"), None, ("head", "sub")),
            P(("head", "sub"), ("groups", "seq")),
            P(("head", "sub")),
            P(("head", "sub")),
            P(("head", "sub")),
            P(None, ("head", "sub")),
            P(("head", "sub")),
            P(None, None, ("head", "sub")),
            P(None, ("head", "sub")),
            P("groups"),
        ),
        out_specs=P(("groups", "seq"), ("head", "sub")),
        check_vma=False,
    )
```

```python
import functools
import math

import jax
import jax.numpy as jnp
from jax import lax
from jax.experimental import pallas as pl
from jax.experimental.pallas import tpu as pltpu
from jax.sharding import PartitionSpec as P

D = 128
Q = 128
BLK = 512
NQ = BLK // Q
HC = 4
CW = HC * D
RIM = 8
LOG2E = math.log2(math.e)
F32 = jnp.float32
BF16 = jnp.bfloat16


def doc_of(pos, starts_ref):
    count = jnp.zeros_like(pos)
    for j in range(starts_ref.shape[0]):
        count = count + (pos >= starts_ref[j]).astype(jnp.int32)
    return count - 1


def silu_half(u):
    return u + u * jnp.tanh(u)


def doc_at(pos, starts_ref):
    count = jnp.int32(-1)
    for j in range(starts_ref.shape[0]):
        count = count + (pos >= starts_ref[j]).astype(jnp.int32)
    return count


def column_of(ref):
    heads = ref.shape[0]
    index = lax.broadcasted_iota(jnp.int32, (heads, 1), 0)
    column = jnp.zeros((heads, 1), F32)
    for h in range(heads):
        column = jnp.where(index == h, ref[h], column)
    return column


def split(value, parts):
    pieces = []
    for _ in range(parts - 1):
        piece = value.astype(BF16).astype(F32)
        pieces.append(piece)
        value = value - piece
    return pieces + [value]


def doc_at(pos, starts_ref):
    count = jnp.int32(-1)
    for j in range(starts_ref.shape[0]):
        count = count + (pos >= starts_ref[j]).astype(jnp.int32)
    return count


def column_of(ref):
    heads = ref.shape[0]
    index = lax.broadcasted_iota(jnp.int32, (heads, 1), 0)
    column = jnp.zeros((heads, 1), F32)
    for h in range(heads):
        column = jnp.where(index == h, ref[h], column)
    return column


def split(value, parts):
    pieces = []
    for _ in range(parts - 1):
        piece = value.astype(BF16).astype(F32)
        pieces.append(piece)
        value = value - piece
    return pieces + [value]


def doc_at(pos, starts_ref):
    count = jnp.int32(-1)
    for j in range(starts_ref.shape[0]):
        count = count + (pos >= starts_ref[j]).astype(jnp.int32)
    return count


def column_of(ref):
    heads = ref.shape[0]
    index = lax.broadcasted_iota(jnp.int32, (heads, 1), 0)
    column = jnp.zeros((heads, 1), F32)
    for h in range(heads):
        column = jnp.where(index == h, ref[h], column)
    return column


def split(value, parts):
    pieces = []
    for _ in range(parts - 1):
        piece = value.astype(BF16).astype(F32)
        pieces.append(piece)
        value = value - piece
    return pieces + [value]


def doc_at(pos, starts_ref):
    count = jnp.int32(-1)
    for j in range(starts_ref.shape[0]):
        count = count + (pos >= starts_ref[j]).astype(jnp.int32)
    return count


def column_of(ref):
    heads = ref.shape[0]
    index = lax.broadcasted_iota(jnp.int32, (heads, 1), 0)
    column = jnp.zeros((heads, 1), F32)
    for h in range(heads):
        column = jnp.where(index == h, ref[h], column)
    return column


def split(value, parts):
    pieces = []
    for _ in range(parts - 1):
        piece = value.astype(BF16).astype(F32)
        pieces.append(piece)
        value = value - piece
    return pieces + [value]


def doc_at(pos, starts_ref):
    count = jnp.int32(-1)
    for j in range(starts_ref.shape[0]):
        count = count + (pos >= starts_ref[j]).astype(jnp.int32)
    return count


def column_of(ref):
    heads = ref.shape[0]
    index = lax.broadcasted_iota(jnp.int32, (heads, 1), 0)
    column = jnp.zeros((heads, 1), F32)
    for h in range(heads):
        column = jnp.where(index == h, ref[h], column)
    return column


def split(value, parts):
    pieces = []
    for _ in range(parts - 1):
        piece = value.astype(BF16).astype(F32)
        pieces.append(piece)
        value = value - piece
    return pieces + [value]


def params_kernel(
    starts_ref, bias_ref, alog_ref, skip_ref, dt_ref, scale_ref, cum_ref, rows_ref, fade_ref, shift_ref, keep_ref
):
    first = lax.axis_index("seq") * BLK
    heads = dt_ref.shape[0]
    v = dt_ref[...] + column_of(bias_ref)
    step = jnp.maximum(v, 0.0) + jnp.log(1.0 + jnp.exp(-jnp.abs(v)))
    rate = -jnp.exp(column_of(alog_ref)) * step
    tri = (
        lax.broadcasted_iota(jnp.int32, (Q, Q), 0) <= lax.broadcasted_iota(jnp.int32, (Q, Q), 1)
    ).astype(F32)
    doc_before = doc_at(first - 1, starts_ref)
    doc_last = doc_at(first + BLK - 1, starts_ref)
    cums = []
    base = jnp.zeros((heads, 1), F32)
    for q in range(NQ):
        part = jnp.dot(
            rate[:, q * Q : (q + 1) * Q], tri, precision=lax.Precision.HIGHEST, preferred_element_type=F32
        )
        cums.append(part + base)
        base = base + part[:, Q - 1 : Q]
    for q in range(NQ):
        span = slice(q * Q, (q + 1) * Q)
        cum = cums[q]
        step_q = step[:, span]
        pos = first + q * Q + lax.broadcasted_iota(jnp.int32, (1, Q), 1)
        doc = doc_of(pos, starts_ref)
        tail = jnp.where(doc == doc_last, jnp.exp(base - cum) * step_q, 0.0)
        entry = jnp.where(doc == doc_before, jnp.exp(cum), 0.0)
        packed = split(tail, 2) + split(entry, 2)
        if 4 * heads < D:
            packed.append(jnp.zeros((D - 4 * heads, Q), F32))
        scale_ref[span, :] = jnp.transpose(jnp.concatenate(packed, axis=0), (1, 0)).astype(BF16)
        packed = split(cum * LOG2E, 3) + [jnp.zeros((D - 3 * heads, Q), F32)]
        cum_ref[span, :] = jnp.transpose(jnp.concatenate(packed, axis=0), (1, 0)).astype(BF16)
        terms = (cum - jnp.log(step_q)) * LOG2E
        for c in range(heads // HC):
            rows_ref[c, :, span] = terms[c * HC : (c + 1) * HC]
    decay = jnp.exp(base) * jnp.where(doc_last == doc_before, 1.0, 0.0)
    skip = column_of(skip_ref)
    for c in range(heads // HC):
        for i in range(HC):
            h = c * HC + i
            lanes = slice(i * D, (i + 1) * D)
            fade_ref[c, 0:1, lanes] = jnp.broadcast_to(skip[h : h + 1], (1, D))
            fade_ref[c, 1:2, lanes] = jnp.broadcast_to(decay[h : h + 1], (1, D))
    for q in range(NQ):
        row = lax.broadcasted_iota(jnp.int32, (Q, 2 * Q), 0)
        col = lax.broadcasted_iota(jnp.int32, (Q, 2 * Q), 1) - Q
        at = first + q * Q
        same = doc_of(at + row, starts_ref) == doc_of(at + col, starts_ref)
        for k in range(3):
            hit = same & (col == row - (3 - k))
            shift_ref[q, k * Q : (k + 1) * Q, :] = jnp.where(hit, 1.0, 0.0).astype(BF16)
        doc_row = doc_of(at + lax.broadcasted_iota(jnp.int32, (Q, BLK), 0), starts_ref)
        col = lax.broadcasted_iota(jnp.int32, (Q, BLK), 1)
        row = q * Q + lax.broadcasted_iota(jnp.int32, (Q, BLK), 0)
        keep = (row >= col) & (doc_row == doc_of(first + col, starts_ref))
        keep_ref[q * Q : (q + 1) * Q, :] = jnp.where(keep, 1.0, 0.0)


def chooser(heads, chunk, lo, hi, width):
    k = lax.broadcasted_iota(jnp.int32, (D, width), 0)
    head = HC * chunk + lax.broadcasted_iota(jnp.int32, (D, width), 1) // D
    hit = ((k & (heads - 1)) == head) & (k >= lo * heads) & (k < hi * heads)
    return jnp.where(hit, 1.0, 0.0).astype(BF16)


def convolved(q, window, now, shift_ref, taps, bias):
    moved = jnp.dot(shift_ref[q], window, preferred_element_type=F32)
    total = (0.5 * taps[3]) * now.astype(F32) + 0.5 * bias
    for k in range(3):
        total = total + (0.5 * taps[k]) * moved[k * Q : (k + 1) * Q]
    return silu_half(total)


def window_of(q, edge_ref, x_ref):
    return edge_ref[...] if q == 0 else x_ref[(q - 1) * Q : (q + 1) * Q, :]


def edge(edge_ref, rim_ref, x_ref):
    width = x_ref.shape[1]
    rim = jnp.concatenate([jnp.zeros((Q - RIM, width), F32), rim_ref[...].astype(F32)], axis=0)
    edge_ref[0:Q, 0:width] = rim.astype(BF16)
    edge_ref[Q : 2 * Q, 0:width] = x_ref[0:Q, :]


def state_body(
    chunk, heads, per_group, x_ref, rim_ref, wx_ref, bx_ref, shift_ref, scale_ref, bt_ref,
    mx_ref, end_ref, edge_ref, tail_ref, send_ref=None,
):
    edge(edge_ref, rim_ref, x_ref)
    pick = chooser(heads, chunk, 0, 2, CW)
    taps = [wx_ref[k : k + 1, :] for k in range(4)]
    for q in range(NQ):
        span = slice(q * Q, (q + 1) * Q)
        mixed = convolved(q, window_of(q, edge_ref, x_ref), x_ref[span, :], shift_ref, taps, bx_ref[...])
        mx_ref[0, span, :] = mixed.astype(BF16)
        scale = jnp.dot(scale_ref[span, :], pick, preferred_element_type=F32)
        tail_ref[span, :] = (mixed * scale).astype(BF16)
    state = jnp.dot(bt_ref[lax.div(chunk, per_group)], tail_ref[...], preferred_element_type=F32)
    end_ref[0] = state
    if send_ref is not None:
        send_ref[...] = state.astype(BF16)


def first_kernel(
    x_ref, rim_ref, wx_ref, bx_ref, shift_ref, scale_ref, keep_ref, bc_ref, rimbc_ref, wbc_ref, bbc_ref,
    mx_ref, end_ref, send_ref, bt_ref, c_ref, score_ref,
    edge_ref, tail_ref, *, heads, per_group,
):
    groups = bt_ref.shape[0]
    wide = 2 * groups * D
    edge(edge_ref, rimbc_ref, bc_ref)

    def joined(rows):
        return jnp.concatenate(rows, axis=1)

    taps = [joined([wbc_ref[k, p : p + 1, :] for p in range(2)]) for k in range(4)]
    bias = joined([bbc_ref[p : p + 1, :] for p in range(2)])
    for q in range(NQ):
        span = slice(q * Q, (q + 1) * Q)
        window = edge_ref[:, 0:wide] if q == 0 else bc_ref[(q - 1) * Q : (q + 1) * Q, :]
        mixed = convolved(q, window, bc_ref[span, :], shift_ref, taps, bias)
        upto = (q + 1) * Q
        for g in range(groups):
            bt_ref[g, :, span] = jnp.transpose(mixed[:, g * D : (g + 1) * D], (1, 0)).astype(BF16)
            c = mixed[:, (groups + g) * D : (groups + g + 1) * D].astype(BF16)
            c_ref[g, span, :] = c
            score = jnp.dot(c, bt_ref[g, :, 0:upto], preferred_element_type=F32)
            score_ref[g, span, 0:upto] = keep_ref[span, 0:upto] * score
    state_body(
        0, heads, per_group, x_ref, rim_ref, wx_ref, bx_ref, shift_ref, scale_ref, bt_ref,
        mx_ref, end_ref, edge_ref, tail_ref, send_ref,
    )


def more_kernel(
    x_ref, rim_ref, wx_ref, bx_ref, shift_ref, scale_ref, bt_ref, old1, old2,
    mx_ref, end_ref, *rest, heads, per_group, chunk_of, sends,
):
    state_body(
        chunk_of(pl.program_id(0)), heads, per_group, x_ref, rim_ref, wx_ref, bx_ref, shift_ref, scale_ref,
        bt_ref, mx_ref, end_ref, *rest[-2:], *rest[:sends],
    )


def join_kernel(fade_ref, recv_ref, end_ref, token_ref, send_ref, *, turn, stream, per_stream):
    chunk = stream * per_stream + jnp.clip(turn - lax.axis_index("seq"), 0, per_stream - 1)
    send_ref[...] = (fade_ref[chunk, 1:2, :] * recv_ref[...].astype(F32) + end_ref[chunk]).astype(BF16)


def out_kernel(
    fade_ref, mx_ref, c_ref, score_ref, scale_ref, cum_ref, rows_ref, recv_ref,
    *rest, turn, stream, per_stream, per_group, heads,
):
    out_ref, token_ref, ready_ref, sem = rest[-4:]
    token_ref[...] = jnp.zeros_like(token_ref)
    rank = turn - lax.axis_index("seq")

    @pl.when((rank >= 0) & (rank < per_stream))
    def compute():
        chunk = stream * per_stream + rank
        g = lax.div(chunk, per_group)
        pick_cum = chooser(heads, chunk, 0, 3, CW)
        pick_entry = chooser(heads, chunk, 2, 4, CW)
        copies = []
        for q in range(NQ):
            span = slice(q * Q, (q + 1) * Q)
            cums = jnp.dot(cum_ref[span, :], pick_cum, preferred_element_type=F32)
            entry = jnp.dot(scale_ref[span, :], pick_entry, preferred_element_type=F32)
            far = jnp.dot(c_ref[g, span, :], recv_ref[...], preferred_element_type=F32)
            for i in range(HC):
                lanes = slice(i * D, (i + 1) * D)
                parts = []
                for j in range(q + 1):
                    there = slice(j * Q, (j + 1) * Q)
                    gap = cums[:, lanes] - rows_ref[chunk, i : i + 1, there]
                    if j == q:
                        gap = jnp.minimum(gap, 100.0)
                    parts.append((score_ref[g, span, there] * jnp.exp2(gap)).astype(BF16))
                weight = jnp.concatenate(parts, axis=1)
                y = jnp.dot(weight, mx_ref[chunk, 0 : (q + 1) * Q, lanes], preferred_element_type=F32)
                x = mx_ref[chunk, span, lanes].astype(F32)
                y = y + entry[:, lanes] * far[:, lanes] + fade_ref[chunk, 0:1, lanes] * x
                ready_ref[span, lanes] = y.astype(BF16)
            to = out_ref.at[pl.ds(q * Q, Q), pl.ds(pl.multiple_of(chunk * CW, CW), CW)]
            copy = pltpu.make_async_copy(ready_ref.at[pl.ds(q * Q, Q), :], to, sem.at[q])
            copy.start()
            copies.append(copy)
        for copy in copies:
            copy.wait()


SMEM = pl.BlockSpec(memory_space=pltpu.SMEM)
ROOM = pltpu.CompilerParams(vmem_limit_bytes=16 * 2**20)
ANY = pl.BlockSpec(memory_space=pl.ANY)
VMEM = pl.BlockSpec(memory_space=pltpu.VMEM)


def whole(shape):
    return pl.BlockSpec(shape, lambda *_: (0,) * len(shape))


def shape_of(shape, dtype):
    return jax.ShapeDtypeStruct(shape, dtype)


def per_device(
    x_raw, bc_raw, dt_raw, dt_bias, a_log, d_skip, conv_x, conv_x_bias, conv_bc, conv_bc_bias, doc_starts
):
    rows, width = x_raw.shape
    held = [x_raw, dt_raw, dt_bias, a_log, d_skip, conv_x, conv_x_bias[None], conv_bc, conv_bc_bias, doc_starts]
    held = [pltpu.with_memory_space_constraint(a, pltpu.HBM) for a in held]
    x_pin, dt_raw, dt_bias, a_log, d_skip, conv_x, bias_x, conv_bc, conv_bc_bias, doc_starts = held
    groups = bc_raw.shape[2] // D
    heads = dt_raw.shape[0]
    chunks = heads // HC
    per_group = chunks // groups
    wide = 2 * groups * D
    seq = lax.axis_size("seq")
    ring = [(i, (i + 1) % seq) for i in range(seq)]
    streams = 2
    per_stream = chunks // streams
    slots = per_stream + seq - 2

    tail = jnp.concatenate([x_raw[rows - RIM :], bc_raw[rows - RIM :].reshape(RIM, -1)], axis=1)
    rim = lax.ppermute(tail, "seq", ring)
    bc = bc_raw.reshape(rows, -1)

    scale, cums, row_terms, fade, shift, keep = pl.pallas_call(
        params_kernel,
        in_specs=[SMEM] * 4 + [VMEM],
        out_specs=[VMEM] * 6,
        out_shape=[
            shape_of((BLK, D), BF16),
            shape_of((BLK, D), BF16),
            shape_of((chunks, HC, BLK), F32),
            shape_of((chunks, 2, CW), F32),
            shape_of((NQ, 3 * Q, 2 * Q), BF16),
            shape_of((BLK, BLK), F32),
        ],
        compiler_params=ROOM,
        name="params",
    )(doc_starts, dt_bias, a_log, d_skip, dt_raw)

    def chunk_specs(chunk_of):
        ins = [
            pl.BlockSpec((BLK, CW), lambda i: (0, chunk_of(i))),
            pl.BlockSpec((RIM, CW), lambda i: (0, chunk_of(i))),
            pl.BlockSpec((4, CW), lambda i: (0, chunk_of(i))),
            pl.BlockSpec((1, CW), lambda i: (0, chunk_of(i))),
            whole((NQ, 3 * Q, 2 * Q)),
            whole((BLK, D)),
        ]
        outs = [
            pl.BlockSpec((1, BLK, CW), lambda i: (chunk_of(i), 0, 0)),
            pl.BlockSpec((1, D, CW), lambda i: (chunk_of(i), 0, 0)),
        ]
        return ins, outs

    big = [shape_of((chunks, BLK, CW), BF16), shape_of((chunks, D, CW), F32)]
    chunk_shape = shape_of((D, CW), BF16)
    scratch = [pltpu.VMEM((2 * Q, CW), BF16), pltpu.VMEM((BLK, CW), BF16)]
    ins, outs = chunk_specs(lambda i: 0)
    mixed_x, end, send_a, bt, mixed_c, score = pl.pallas_call(
        functools.partial(first_kernel, heads=heads, per_group=per_group),
        grid=(1,),
        in_specs=[
            *ins,
            whole((BLK, BLK)),
            whole((BLK, wide)),
            pl.BlockSpec((RIM, wide), lambda i: (0, width // wide)),
            whole((4, 2, groups * D)),
            whole((2, groups * D)),
        ],
        out_specs=[
            *outs,
            whole((D, CW)),
            whole((groups, D, BLK)),
            whole((groups, BLK, D)),
            whole((groups, BLK, BLK)),
        ],
        out_shape=[
            *big,
            chunk_shape,
            shape_of((groups, D, BLK), BF16),
            shape_of((groups, BLK, D), BF16),
            shape_of((groups, BLK, BLK), F32),
        ],
        scratch_shapes=scratch,
        compiler_params=ROOM,
        name="first",
    )(x_pin, rim, conv_x, bias_x, shift, scale, keep, bc, rim, conv_bc, conv_bc_bias)

    def more(count, chunk_of, sends, mixed_x, end):
        ins, outs = chunk_specs(chunk_of)
        return pl.pallas_call(
            functools.partial(more_kernel, heads=heads, per_group=per_group, chunk_of=chunk_of, sends=sends),
            grid=(count,),
            in_specs=[*ins, whole((groups, D, BLK)), ANY, ANY],
            out_specs=outs + [whole((D, CW))] * sends,
            out_shape=big + [chunk_shape] * sends,
            input_output_aliases={7: 0, 8: 1},
            scratch_shapes=scratch,
            compiler_params=ROOM,
            cost_estimate=pl.CostEstimate(
                flops=4 * count * BLK * D * CW, bytes_accessed=4 * count * BLK * CW, transcendentals=0
            ),
            name="more",
        )(x_pin, rim, conv_x, bias_x, shift, scale, bt, mixed_x, end)

    flying = [lax.ppermute(send_a, "seq", ring), None]
    mixed_x, end, send_b = more(1, lambda i: per_stream, 1, mixed_x, end)
    flying[1] = lax.ppermute(send_b, "seq", ring)

    def join(turn, s, recv, token):
        return pl.pallas_call(
            functools.partial(join_kernel, turn=turn, stream=s, per_stream=per_stream),
            in_specs=[VMEM, VMEM, VMEM, VMEM],
            out_specs=VMEM,
            out_shape=chunk_shape,
            compiler_params=ROOM,
            name="join",
        )(fade, recv, end, token)

    def output(turn, s, recv, out):
        old = [] if out is None else [out]
        return pl.pallas_call(
            functools.partial(
                out_kernel, turn=turn, stream=s, per_stream=per_stream, per_group=per_group, heads=heads
            ),
            in_specs=[VMEM] * 8 + [ANY] * len(old),
            out_specs=[ANY, VMEM],
            out_shape=[pltpu.HBM((BLK, width), BF16), shape_of((8, D), F32)],
            input_output_aliases={8: 0} if old else {},
            scratch_shapes=[pltpu.VMEM((BLK, CW), BF16), pltpu.SemaphoreType.DMA((NQ,))],
            compiler_params=ROOM,
            cost_estimate=pl.CostEstimate(
                flops=8 * BLK * Q * CW, bytes_accessed=6 * BLK * CW, transcendentals=0
            ),
            name="out",
        )(fade, mixed_x, mixed_c, score, scale, cums, row_terms, recv, *old)

    out, token = None, None
    carried = [send_a, send_b]
    for turn in range(slots + 1):
        if 0 < turn < per_stream:
            mixed_x, end = more(streams, lambda i, t=turn: t + i * per_stream, 0, mixed_x, end)
        for s in range(streams):
            if turn:
                recv = flying[s]
                if turn < slots:
                    flying[s] = lax.ppermute(join(turn, s, recv, token), "seq", ring)
                carried[s] = recv
            out, token = output(turn, s, carried[s], out)
    return out


def solution(mesh):
    return jax.shard_map(
        per_device,
        mesh=mesh,
        in_specs=(
            P(("groups", "seq"), ("head", "sub")),
            P(("groups", "seq"), None, ("head", "sub")),
            P(("head", "sub"), ("groups", "seq")),
            P(("head", "sub")),
            P(("head", "sub")),
            P(("head", "sub")),
            P(None, ("head", "sub")),
            P(("head", "sub")),
            P(None, None, ("head", "sub")),
            P(None, ("head", "sub")),
            P("groups"),
        ),
        out_specs=P(("groups", "seq"), ("head", "sub")),
        check_vma=False,
    )
```

```python
import functools
import math

import jax
import jax.numpy as jnp
from jax import lax
from jax.experimental import pallas as pl
from jax.experimental.pallas import tpu as pltpu
from jax.sharding import PartitionSpec as P

D = 128
Q = 128
BLK = 512
NQ = BLK // Q
HC = 4
CW = HC * D
RIM = 8
LOG2E = math.log2(math.e)
F32 = jnp.float32
BF16 = jnp.bfloat16


def doc_of(pos, starts_ref):
    count = jnp.zeros_like(pos)
    for j in range(starts_ref.shape[0]):
        count = count + (pos >= starts_ref[j]).astype(jnp.int32)
    return count - 1


def silu_half(u):
    return u + u * jnp.tanh(u)


def doc_at(pos, starts_ref):
    count = jnp.int32(-1)
    for j in range(starts_ref.shape[0]):
        count = count + (pos >= starts_ref[j]).astype(jnp.int32)
    return count


def column_of(ref):
    heads = ref.shape[0]
    index = lax.broadcasted_iota(jnp.int32, (heads, 1), 0)
    column = jnp.zeros((heads, 1), F32)
    for h in range(heads):
        column = jnp.where(index == h, ref[h], column)
    return column


def split(value, parts):
    pieces = []
    for _ in range(parts - 1):
        piece = value.astype(BF16).astype(F32)
        pieces.append(piece)
        value = value - piece
    return pieces + [value]


def doc_at(pos, starts_ref):
    count = jnp.int32(-1)
    for j in range(starts_ref.shape[0]):
        count = count + (pos >= starts_ref[j]).astype(jnp.int32)
    return count


def column_of(ref):
    heads = ref.shape[0]
    index = lax.broadcasted_iota(jnp.int32, (heads, 1), 0)
    column = jnp.zeros((heads, 1), F32)
    for h in range(heads):
        column = jnp.where(index == h, ref[h], column)
    return column


def split(value, parts):
    pieces = []
    for _ in range(parts - 1):
        piece = value.astype(BF16).astype(F32)
        pieces.append(piece)
        value = value - piece
    return pieces + [value]


def doc_at(pos, starts_ref):
    count = jnp.int32(-1)
    for j in range(starts_ref.shape[0]):
        count = count + (pos >= starts_ref[j]).astype(jnp.int32)
    return count


def column_of(ref):
    heads = ref.shape[0]
    index = lax.broadcasted_iota(jnp.int32, (heads, 1), 0)
    column = jnp.zeros((heads, 1), F32)
    for h in range(heads):
        column = jnp.where(index == h, ref[h], column)
    return column


def split(value, parts):
    pieces = []
    for _ in range(parts - 1):
        piece = value.astype(BF16).astype(F32)
        pieces.append(piece)
        value = value - piece
    return pieces + [value]


def doc_at(pos, starts_ref):
    count = jnp.int32(-1)
    for j in range(starts_ref.shape[0]):
        count = count + (pos >= starts_ref[j]).astype(jnp.int32)
    return count


def column_of(ref):
    heads = ref.shape[0]
    index = lax.broadcasted_iota(jnp.int32, (heads, 1), 0)
    column = jnp.zeros((heads, 1), F32)
    for h in range(heads):
        column = jnp.where(index == h, ref[h], column)
    return column


def split(value, parts):
    pieces = []
    for _ in range(parts - 1):
        piece = value.astype(BF16).astype(F32)
        pieces.append(piece)
        value = value - piece
    return pieces + [value]


def doc_at(pos, starts_ref):
    count = jnp.int32(-1)
    for j in range(starts_ref.shape[0]):
        count = count + (pos >= starts_ref[j]).astype(jnp.int32)
    return count


def column_of(ref):
    heads = ref.shape[0]
    index = lax.broadcasted_iota(jnp.int32, (heads, 1), 0)
    column = jnp.zeros((heads, 1), F32)
    for h in range(heads):
        column = jnp.where(index == h, ref[h], column)
    return column


def split(value, parts):
    pieces = []
    for _ in range(parts - 1):
        piece = value.astype(BF16).astype(F32)
        pieces.append(piece)
        value = value - piece
    return pieces + [value]


def doc_at(pos, starts_ref):
    count = jnp.int32(-1)
    for j in range(starts_ref.shape[0]):
        count = count + (pos >= starts_ref[j]).astype(jnp.int32)
    return count


def column_of(ref):
    heads = ref.shape[0]
    index = lax.broadcasted_iota(jnp.int32, (heads, 1), 0)
    column = jnp.zeros((heads, 1), F32)
    for h in range(heads):
        column = jnp.where(index == h, ref[h], column)
    return column


def split(value, parts):
    pieces = []
    for _ in range(parts - 1):
        piece = value.astype(BF16).astype(F32)
        pieces.append(piece)
        value = value - piece
    return pieces + [value]


def doc_at(pos, starts_ref):
    count = jnp.int32(-1)
    for j in range(starts_ref.shape[0]):
        count = count + (pos >= starts_ref[j]).astype(jnp.int32)
    return count


def column_of(ref):
    heads = ref.shape[0]
    index = lax.broadcasted_iota(jnp.int32, (heads, 1), 0)
    column = jnp.zeros((heads, 1), F32)
    for h in range(heads):
        column = jnp.where(index == h, ref[h], column)
    return column


def split(value, parts):
    pieces = []
    for _ in range(parts - 1):
        piece = value.astype(BF16).astype(F32)
        pieces.append(piece)
        value = value - piece
    return pieces + [value]


def doc_at(pos, starts_ref):
    count = jnp.int32(-1)
    for j in range(starts_ref.shape[0]):
        count = count + (pos >= starts_ref[j]).astype(jnp.int32)
    return count


def column_of(ref):
    heads = ref.shape[0]
    index = lax.broadcasted_iota(jnp.int32, (heads, 1), 0)
    column = jnp.zeros((heads, 1), F32)
    for h in range(heads):
        column = jnp.where(index == h, ref[h], column)
    return column


def split(value, parts):
    pieces = []
    for _ in range(parts - 1):
        piece = value.astype(BF16).astype(F32)
        pieces.append(piece)
        value = value - piece
    return pieces + [value]


def doc_at(pos, starts_ref):
    count = jnp.int32(-1)
    for j in range(starts_ref.shape[0]):
        count = count + (pos >= starts_ref[j]).astype(jnp.int32)
    return count


def column_of(ref):
    heads = ref.shape[0]
    index = lax.broadcasted_iota(jnp.int32, (heads, 1), 0)
    column = jnp.zeros((heads, 1), F32)
    for h in range(heads):
        column = jnp.where(index == h, ref[h], column)
    return column


def split(value, parts):
    pieces = []
    for _ in range(parts - 1):
        piece = value.astype(BF16).astype(F32)
        pieces.append(piece)
        value = value - piece
    return pieces + [value]


def doc_at(pos, starts_ref):
    count = jnp.int32(-1)
    for j in range(starts_ref.shape[0]):
        count = count + (pos >= starts_ref[j]).astype(jnp.int32)
    return count


def column_of(ref):
    heads = ref.shape[0]
    index = lax.broadcasted_iota(jnp.int32, (heads, 1), 0)
    column = jnp.zeros((heads, 1), F32)
    for h in range(heads):
        column = jnp.where(index == h, ref[h], column)
    return column


def split(value, parts):
    pieces = []
    for _ in range(parts - 1):
        piece = value.astype(BF16).astype(F32)
        pieces.append(piece)
        value = value - piece
    return pieces + [value]


def doc_at(pos, starts_ref):
    count = jnp.int32(-1)
    for j in range(starts_ref.shape[0]):
        count = count + (pos >= starts_ref[j]).astype(jnp.int32)
    return count


def column_of(ref):
    heads = ref.shape[0]
    index = lax.broadcasted_iota(jnp.int32, (heads, 1), 0)
    column = jnp.zeros((heads, 1), F32)
    for h in range(heads):
        column = jnp.where(index == h, ref[h], column)
    return column


def split(value, parts):
    pieces = []
    for _ in range(parts - 1):
        piece = value.astype(BF16).astype(F32)
        pieces.append(piece)
        value = value - piece
    return pieces + [value]


def params_kernel(
    starts_ref, bias_ref, alog_ref, skip_ref, dt_ref, far_x_ref,
    scale_ref, cols_ref, rows_ref, fade_ref, shift_ref, keep_ref, x_ref, sem,
):
    copies = []
    width = x_ref.shape[1]
    for part in range(4):
        lanes = pl.ds(part * (width // 4), width // 4)
        copies.append(pltpu.make_async_copy(far_x_ref.at[:, lanes], x_ref.at[:, lanes], sem.at[part]))
        copies[-1].start()
    first = lax.axis_index("seq") * BLK
    heads = dt_ref.shape[0]
    v = dt_ref[...] + column_of(bias_ref)
    step = jnp.maximum(v, 0.0) + jnp.log(1.0 + jnp.exp(-jnp.abs(v)))
    rate = -jnp.exp(column_of(alog_ref)) * step
    tri = (
        lax.broadcasted_iota(jnp.int32, (Q, Q), 0) <= lax.broadcasted_iota(jnp.int32, (Q, Q), 1)
    ).astype(F32)
    doc_before = doc_at(first - 1, starts_ref)
    doc_last = doc_at(first + BLK - 1, starts_ref)
    cums = []
    base = jnp.zeros((heads, 1), F32)
    for q in range(NQ):
        part = jnp.dot(
            rate[:, q * Q : (q + 1) * Q], tri, precision=lax.Precision.HIGHEST, preferred_element_type=F32
        )
        cums.append(part + base)
        base = base + part[:, Q - 1 : Q]
    for q in range(NQ):
        span = slice(q * Q, (q + 1) * Q)
        cum = cums[q]
        step_q = step[:, span]
        pos = first + q * Q + lax.broadcasted_iota(jnp.int32, (1, Q), 1)
        doc = doc_of(pos, starts_ref)
        tail = jnp.where(doc == doc_last, jnp.exp(base - cum) * step_q, 0.0)
        entry = jnp.where(doc == doc_before, jnp.exp(cum), 0.0)
        rest = jnp.zeros((D - 2 * heads, Q), F32)
        packed = split(tail, 2) + [rest]
        scale_ref[span, :] = jnp.transpose(jnp.concatenate(packed, axis=0), (1, 0)).astype(BF16)
        packed = [cum * LOG2E, entry, rest]
        cols_ref[span, :] = jnp.transpose(jnp.concatenate(packed, axis=0), (1, 0))
        terms = (cum - jnp.log(step_q)) * LOG2E
        for c in range(heads // HC):
            rows_ref[c, :, span] = terms[c * HC : (c + 1) * HC]
    decay = jnp.exp(base) * jnp.where(doc_last == doc_before, 1.0, 0.0)
    skip = column_of(skip_ref)
    for c in range(heads // HC):
        for i in range(HC):
            h = c * HC + i
            lanes = slice(i * D, (i + 1) * D)
            fade_ref[c, 0:1, lanes] = jnp.broadcast_to(skip[h : h + 1], (1, D))
            fade_ref[c, 1:2, lanes] = jnp.broadcast_to(decay[h : h + 1], (1, D))
    for q in range(NQ):
        row = lax.broadcasted_iota(jnp.int32, (Q, 2 * Q), 0)
        col = lax.broadcasted_iota(jnp.int32, (Q, 2 * Q), 1) - Q
        at = first + q * Q
        same = doc_of(at + row, starts_ref) == doc_of(at + col, starts_ref)
        for k in range(3):
            hit = same & (col == row - (3 - k))
            shift_ref[q, k * Q : (k + 1) * Q, :] = jnp.where(hit, 1.0, 0.0).astype(BF16)
        doc_row = doc_of(at + lax.broadcasted_iota(jnp.int32, (Q, BLK), 0), starts_ref)
        col = lax.broadcasted_iota(jnp.int32, (Q, BLK), 1)
        row = q * Q + lax.broadcasted_iota(jnp.int32, (Q, BLK), 0)
        keep = (row >= col) & (doc_row == doc_of(first + col, starts_ref))
        keep_ref[q * Q : (q + 1) * Q, :] = jnp.where(keep, 1.0, 0.0)
    for copy in copies:
        copy.wait()


def chooser(heads, chunk, lo, hi, width):
    k = lax.broadcasted_iota(jnp.int32, (D, width), 0)
    head = HC * chunk + lax.broadcasted_iota(jnp.int32, (D, width), 1) // D
    hit = ((k & (heads - 1)) == head) & (k >= lo * heads) & (k < hi * heads)
    return jnp.where(hit, 1.0, 0.0).astype(BF16)


def convolved(q, window, now, shift_ref, taps, bias):
    moved = jnp.dot(shift_ref[q], window, preferred_element_type=F32)
    total = (0.5 * taps[3]) * now.astype(F32) + 0.5 * bias
    for k in range(3):
        total = total + (0.5 * taps[k]) * moved[k * Q : (k + 1) * Q]
    return silu_half(total)


def window_of(q, edge_ref, x_ref):
    return edge_ref[...] if q == 0 else x_ref[(q - 1) * Q : (q + 1) * Q, :]


def edge(edge_ref, rim, x):
    width = x.shape[1]
    rim = jnp.concatenate([jnp.zeros((Q - RIM, width), F32), rim.astype(F32)], axis=0)
    edge_ref[0:Q, 0:width] = rim.astype(BF16)
    edge_ref[Q : 2 * Q, 0:width] = x


def state_body(
    chunk, heads, per_group, x_ref, rim_ref, wx_ref, bx_ref, shift_ref, scale_ref, bt_ref,
    mx_ref, end_ref, edge_ref, tail_ref, send_ref=None,
):
    wide = slice(chunk * CW, (chunk + 1) * CW)
    edge(edge_ref, rim_ref[:, wide], x_ref[0:Q, wide])
    pick = chooser(heads, chunk, 0, 2, CW)
    taps = [wx_ref[k : k + 1, wide] for k in range(4)]
    for q in range(NQ):
        span = slice(q * Q, (q + 1) * Q)
        window = x_ref[(q - 1) * Q : (q + 1) * Q, wide] if q else edge_ref[...]
        mixed = convolved(q, window, x_ref[span, wide], shift_ref, taps, bx_ref[:, wide])
        mx_ref[chunk, span, :] = mixed.astype(BF16)
        scale = jnp.dot(scale_ref[span, :], pick, preferred_element_type=F32)
        tail_ref[span, :] = (mixed * scale).astype(BF16)
    state = jnp.dot(bt_ref[chunk // per_group], tail_ref[...], preferred_element_type=F32)
    end_ref[chunk] = state
    if send_ref is not None:
        send_ref[...] = state.astype(BF16)


def first_kernel(
    x_ref, rim_ref, wx_ref, bx_ref, shift_ref, scale_ref, keep_ref, bc_ref, wbc_ref, bbc_ref,
    mx_ref, end_ref, send_ref, bt_ref, c_ref, score_ref,
    edge_ref, tail_ref, *, heads, per_group,
):
    groups = bt_ref.shape[0]
    wide = 2 * groups * D
    edge(edge_ref, rim_ref[:, x_ref.shape[1] :], bc_ref[0:Q, :])

    def joined(rows):
        return jnp.concatenate(rows, axis=1)

    taps = [joined([wbc_ref[k, p : p + 1, :] for p in range(2)]) for k in range(4)]
    bias = joined([bbc_ref[p : p + 1, :] for p in range(2)])
    for q in range(NQ):
        span = slice(q * Q, (q + 1) * Q)
        window = edge_ref[:, 0:wide] if q == 0 else bc_ref[(q - 1) * Q : (q + 1) * Q, :]
        mixed = convolved(q, window, bc_ref[span, :], shift_ref, taps, bias)
        upto = (q + 1) * Q
        for g in range(groups):
            bt_ref[g, :, span] = jnp.transpose(mixed[:, g * D : (g + 1) * D], (1, 0)).astype(BF16)
            c = mixed[:, (groups + g) * D : (groups + g + 1) * D].astype(BF16)
            c_ref[g, span, :] = c
            score = jnp.dot(c, bt_ref[g, :, 0:upto], preferred_element_type=F32)
            score_ref[g, span, 0:upto] = keep_ref[span, 0:upto] * score
    state_body(
        0, heads, per_group, x_ref, rim_ref, wx_ref, bx_ref, shift_ref, scale_ref, bt_ref,
        mx_ref, end_ref, edge_ref, tail_ref, send_ref,
    )


def more_kernel(
    x_ref, rim_ref, wx_ref, bx_ref, shift_ref, scale_ref, bt_ref, old1, old2,
    mx_ref, end_ref, *rest, heads, per_group, some, sends,
):
    for chunk in some:
        state_body(
            chunk, heads, per_group, x_ref, rim_ref, wx_ref, bx_ref, shift_ref, scale_ref,
            bt_ref, mx_ref, end_ref, *rest[-2:], *rest[:sends],
        )


def join_kernel(fade_ref, recv_ref, end_ref, token_ref, send_ref, *, turn, stream, per_stream):
    chunk = stream * per_stream + jnp.clip(turn - lax.axis_index("seq"), 0, per_stream - 1)
    send_ref[...] = (fade_ref[chunk, 1:2, :] * recv_ref[...].astype(F32) + end_ref[chunk]).astype(BF16)


def out_kernel(
    fade_ref, mx_ref, c_ref, score_ref, cols_ref, rows_ref, recv_ref,
    *rest, turn, stream, before, final, per_stream, per_group, heads,
):
    out_ref, block_ref, sem = rest[-3:]
    place = lax.axis_index("seq")

    def spot(when, which):
        chunk = which * per_stream + jnp.clip(when - place, 0, per_stream - 1)
        return pl.ds(pl.multiple_of(chunk * CW, CW), CW)

    def is_valid(when):
        return (when - place >= 0) & (when - place < per_stream)

    def half_copy(ref, when, which, half, slot=0):
        rows = pl.ds(half * 2 * Q, 2 * Q)
        return pltpu.make_async_copy(ref.at[rows, :], out_ref.at[rows, spot(when, which)], sem.at[2 * slot + half])

    if before:
        @pl.when(is_valid(before[0]))
        def send():
            for half in range(2):
                half_copy(rest[0], *before, half).start()

    @pl.when(is_valid(turn))
    def compute():
        chunk = stream * per_stream + turn - place
        g = lax.div(chunk, per_group)
        cols = pltpu.roll(cols_ref[...], lax.rem(D - HC * chunk, D), 1)
        far = jnp.dot(c_ref[g], recv_ref[...], preferred_element_type=F32)
        zero = jnp.zeros((Q, Q), BF16)
        for i in range(HC):
            lanes = slice(i * D, (i + 1) * D)
            cum = jnp.broadcast_to(cols[:, i : i + 1], (BLK, Q))
            entry = jnp.broadcast_to(cols[:, heads + i : heads + i + 1], (BLK, Q))
            tiles = []
            for q in range(NQ):
                span = slice(q * Q, (q + 1) * Q)
                line = []
                for j in range(q + 1):
                    there = slice(j * Q, (j + 1) * Q)
                    gap = cum[span] - rows_ref[chunk, i : i + 1, there]
                    if j == q:
                        gap = jnp.minimum(gap, 100.0)
                    line.append((score_ref[g, span, there] * jnp.exp2(gap)).astype(BF16))
                tiles.append(line + [zero] * (NQ - 1 - q))

            def weights(lines, halves):
                return jnp.concatenate([jnp.concatenate([tiles[q][j] for j in halves], axis=1) for q in lines], axis=0)

            left = jnp.dot(weights(range(NQ), (0, 1)), mx_ref[chunk, 0 : 2 * Q, lanes], preferred_element_type=F32)
            right = jnp.dot(weights((2, 3), (2, 3)), mx_ref[chunk, 2 * Q :, lanes], preferred_element_type=F32)
            for half in range(2):
                span = slice(half * 2 * Q, (half + 1) * 2 * Q)
                y = left[span] + right if half else left[span]
                x = mx_ref[chunk, span, lanes].astype(F32)
                y = y + entry[span] * far[span, lanes] + fade_ref[chunk, 0:1, lanes] * x
                block_ref[span, lanes] = y.astype(BF16)
        if final:
            for half in range(2):
                half_copy(block_ref, turn, stream, half, 1).start()
            for half in range(2):
                half_copy(block_ref, turn, stream, half, 1).wait()

    if before:
        @pl.when(is_valid(before[0]))
        def wait():
            for half in range(2):
                half_copy(rest[0], *before, half).wait()


SMEM = pl.BlockSpec(memory_space=pltpu.SMEM)
ROOM = pltpu.CompilerParams(vmem_limit_bytes=16 * 2**20)
ANY = pl.BlockSpec(memory_space=pl.ANY)
VMEM = pl.BlockSpec(memory_space=pltpu.VMEM)


def whole(shape):
    return pl.BlockSpec(shape, lambda *_: (0,) * len(shape))


def shape_of(shape, dtype):
    return jax.ShapeDtypeStruct(shape, dtype)


def per_device(
    x_raw, bc_raw, dt_raw, dt_bias, a_log, d_skip, conv_x, conv_x_bias, conv_bc, conv_bc_bias, doc_starts
):
    rows, width = x_raw.shape
    held = [x_raw, dt_raw, dt_bias, a_log, d_skip, conv_bc, conv_bc_bias, doc_starts]
    held = [pltpu.with_memory_space_constraint(a, pltpu.HBM) for a in held]
    x_far, dt_raw, dt_bias, a_log, d_skip, conv_bc, conv_bc_bias, doc_starts = held
    bias_x = conv_x_bias[None]
    groups = bc_raw.shape[2] // D
    heads = dt_raw.shape[0]
    chunks = heads // HC
    per_group = chunks // groups
    seq = lax.axis_size("seq")
    ring = [(i, (i + 1) % seq) for i in range(seq)]
    streams = 2
    per_stream = chunks // streams
    slots = per_stream + seq - 2

    tail = jnp.concatenate([x_raw[rows - RIM :], bc_raw[rows - RIM :].reshape(RIM, -1)], axis=1)
    rim = lax.ppermute(tail, "seq", ring)
    bc = bc_raw.reshape(rows, -1)

    scale, cols, row_terms, fade, shift, keep, x_near = pl.pallas_call(
        params_kernel,
        in_specs=[SMEM] * 4 + [VMEM, ANY],
        out_specs=[VMEM] * 7,
        out_shape=[
            shape_of((BLK, D), BF16),
            shape_of((BLK, D), F32),
            shape_of((chunks, HC, BLK), F32),
            shape_of((chunks, 2, CW), F32),
            shape_of((NQ, 3 * Q, 2 * Q), BF16),
            shape_of((BLK, BLK), F32),
            pltpu.VMEM((rows, width), BF16),
        ],
        scratch_shapes=[pltpu.SemaphoreType.DMA((4,))],
        compiler_params=ROOM,
        name="params",
    )(doc_starts, dt_bias, a_log, d_skip, dt_raw, x_far)

    big = [pltpu.VMEM((chunks, BLK, CW), BF16), pltpu.VMEM((chunks, D, CW), F32)]
    chunk_shape = shape_of((D, CW), BF16)
    scratch = [pltpu.VMEM((2 * Q, CW), BF16), pltpu.VMEM((BLK, CW), BF16)]
    mixed_x, end, send_a, bt, mixed_c, score = pl.pallas_call(
        functools.partial(first_kernel, heads=heads, per_group=per_group),
        in_specs=[VMEM] * 10,
        out_specs=[VMEM] * 6,
        out_shape=[
            *big,
            chunk_shape,
            shape_of((groups, D, BLK), BF16),
            shape_of((groups, BLK, D), BF16),
            shape_of((groups, BLK, BLK), F32),
        ],
        scratch_shapes=scratch,
        compiler_params=ROOM,
        name="first",
    )(x_near, rim, conv_x, bias_x, shift, scale, keep, bc, conv_bc, conv_bc_bias)

    def more(some, sends, mixed_x, end):
        return pl.pallas_call(
            functools.partial(more_kernel, heads=heads, per_group=per_group, some=some, sends=sends),
            in_specs=[VMEM] * 9,
            out_specs=[VMEM] * (2 + sends),
            out_shape=big + [chunk_shape] * sends,
            input_output_aliases={7: 0, 8: 1},
            scratch_shapes=scratch,
            compiler_params=ROOM,
            cost_estimate=pl.CostEstimate(
                flops=4 * len(some) * BLK * D * CW, bytes_accessed=4 * len(some) * BLK * CW, transcendentals=0
            ),
            name="more",
        )(x_near, rim, conv_x, bias_x, shift, scale, bt, near(mixed_x), near(end))

    def near(array):
        return pltpu.with_memory_space_constraint(array, pltpu.VMEM)

    flying = [lax.ppermute(send_a, "seq", ring), None]
    mixed_x, end, send_b = more([per_stream], 1, mixed_x, end)
    flying[1] = lax.ppermute(send_b, "seq", ring)

    def join(turn, s, recv, token):
        return pl.pallas_call(
            functools.partial(join_kernel, turn=turn, stream=s, per_stream=per_stream),
            in_specs=[VMEM, VMEM, VMEM, ANY],
            out_specs=VMEM,
            out_shape=chunk_shape,
            compiler_params=ROOM,
            name="join",
        )(fade, recv, end, token)

    def output(turn, s, recv, before, block, out):
        old = [] if out is None else [block, out]
        return pl.pallas_call(
            functools.partial(
                out_kernel, turn=turn, stream=s, before=before, final=turn == slots and s == streams - 1,
                per_stream=per_stream, per_group=per_group, heads=heads,
            ),
            in_specs=[VMEM] * 7 + [VMEM, ANY][: len(old)],
            out_specs=[ANY, VMEM],
            out_shape=[pltpu.HBM((BLK, width), BF16), shape_of((BLK, CW), BF16)],
            input_output_aliases={8: 0} if old else {},
            scratch_shapes=[pltpu.SemaphoreType.DMA((4,))],
            compiler_params=ROOM,
            cost_estimate=pl.CostEstimate(
                flops=8 * BLK * Q * CW, bytes_accessed=6 * BLK * CW, transcendentals=0
            ),
            name="out",
        )(fade, mixed_x, mixed_c, score, cols, row_terms, recv, *old)

    out, block, before = None, None, None
    carried = [send_a, send_b]
    for turn in range(slots + 1):
        if 0 < turn < per_stream:
            mixed_x, end = more([turn + i * per_stream for i in range(streams)], 0, mixed_x, end)
        for s in range(streams):
            if turn:
                recv = flying[s]
                if turn < slots:
                    flying[s] = lax.ppermute(join(turn, s, recv, block), "seq", ring)
                carried[s] = recv
            out, block = output(turn, s, carried[s], before, block, out)
            before = (turn, s)
    return out


def solution(mesh):
    return jax.shard_map(
        per_device,
        mesh=mesh,
        in_specs=(
            P(("groups", "seq"), ("head", "sub")),
            P(("groups", "seq"), None, ("head", "sub")),
            P(("head", "sub"), ("groups", "seq")),
            P(("head", "sub")),
            P(("head", "sub")),
            P(("head", "sub")),
            P(None, ("head", "sub")),
            P(("head", "sub")),
            P(None, None, ("head", "sub")),
            P(None, ("head", "sub")),
            P("groups"),
        ),
        out_specs=P(("groups", "seq"), ("head", "sub")),
        check_vma=False,
    )
```

```python
import functools
import math

import jax
import jax.numpy as jnp
from jax import lax
from jax.experimental import pallas as pl
from jax.experimental.pallas import tpu as pltpu
from jax.sharding import PartitionSpec as P

D = 128
Q = 128
BLK = 512
NQ = BLK // Q
HC = 4
CW = HC * D
PARTS = 2
PW = CW // PARTS
RIM = 8
LOG2E = math.log2(math.e)
F32 = jnp.float32
BF16 = jnp.bfloat16


def doc_of(pos, starts_ref):
    count = jnp.zeros_like(pos)
    for j in range(starts_ref.shape[0]):
        count = count + (pos >= starts_ref[j]).astype(jnp.int32)
    return count - 1


def silu_half(u):
    return u + u * jnp.tanh(u)


def doc_at(pos, starts_ref):
    count = jnp.int32(-1)
    for j in range(starts_ref.shape[0]):
        count = count + (pos >= starts_ref[j]).astype(jnp.int32)
    return count


def column_of(ref):
    heads = ref.shape[0]
    index = lax.broadcasted_iota(jnp.int32, (heads, 1), 0)
    column = jnp.zeros((heads, 1), F32)
    for h in range(heads):
        column = jnp.where(index == h, ref[h], column)
    return column


def split(value, parts):
    pieces = []
    for _ in range(parts - 1):
        piece = value.astype(BF16).astype(F32)
        pieces.append(piece)
        value = value - piece
    return pieces + [value]


def doc_at(pos, starts_ref):
    count = jnp.int32(-1)
    for j in range(starts_ref.shape[0]):
        count = count + (pos >= starts_ref[j]).astype(jnp.int32)
    return count


def column_of(ref):
    heads = ref.shape[0]
    index = lax.broadcasted_iota(jnp.int32, (heads, 1), 0)
    column = jnp.zeros((heads, 1), F32)
    for h in range(heads):
        column = jnp.where(index == h, ref[h], column)
    return column


def split(value, parts):
    pieces = []
    for _ in range(parts - 1):
        piece = value.astype(BF16).astype(F32)
        pieces.append(piece)
        value = value - piece
    return pieces + [value]


def doc_at(pos, starts_ref):
    count = jnp.int32(-1)
    for j in range(starts_ref.shape[0]):
        count = count + (pos >= starts_ref[j]).astype(jnp.int32)
    return count


def column_of(ref):
    heads = ref.shape[0]
    index = lax.broadcasted_iota(jnp.int32, (heads, 1), 0)
    column = jnp.zeros((heads, 1), F32)
    for h in range(heads):
        column = jnp.where(index == h, ref[h], column)
    return column


def split(value, parts):
    pieces = []
    for _ in range(parts - 1):
        piece = value.astype(BF16).astype(F32)
        pieces.append(piece)
        value = value - piece
    return pieces + [value]


def doc_at(pos, starts_ref):
    count = jnp.int32(-1)
    for j in range(starts_ref.shape[0]):
        count = count + (pos >= starts_ref[j]).astype(jnp.int32)
    return count


def column_of(ref):
    heads = ref.shape[0]
    index = lax.broadcasted_iota(jnp.int32, (heads, 1), 0)
    column = jnp.zeros((heads, 1), F32)
    for h in range(heads):
        column = jnp.where(index == h, ref[h], column)
    return column


def split(value, parts):
    pieces = []
    for _ in range(parts - 1):
        piece = value.astype(BF16).astype(F32)
        pieces.append(piece)
        value = value - piece
    return pieces + [value]


def doc_at(pos, starts_ref):
    count = jnp.int32(-1)
    for j in range(starts_ref.shape[0]):
        count = count + (pos >= starts_ref[j]).astype(jnp.int32)
    return count


def column_of(ref):
    heads = ref.shape[0]
    index = lax.broadcasted_iota(jnp.int32, (heads, 1), 0)
    column = jnp.zeros((heads, 1), F32)
    for h in range(heads):
        column = jnp.where(index == h, ref[h], column)
    return column


def split(value, parts):
    pieces = []
    for _ in range(parts - 1):
        piece = value.astype(BF16).astype(F32)
        pieces.append(piece)
        value = value - piece
    return pieces + [value]


def doc_at(pos, starts_ref):
    count = jnp.int32(-1)
    for j in range(starts_ref.shape[0]):
        count = count + (pos >= starts_ref[j]).astype(jnp.int32)
    return count


def column_of(ref):
    heads = ref.shape[0]
    index = lax.broadcasted_iota(jnp.int32, (heads, 1), 0)
    column = jnp.zeros((heads, 1), F32)
    for h in range(heads):
        column = jnp.where(index == h, ref[h], column)
    return column


def split(value, parts):
    pieces = []
    for _ in range(parts - 1):
        piece = value.astype(BF16).astype(F32)
        pieces.append(piece)
        value = value - piece
    return pieces + [value]


def doc_at(pos, starts_ref):
    count = jnp.int32(-1)
    for j in range(starts_ref.shape[0]):
        count = count + (pos >= starts_ref[j]).astype(jnp.int32)
    return count


def column_of(ref):
    heads = ref.shape[0]
    index = lax.broadcasted_iota(jnp.int32, (heads, 1), 0)
    column = jnp.zeros((heads, 1), F32)
    for h in range(heads):
        column = jnp.where(index == h, ref[h], column)
    return column


def split(value, parts):
    pieces = []
    for _ in range(parts - 1):
        piece = value.astype(BF16).astype(F32)
        pieces.append(piece)
        value = value - piece
    return pieces + [value]


def doc_at(pos, starts_ref):
    count = jnp.int32(-1)
    for j in range(starts_ref.shape[0]):
        count = count + (pos >= starts_ref[j]).astype(jnp.int32)
    return count


def column_of(ref):
    heads = ref.shape[0]
    index = lax.broadcasted_iota(jnp.int32, (heads, 1), 0)
    column = jnp.zeros((heads, 1), F32)
    for h in range(heads):
        column = jnp.where(index == h, ref[h], column)
    return column


def split(value, parts):
    pieces = []
    for _ in range(parts - 1):
        piece = value.astype(BF16).astype(F32)
        pieces.append(piece)
        value = value - piece
    return pieces + [value]


def doc_at(pos, starts_ref):
    count = jnp.int32(-1)
    for j in range(starts_ref.shape[0]):
        count = count + (pos >= starts_ref[j]).astype(jnp.int32)
    return count


def column_of(ref):
    heads = ref.shape[0]
    index = lax.broadcasted_iota(jnp.int32, (heads, 1), 0)
    column = jnp.zeros((heads, 1), F32)
    for h in range(heads):
        column = jnp.where(index == h, ref[h], column)
    return column


def split(value, parts):
    pieces = []
    for _ in range(parts - 1):
        piece = value.astype(BF16).astype(F32)
        pieces.append(piece)
        value = value - piece
    return pieces + [value]


def doc_at(pos, starts_ref):
    count = jnp.int32(-1)
    for j in range(starts_ref.shape[0]):
        count = count + (pos >= starts_ref[j]).astype(jnp.int32)
    return count


def column_of(ref):
    heads = ref.shape[0]
    index = lax.broadcasted_iota(jnp.int32, (heads, 1), 0)
    column = jnp.zeros((heads, 1), F32)
    for h in range(heads):
        column = jnp.where(index == h, ref[h], column)
    return column


def split(value, parts):
    pieces = []
    for _ in range(parts - 1):
        piece = value.astype(BF16).astype(F32)
        pieces.append(piece)
        value = value - piece
    return pieces + [value]


def doc_at(pos, starts_ref):
    count = jnp.int32(-1)
    for j in range(starts_ref.shape[0]):
        count = count + (pos >= starts_ref[j]).astype(jnp.int32)
    return count


def column_of(ref):
    heads = ref.shape[0]
    index = lax.broadcasted_iota(jnp.int32, (heads, 1), 0)
    column = jnp.zeros((heads, 1), F32)
    for h in range(heads):
        column = jnp.where(index == h, ref[h], column)
    return column


def split(value, parts):
    pieces = []
    for _ in range(parts - 1):
        piece = value.astype(BF16).astype(F32)
        pieces.append(piece)
        value = value - piece
    return pieces + [value]


def doc_at(pos, starts_ref):
    count = jnp.int32(-1)
    for j in range(starts_ref.shape[0]):
        count = count + (pos >= starts_ref[j]).astype(jnp.int32)
    return count


def column_of(ref):
    heads = ref.shape[0]
    index = lax.broadcasted_iota(jnp.int32, (heads, 1), 0)
    column = jnp.zeros((heads, 1), F32)
    for h in range(heads):
        column = jnp.where(index == h, ref[h], column)
    return column


def split(value, parts):
    pieces = []
    for _ in range(parts - 1):
        piece = value.astype(BF16).astype(F32)
        pieces.append(piece)
        value = value - piece
    return pieces + [value]


def doc_at(pos, starts_ref):
    count = jnp.int32(-1)
    for j in range(starts_ref.shape[0]):
        count = count + (pos >= starts_ref[j]).astype(jnp.int32)
    return count


def column_of(ref):
    heads = ref.shape[0]
    index = lax.broadcasted_iota(jnp.int32, (heads, 1), 0)
    column = jnp.zeros((heads, 1), F32)
    for h in range(heads):
        column = jnp.where(index == h, ref[h], column)
    return column


def split(value, parts):
    pieces = []
    for _ in range(parts - 1):
        piece = value.astype(BF16).astype(F32)
        pieces.append(piece)
        value = value - piece
    return pieces + [value]


def doc_at(pos, starts_ref):
    count = jnp.int32(-1)
    for j in range(starts_ref.shape[0]):
        count = count + (pos >= starts_ref[j]).astype(jnp.int32)
    return count


def column_of(ref):
    heads = ref.shape[0]
    index = lax.broadcasted_iota(jnp.int32, (heads, 1), 0)
    column = jnp.zeros((heads, 1), F32)
    for h in range(heads):
        column = jnp.where(index == h, ref[h], column)
    return column


def split(value, parts):
    pieces = []
    for _ in range(parts - 1):
        piece = value.astype(BF16).astype(F32)
        pieces.append(piece)
        value = value - piece
    return pieces + [value]


def doc_at(pos, starts_ref):
    count = jnp.int32(-1)
    for j in range(starts_ref.shape[0]):
        count = count + (pos >= starts_ref[j]).astype(jnp.int32)
    return count


def column_of(ref):
    heads = ref.shape[0]
    index = lax.broadcasted_iota(jnp.int32, (heads, 1), 0)
    column = jnp.zeros((heads, 1), F32)
    for h in range(heads):
        column = jnp.where(index == h, ref[h], column)
    return column


def split(value, parts):
    pieces = []
    for _ in range(parts - 1):
        piece = value.astype(BF16).astype(F32)
        pieces.append(piece)
        value = value - piece
    return pieces + [value]


def params_kernel(
    starts_ref, bias_ref, alog_ref, skip_ref, dt_ref, far_x_ref,
    scale_ref, cols_ref, rows_ref, fade_ref, shift_ref, keep_ref, x_ref, sem,
):
    copies = []
    width = x_ref.shape[1]
    for part in range(4):
        lanes = pl.ds(part * (width // 4), width // 4)
        copies.append(pltpu.make_async_copy(far_x_ref.at[:, lanes], x_ref.at[:, lanes], sem.at[part]))
        copies[-1].start()
    first = lax.axis_index("seq") * BLK
    heads = dt_ref.shape[0]
    v = dt_ref[...] + column_of(bias_ref)
    step = jnp.maximum(v, 0.0) + jnp.log(1.0 + jnp.exp(-jnp.abs(v)))
    rate = -jnp.exp(column_of(alog_ref)) * step
    tri = (
        lax.broadcasted_iota(jnp.int32, (Q, Q), 0) <= lax.broadcasted_iota(jnp.int32, (Q, Q), 1)
    ).astype(F32)
    doc_before = doc_at(first - 1, starts_ref)
    doc_last = doc_at(first + BLK - 1, starts_ref)
    cums = []
    base = jnp.zeros((heads, 1), F32)
    for q in range(NQ):
        part = jnp.dot(
            rate[:, q * Q : (q + 1) * Q], tri, precision=lax.Precision.HIGHEST, preferred_element_type=F32
        )
        cums.append(part + base)
        base = base + part[:, Q - 1 : Q]
    for q in range(NQ):
        span = slice(q * Q, (q + 1) * Q)
        cum = cums[q]
        step_q = step[:, span]
        pos = first + q * Q + lax.broadcasted_iota(jnp.int32, (1, Q), 1)
        doc = doc_of(pos, starts_ref)
        tail = jnp.where(doc == doc_last, jnp.exp(base - cum) * step_q, 0.0)
        entry = jnp.where(doc == doc_before, jnp.exp(cum), 0.0)
        rest = jnp.zeros((D - 2 * heads, Q), F32)
        packed = split(tail, 2) + [rest]
        scale_ref[span, :] = jnp.transpose(jnp.concatenate(packed, axis=0), (1, 0)).astype(BF16)
        packed = [cum * LOG2E, entry, rest]
        cols_ref[span, :] = jnp.transpose(jnp.concatenate(packed, axis=0), (1, 0))
        terms = (cum - jnp.log(step_q)) * LOG2E
        for c in range(heads // HC):
            rows_ref[c, :, span] = terms[c * HC : (c + 1) * HC]
    decay = jnp.exp(base) * jnp.where(doc_last == doc_before, 1.0, 0.0)
    skip = column_of(skip_ref)
    for c in range(heads // HC):
        for i in range(HC):
            h = c * HC + i
            lanes = slice(i * D, (i + 1) * D)
            fade_ref[c, 0:1, lanes] = jnp.broadcast_to(skip[h : h + 1], (1, D))
            fade_ref[c, 1:2, lanes] = jnp.broadcast_to(decay[h : h + 1], (1, D))
    for q in range(NQ):
        row = lax.broadcasted_iota(jnp.int32, (Q, 2 * Q), 0)
        col = lax.broadcasted_iota(jnp.int32, (Q, 2 * Q), 1) - Q
        at = first + q * Q
        same = doc_of(at + row, starts_ref) == doc_of(at + col, starts_ref)
        for k in range(3):
            hit = same & (col == row - (3 - k))
            shift_ref[q, k * Q : (k + 1) * Q, :] = jnp.where(hit, 1.0, 0.0).astype(BF16)
        doc_row = doc_of(at + lax.broadcasted_iota(jnp.int32, (Q, BLK), 0), starts_ref)
        col = lax.broadcasted_iota(jnp.int32, (Q, BLK), 1)
        row = q * Q + lax.broadcasted_iota(jnp.int32, (Q, BLK), 0)
        keep = (row >= col) & (doc_row == doc_of(first + col, starts_ref))
        keep_ref[q * Q : (q + 1) * Q, :] = jnp.where(keep, 1.0, 0.0)
    for copy in copies:
        copy.wait()


def chooser(heads, chunk, lo, hi, width):
    k = lax.broadcasted_iota(jnp.int32, (D, width), 0)
    head = HC * chunk + lax.broadcasted_iota(jnp.int32, (D, width), 1) // D
    hit = ((k & (heads - 1)) == head) & (k >= lo * heads) & (k < hi * heads)
    return jnp.where(hit, 1.0, 0.0).astype(BF16)


def convolved(q, window, now, shift_ref, taps, bias):
    moved = jnp.dot(shift_ref[q], window, preferred_element_type=F32)
    total = (0.5 * taps[3]) * now.astype(F32) + 0.5 * bias
    for k in range(3):
        total = total + (0.5 * taps[k]) * moved[k * Q : (k + 1) * Q]
    return silu_half(total)


def window_of(q, edge_ref, x_ref):
    return edge_ref[...] if q == 0 else x_ref[(q - 1) * Q : (q + 1) * Q, :]


def edge(edge_ref, rim, x):
    width = x.shape[1]
    if rim is None:
        rim = jnp.zeros((Q, width), F32)
    else:
        rim = jnp.concatenate([jnp.zeros((Q - RIM, width), F32), rim.astype(F32)], axis=0)
    edge_ref[0:Q, 0:width] = rim.astype(BF16)
    edge_ref[Q : 2 * Q, 0:width] = x


def state_of(
    chunk, heads, x_ref, rim, wx_ref, bx_ref, shift_ref, scale_ref, bt, edge_ref, tail_ref, mx_ref=None
):
    wide = slice(chunk * CW, (chunk + 1) * CW)
    edge(edge_ref, rim, x_ref[0:Q, :])
    pick = chooser(heads, chunk, 0, 2, CW)
    taps = [wx_ref[k : k + 1, wide] for k in range(4)]
    for q in range(NQ):
        span = slice(q * Q, (q + 1) * Q)
        window = x_ref[(q - 1) * Q : (q + 1) * Q, :] if q else edge_ref[:, 0:CW]
        mixed = convolved(q, window, x_ref[span, :], shift_ref, taps, bx_ref[:, wide])
        if mx_ref is not None:
            mx_ref[chunk, span, :] = mixed.astype(BF16)
        scale = jnp.dot(scale_ref[span, :], pick, preferred_element_type=F32)
        tail_ref[span, :] = (mixed * scale).astype(BF16)
    return jnp.dot(bt, tail_ref[...], preferred_element_type=F32)


def chunk_of(x_ref, chunk):
    return x_ref.at[:, pl.ds(chunk * CW, CW)]


def mixed_of(q, part, edge_ref, bc_ref, shift_ref, wbc_ref, bbc_ref, wide):
    half = slice(part * wide, (part + 1) * wide)
    window = bc_ref[(q - 1) * Q : (q + 1) * Q, half] if q else edge_ref[:, 0:wide]
    taps = [wbc_ref[k, part : part + 1, :] for k in range(4)]
    return convolved(q, window, bc_ref[q * Q : (q + 1) * Q, half], shift_ref, taps, bbc_ref[part : part + 1, :])


def first_kernel(
    x_ref, rim_ref, wx_ref, bx_ref, shift_ref, scale_ref, bc_ref, wbc_ref, bbc_ref,
    mx_ref, end_ref, send_ref, bt_ref, edge_ref, tail_ref, *, heads,
):
    groups = bt_ref.shape[0]
    wide = groups * D
    start = x_ref.shape[1]
    edge(edge_ref, rim_ref[:, start : start + wide], bc_ref[0:Q, 0:wide])
    for q in range(NQ):
        mixed = mixed_of(q, 0, edge_ref, bc_ref, shift_ref, wbc_ref, bbc_ref, wide)
        for g in range(groups):
            bt_ref[g, :, q * Q : (q + 1) * Q] = jnp.transpose(mixed[:, g * D : (g + 1) * D], (1, 0)).astype(BF16)
    state = state_of(
        0, heads, chunk_of(x_ref, 0), rim_ref[:, 0:CW], wx_ref, bx_ref, shift_ref, scale_ref, bt_ref[0],
        edge_ref, tail_ref, mx_ref,
    )
    end_ref[0] = state
    send_ref[...] = state.astype(BF16)


def score_kernel(
    rim_ref, shift_ref, keep_ref, bc_ref, wbc_ref, bbc_ref, bt_ref, after_ref, c_ref, score_ref, edge_ref
):
    groups = bt_ref.shape[0]
    wide = groups * D
    start = rim_ref.shape[1] - wide
    edge(edge_ref, rim_ref[:, start:], bc_ref[0:Q, wide:])
    for q in range(NQ):
        span = slice(q * Q, (q + 1) * Q)
        upto = (q + 1) * Q
        mixed = mixed_of(q, 1, edge_ref, bc_ref, shift_ref, wbc_ref, bbc_ref, wide)
        for g in range(groups):
            c = mixed[:, g * D : (g + 1) * D].astype(BF16)
            c_ref[g, span, :] = c
            score = jnp.dot(c, bt_ref[g, :, 0:upto], preferred_element_type=F32)
            score_ref[g, span, 0:upto] = keep_ref[span, 0:upto] * score


def more_kernel(
    x_ref, rim_ref, wx_ref, bx_ref, shift_ref, scale_ref, bt_ref, old1, old2,
    mx_ref, end_ref, *rest, heads, per_group, some,
):
    edge_ref, tail_ref = rest[-2:]
    for chunk in some:
        wide = slice(chunk * CW, (chunk + 1) * CW)
        state = state_of(
            chunk, heads, chunk_of(x_ref, chunk), rim_ref[:, wide], wx_ref, bx_ref, shift_ref, scale_ref,
            bt_ref[chunk // per_group], edge_ref, tail_ref, mx_ref,
        )
        end_ref[chunk] = state
        for send_ref in rest[:-2]:
            send_ref[...] = state.astype(BF16)


def join_kernel(fade_ref, recv_ref, end_ref, token_ref, send_ref, *, turn, stream, per_stream):
    chunk = stream * per_stream + jnp.clip(turn - lax.axis_index("seq"), 0, per_stream - 1)
    send_ref[...] = (fade_ref[chunk, 1:2, :] * recv_ref[...].astype(F32) + end_ref[chunk]).astype(BF16)


def out_kernel(
    fade_ref, mx_ref, c_ref, score_ref, cols_ref, rows_ref, recv_ref,
    *rest, turn, stream, before, final, per_stream, per_group, heads,
):
    out_ref, block_ref, sem = rest[-3:]
    place = lax.axis_index("seq")

    def spot(when, which):
        chunk = which * per_stream + jnp.clip(when - place, 0, per_stream - 1)
        return pl.ds(pl.multiple_of(chunk * CW, CW), CW)

    def is_valid(when):
        return (when - place >= 0) & (when - place < per_stream)

    def half_copy(ref, when, which, half):
        rows = pl.ds(half * 2 * Q, 2 * Q)
        return pltpu.make_async_copy(ref.at[rows, :], out_ref.at[rows, spot(when, which)], sem.at[half])

    if before:
        @pl.when(is_valid(before[0]))
        def send():
            for half in range(2):
                half_copy(rest[0], *before, half).start()

    @pl.when(is_valid(turn))
    def compute():
        chunk = stream * per_stream + turn - place
        g = lax.div(chunk, per_group)
        cols = pltpu.roll(cols_ref[...], lax.rem(D - HC * chunk, D), 1)
        far = jnp.dot(c_ref[g], recv_ref[...], preferred_element_type=F32)
        zero = jnp.zeros((Q, Q), BF16)
        last = []
        for i in range(HC):
            lanes = slice(i * D, (i + 1) * D)
            cum = jnp.broadcast_to(cols[:, i : i + 1], (BLK, Q))
            entry = jnp.broadcast_to(cols[:, heads + i : heads + i + 1], (BLK, Q))
            tiles = []
            for q in range(NQ):
                span = slice(q * Q, (q + 1) * Q)
                line = []
                for j in range(q + 1):
                    there = slice(j * Q, (j + 1) * Q)
                    gap = cum[span] - rows_ref[chunk, i : i + 1, there]
                    if j == q:
                        gap = jnp.minimum(gap, 100.0)
                    line.append((score_ref[g, span, there] * jnp.exp2(gap)).astype(BF16))
                tiles.append(line + [zero] * (NQ - 1 - q))

            def weights(lines, halves):
                return jnp.concatenate([jnp.concatenate([tiles[q][j] for j in halves], axis=1) for q in lines], axis=0)

            left = jnp.dot(weights(range(NQ), (0, 1)), mx_ref[chunk, 0 : 2 * Q, lanes], preferred_element_type=F32)
            right = jnp.dot(weights((2, 3), (2, 3)), mx_ref[chunk, 2 * Q :, lanes], preferred_element_type=F32)
            for half in range(2):
                span = slice(half * 2 * Q, (half + 1) * 2 * Q)
                y = left[span] + right if half else left[span]
                x = mx_ref[chunk, span, lanes].astype(F32)
                y = y + entry[span] * far[span, lanes] + fade_ref[chunk, 0:1, lanes] * x
                block_ref[span, lanes] = y.astype(BF16)
            if final:
                there = pl.ds(pl.multiple_of(chunk * CW + i * D, D), D)
                last.append(
                    pltpu.make_async_copy(block_ref.at[:, pl.ds(i * D, D)], out_ref.at[:, there], sem.at[2 + i])
                )
                last[-1].start()
        for copy in last:
            copy.wait()

    if before:
        @pl.when(is_valid(before[0]))
        def wait():
            for half in range(2):
                half_copy(rest[0], *before, half).wait()


SMEM = pl.BlockSpec(memory_space=pltpu.SMEM)
ROOM = pltpu.CompilerParams(vmem_limit_bytes=16 * 2**20)
ANY = pl.BlockSpec(memory_space=pl.ANY)
VMEM = pl.BlockSpec(memory_space=pltpu.VMEM)


def whole(shape):
    return pl.BlockSpec(shape, lambda *_: (0,) * len(shape))


def shape_of(shape, dtype):
    return jax.ShapeDtypeStruct(shape, dtype)


def per_device(
    x_raw, bc_raw, dt_raw, dt_bias, a_log, d_skip, conv_x, conv_x_bias, conv_bc, conv_bc_bias, doc_starts
):
    rows, width = x_raw.shape
    held = [x_raw, dt_raw, dt_bias, a_log, d_skip, conv_bc, conv_bc_bias, doc_starts]
    held = [pltpu.with_memory_space_constraint(a, pltpu.HBM) for a in held]
    x_far, dt_raw, dt_bias, a_log, d_skip, conv_bc, conv_bc_bias, doc_starts = held
    bias_x = conv_x_bias[None]
    groups = bc_raw.shape[2] // D
    heads = dt_raw.shape[0]
    chunks = heads // HC
    per_group = chunks // groups
    seq = lax.axis_size("seq")
    ring = [(i, (i + 1) % seq) for i in range(seq)]
    swaps = [(i, i ^ 1) for i in range(seq)] if seq % 2 == 0 else ring
    streams = 2
    per_stream = chunks // streams
    slots = per_stream + seq - 2

    tail = jnp.concatenate([x_raw[rows - RIM :], bc_raw[rows - RIM :].reshape(RIM, -1)], axis=1)
    rim = lax.ppermute(tail, "seq", ring)
    bc = bc_raw.reshape(rows, -1)

    scale, cols, row_terms, fade, shift, keep, x_near = pl.pallas_call(
        params_kernel,
        in_specs=[SMEM] * 4 + [VMEM, ANY],
        out_specs=[VMEM] * 7,
        out_shape=[
            shape_of((BLK, D), BF16),
            shape_of((BLK, D), F32),
            shape_of((chunks, HC, BLK), F32),
            shape_of((chunks, 2, CW), F32),
            shape_of((NQ, 3 * Q, 2 * Q), BF16),
            shape_of((BLK, BLK), F32),
            pltpu.VMEM((rows, width), BF16),
        ],
        scratch_shapes=[pltpu.SemaphoreType.DMA((4,))],
        compiler_params=ROOM,
        name="params",
    )(doc_starts, dt_bias, a_log, d_skip, dt_raw, x_far)

    big = [pltpu.VMEM((chunks, BLK, CW), BF16), pltpu.VMEM((chunks, D, CW), F32)]
    chunk_shape = shape_of((D, CW), BF16)
    bt_shape = shape_of((groups, D, BLK), BF16)
    scratch = [pltpu.VMEM((2 * Q, max(CW, 2 * groups * D)), BF16), pltpu.VMEM((BLK, CW), BF16)]

    mixed_x, end, send, bt = pl.pallas_call(
        functools.partial(first_kernel, heads=heads),
        in_specs=[VMEM] * 9,
        out_specs=[VMEM] * 4,
        out_shape=[*big, chunk_shape, bt_shape],
        scratch_shapes=scratch,
        compiler_params=ROOM,
        name="first",
    )(x_near, rim, conv_x, bias_x, shift, scale, bc, conv_bc, conv_bc_bias)

    def near(array):
        return pltpu.with_memory_space_constraint(array, pltpu.VMEM)

    def more(some, sends, mixed_x, end):
        return pl.pallas_call(
            functools.partial(more_kernel, heads=heads, per_group=per_group, some=some),
            in_specs=[VMEM] * 9,
            out_specs=[VMEM] * (2 + sends),
            out_shape=big + [chunk_shape] * sends,
            input_output_aliases={7: 0, 8: 1},
            scratch_shapes=scratch,
            compiler_params=ROOM,
            cost_estimate=pl.CostEstimate(
                flops=4 * len(some) * BLK * D * CW, bytes_accessed=4 * len(some) * BLK * CW, transcendentals=0
            ),
            name="more",
        )(x_near, rim, conv_x, bias_x, shift, scale, bt, near(mixed_x), near(end))

    begun = [send]
    flying = [lax.ppermute(send, "seq", swaps)]
    for s in range(1, streams):
        mixed_x, end, send = more([s * per_stream], 1, mixed_x, end)
        begun.append(send)
        flying.append(lax.ppermute(send, "seq", swaps))

    def scores(after):
        return pl.pallas_call(
            score_kernel,
            in_specs=[VMEM] * 7 + [ANY],
            out_specs=[VMEM] * 2,
            out_shape=[shape_of((groups, BLK, D), BF16), shape_of((groups, BLK, BLK), F32)],
            scratch_shapes=scratch[:1],
            compiler_params=ROOM,
            name="score",
        )(rim, shift, keep, bc, conv_bc, conv_bc_bias, bt, after)

    def join(turn, s, recv, token):
        return pl.pallas_call(
            functools.partial(join_kernel, turn=turn, stream=s, per_stream=per_stream),
            in_specs=[VMEM, VMEM, VMEM, ANY],
            out_specs=VMEM,
            out_shape=chunk_shape,
            compiler_params=ROOM,
            name="join",
        )(fade, recv, end, token)

    def output(turn, s, recv, before, block, out, mixed_c, score):
        old = [] if out is None else [block, out]
        return pl.pallas_call(
            functools.partial(
                out_kernel, turn=turn, stream=s, before=before, final=turn == slots and s == streams - 1,
                per_stream=per_stream, per_group=per_group, heads=heads,
            ),
            in_specs=[VMEM] * 7 + [VMEM, ANY][: len(old)],
            out_specs=[ANY, VMEM],
            out_shape=[pltpu.HBM((BLK, width), BF16), shape_of((BLK, CW), BF16)],
            input_output_aliases={8: 0} if old else {},
            scratch_shapes=[pltpu.SemaphoreType.DMA((2 + HC,))],
            compiler_params=ROOM,
            cost_estimate=pl.CostEstimate(
                flops=8 * BLK * Q * CW, bytes_accessed=6 * BLK * CW, transcendentals=0
            ),
            name="out",
        )(fade, mixed_x, mixed_c, score, cols, row_terms, recv, *old)

    out, block, before = None, None, None
    waiting = [(0, s, begun[s]) for s in range(streams)]
    token = bt
    for turn in range(1, slots + 1):
        if turn < per_stream:
            mixed_x, end = more([turn + i * per_stream for i in range(streams)], 0, mixed_x, end)
        for s in range(streams):
            recv = flying[s]
            if turn < slots:
                send = join(turn, s, recv, token)
                flying[s] = lax.ppermute(send, "seq", swaps if turn == slots - 1 else ring)
            if turn == 1 and s == 0:
                mixed_c, score = scores(send)
            todo = [(turn, s, recv)]
            if waiting and turn >= min(per_stream, slots):
                todo.insert(0, waiting.pop(0))
            for when, which, got in todo:
                out, token = output(when, which, got, before, token, out, mixed_c, score)
                before = (when, which)
    return out


def solution(mesh):
    return jax.shard_map(
        per_device,
        mesh=mesh,
        in_specs=(
            P(("groups", "seq"), ("head", "sub")),
            P(("groups", "seq"), None, ("head", "sub")),
            P(("head", "sub"), ("groups", "seq")),
            P(("head", "sub")),
            P(("head", "sub")),
            P(("head", "sub")),
            P(None, ("head", "sub")),
            P(("head", "sub")),
            P(None, None, ("head", "sub")),
            P(None, ("head", "sub")),
            P("groups"),
        ),
        out_specs=P(("groups", "seq"), ("head", "sub")),
        check_vma=False,
    )
```

```python
import functools
import math

import jax
import jax.numpy as jnp
from jax import lax
from jax.experimental import pallas as pl
from jax.experimental.pallas import tpu as pltpu
from jax.sharding import PartitionSpec as P

D = 128
Q = 128
BLK = 512
NQ = BLK // Q
HC = 4
CW = HC * D
PARTS = 2
PW = CW // PARTS
RIM = 8
LOG2E = math.log2(math.e)
F32 = jnp.float32
BF16 = jnp.bfloat16


def doc_of(pos, starts_ref):
    count = jnp.zeros_like(pos)
    for j in range(starts_ref.shape[0]):
        count = count + (pos >= starts_ref[j]).astype(jnp.int32)
    return count - 1


def silu_half(u):
    return u + u * jnp.tanh(u)


def doc_at(pos, starts_ref):
    count = jnp.int32(-1)
    for j in range(starts_ref.shape[0]):
        count = count + (pos >= starts_ref[j]).astype(jnp.int32)
    return count


def column_of(ref):
    heads = ref.shape[0]
    index = lax.broadcasted_iota(jnp.int32, (heads, 1), 0)
    column = jnp.zeros((heads, 1), F32)
    for h in range(heads):
        column = jnp.where(index == h, ref[h], column)
    return column


def split(value, parts):
    pieces = []
    for _ in range(parts - 1):
        piece = value.astype(BF16).astype(F32)
        pieces.append(piece)
        value = value - piece
    return pieces + [value]


def doc_at(pos, starts_ref):
    count = jnp.int32(-1)
    for j in range(starts_ref.shape[0]):
        count = count + (pos >= starts_ref[j]).astype(jnp.int32)
    return count


def column_of(ref):
    heads = ref.shape[0]
    index = lax.broadcasted_iota(jnp.int32, (heads, 1), 0)
    column = jnp.zeros((heads, 1), F32)
    for h in range(heads):
        column = jnp.where(index == h, ref[h], column)
    return column


def split(value, parts):
    pieces = []
    for _ in range(parts - 1):
        piece = value.astype(BF16).astype(F32)
        pieces.append(piece)
        value = value - piece
    return pieces + [value]


def doc_at(pos, starts_ref):
    count = jnp.int32(-1)
    for j in range(starts_ref.shape[0]):
        count = count + (pos >= starts_ref[j]).astype(jnp.int32)
    return count


def column_of(ref):
    heads = ref.shape[0]
    index = lax.broadcasted_iota(jnp.int32, (heads, 1), 0)
    column = jnp.zeros((heads, 1), F32)
    for h in range(heads):
        column = jnp.where(index == h, ref[h], column)
    return column


def split(value, parts):
    pieces = []
    for _ in range(parts - 1):
        piece = value.astype(BF16).astype(F32)
        pieces.append(piece)
        value = value - piece
    return pieces + [value]


def doc_at(pos, starts_ref):
    count = jnp.int32(-1)
    for j in range(starts_ref.shape[0]):
        count = count + (pos >= starts_ref[j]).astype(jnp.int32)
    return count


def column_of(ref):
    heads = ref.shape[0]
    index = lax.broadcasted_iota(jnp.int32, (heads, 1), 0)
    column = jnp.zeros((heads, 1), F32)
    for h in range(heads):
        column = jnp.where(index == h, ref[h], column)
    return column


def split(value, parts):
    pieces = []
    for _ in range(parts - 1):
        piece = value.astype(BF16).astype(F32)
        pieces.append(piece)
        value = value - piece
    return pieces + [value]


def doc_at(pos, starts_ref):
    count = jnp.int32(-1)
    for j in range(starts_ref.shape[0]):
        count = count + (pos >= starts_ref[j]).astype(jnp.int32)
    return count


def column_of(ref):
    heads = ref.shape[0]
    index = lax.broadcasted_iota(jnp.int32, (heads, 1), 0)
    column = jnp.zeros((heads, 1), F32)
    for h in range(heads):
        column = jnp.where(index == h, ref[h], column)
    return column


def split(value, parts):
    pieces = []
    for _ in range(parts - 1):
        piece = value.astype(BF16).astype(F32)
        pieces.append(piece)
        value = value - piece
    return pieces + [value]


def doc_at(pos, starts_ref):
    count = jnp.int32(-1)
    for j in range(starts_ref.shape[0]):
        count = count + (pos >= starts_ref[j]).astype(jnp.int32)
    return count


def column_of(ref):
    heads = ref.shape[0]
    index = lax.broadcasted_iota(jnp.int32, (heads, 1), 0)
    column = jnp.zeros((heads, 1), F32)
    for h in range(heads):
        column = jnp.where(index == h, ref[h], column)
    return column


def split(value, parts):
    pieces = []
    for _ in range(parts - 1):
        piece = value.astype(BF16).astype(F32)
        pieces.append(piece)
        value = value - piece
    return pieces + [value]


def doc_at(pos, starts_ref):
    count = jnp.int32(-1)
    for j in range(starts_ref.shape[0]):
        count = count + (pos >= starts_ref[j]).astype(jnp.int32)
    return count


def column_of(ref):
    heads = ref.shape[0]
    index = lax.broadcasted_iota(jnp.int32, (heads, 1), 0)
    column = jnp.zeros((heads, 1), F32)
    for h in range(heads):
        column = jnp.where(index == h, ref[h], column)
    return column


def split(value, parts):
    pieces = []
    for _ in range(parts - 1):
        piece = value.astype(BF16).astype(F32)
        pieces.append(piece)
        value = value - piece
    return pieces + [value]


def doc_at(pos, starts_ref):
    count = jnp.int32(-1)
    for j in range(starts_ref.shape[0]):
        count = count + (pos >= starts_ref[j]).astype(jnp.int32)
    return count


def column_of(ref):
    heads = ref.shape[0]
    index = lax.broadcasted_iota(jnp.int32, (heads, 1), 0)
    column = jnp.zeros((heads, 1), F32)
    for h in range(heads):
        column = jnp.where(index == h, ref[h], column)
    return column


def split(value, parts):
    pieces = []
    for _ in range(parts - 1):
        piece = value.astype(BF16).astype(F32)
        pieces.append(piece)
        value = value - piece
    return pieces + [value]


def doc_at(pos, starts_ref):
    count = jnp.int32(-1)
    for j in range(starts_ref.shape[0]):
        count = count + (pos >= starts_ref[j]).astype(jnp.int32)
    return count


def column_of(ref):
    heads = ref.shape[0]
    index = lax.broadcasted_iota(jnp.int32, (heads, 1), 0)
    column = jnp.zeros((heads, 1), F32)
    for h in range(heads):
        column = jnp.where(index == h, ref[h], column)
    return column


def split(value, parts):
    pieces = []
    for _ in range(parts - 1):
        piece = value.astype(BF16).astype(F32)
        pieces.append(piece)
        value = value - piece
    return pieces + [value]


def doc_at(pos, starts_ref):
    count = jnp.int32(-1)
    for j in range(starts_ref.shape[0]):
        count = count + (pos >= starts_ref[j]).astype(jnp.int32)
    return count


def column_of(ref):
    heads = ref.shape[0]
    index = lax.broadcasted_iota(jnp.int32, (heads, 1), 0)
    column = jnp.zeros((heads, 1), F32)
    for h in range(heads):
        column = jnp.where(index == h, ref[h], column)
    return column


def split(value, parts):
    pieces = []
    for _ in range(parts - 1):
        piece = value.astype(BF16).astype(F32)
        pieces.append(piece)
        value = value - piece
    return pieces + [value]


def doc_at(pos, starts_ref):
    count = jnp.int32(-1)
    for j in range(starts_ref.shape[0]):
        count = count + (pos >= starts_ref[j]).astype(jnp.int32)
    return count


def column_of(ref):
    heads = ref.shape[0]
    index = lax.broadcasted_iota(jnp.int32, (heads, 1), 0)
    column = jnp.zeros((heads, 1), F32)
    for h in range(heads):
        column = jnp.where(index == h, ref[h], column)
    return column


def split(value, parts):
    pieces = []
    for _ in range(parts - 1):
        piece = value.astype(BF16).astype(F32)
        pieces.append(piece)
        value = value - piece
    return pieces + [value]


def doc_at(pos, starts_ref):
    count = jnp.int32(-1)
    for j in range(starts_ref.shape[0]):
        count = count + (pos >= starts_ref[j]).astype(jnp.int32)
    return count


def column_of(ref):
    heads = ref.shape[0]
    index = lax.broadcasted_iota(jnp.int32, (heads, 1), 0)
    column = jnp.zeros((heads, 1), F32)
    for h in range(heads):
        column = jnp.where(index == h, ref[h], column)
    return column


def split(value, parts):
    pieces = []
    for _ in range(parts - 1):
        piece = value.astype(BF16).astype(F32)
        pieces.append(piece)
        value = value - piece
    return pieces + [value]


def doc_at(pos, starts_ref):
    count = jnp.int32(-1)
    for j in range(starts_ref.shape[0]):
        count = count + (pos >= starts_ref[j]).astype(jnp.int32)
    return count


def column_of(ref):
    heads = ref.shape[0]
    index = lax.broadcasted_iota(jnp.int32, (heads, 1), 0)
    column = jnp.zeros((heads, 1), F32)
    for h in range(heads):
        column = jnp.where(index == h, ref[h], column)
    return column


def split(value, parts):
    pieces = []
    for _ in range(parts - 1):
        piece = value.astype(BF16).astype(F32)
        pieces.append(piece)
        value = value - piece
    return pieces + [value]


def doc_at(pos, starts_ref):
    count = jnp.int32(-1)
    for j in range(starts_ref.shape[0]):
        count = count + (pos >= starts_ref[j]).astype(jnp.int32)
    return count


def column_of(ref):
    heads = ref.shape[0]
    index = lax.broadcasted_iota(jnp.int32, (heads, 1), 0)
    column = jnp.zeros((heads, 1), F32)
    for h in range(heads):
        column = jnp.where(index == h, ref[h], column)
    return column


def split(value, parts):
    pieces = []
    for _ in range(parts - 1):
        piece = value.astype(BF16).astype(F32)
        pieces.append(piece)
        value = value - piece
    return pieces + [value]


def doc_at(pos, starts_ref):
    count = jnp.int32(-1)
    for j in range(starts_ref.shape[0]):
        count = count + (pos >= starts_ref[j]).astype(jnp.int32)
    return count


def column_of(ref):
    heads = ref.shape[0]
    index = lax.broadcasted_iota(jnp.int32, (heads, 1), 0)
    column = jnp.zeros((heads, 1), F32)
    for h in range(heads):
        column = jnp.where(index == h, ref[h], column)
    return column


def split(value, parts):
    pieces = []
    for _ in range(parts - 1):
        piece = value.astype(BF16).astype(F32)
        pieces.append(piece)
        value = value - piece
    return pieces + [value]


def doc_at(pos, starts_ref):
    count = jnp.int32(-1)
    for j in range(starts_ref.shape[0]):
        count = count + (pos >= starts_ref[j]).astype(jnp.int32)
    return count


def column_of(ref):
    heads = ref.shape[0]
    index = lax.broadcasted_iota(jnp.int32, (heads, 1), 0)
    column = jnp.zeros((heads, 1), F32)
    for h in range(heads):
        column = jnp.where(index == h, ref[h], column)
    return column


def split(value, parts):
    pieces = []
    for _ in range(parts - 1):
        piece = value.astype(BF16).astype(F32)
        pieces.append(piece)
        value = value - piece
    return pieces + [value]


def params_kernel(
    starts_ref, bias_ref, alog_ref, skip_ref, dt_ref, far_x_ref,
    scale_ref, cols_ref, rows_ref, fade_ref, shift_ref, keep_ref, x_ref, sem,
):
    copies = []
    width = x_ref.shape[1]
    for part in range(4):
        lanes = pl.ds(part * (width // 4), width // 4)
        copies.append(pltpu.make_async_copy(far_x_ref.at[:, lanes], x_ref.at[:, lanes], sem.at[part]))
        copies[-1].start()
    first = lax.axis_index("seq") * BLK
    heads = dt_ref.shape[0]
    v = dt_ref[...] + column_of(bias_ref)
    step = jnp.maximum(v, 0.0) + jnp.log(1.0 + jnp.exp(-jnp.abs(v)))
    rate = -jnp.exp(column_of(alog_ref)) * step
    tri = (
        lax.broadcasted_iota(jnp.int32, (Q, Q), 0) <= lax.broadcasted_iota(jnp.int32, (Q, Q), 1)
    ).astype(F32)
    doc_before = doc_at(first - 1, starts_ref)
    doc_last = doc_at(first + BLK - 1, starts_ref)
    cums = []
    base = jnp.zeros((heads, 1), F32)
    for q in range(NQ):
        part = jnp.dot(
            rate[:, q * Q : (q + 1) * Q], tri, precision=lax.Precision.HIGHEST, preferred_element_type=F32
        )
        cums.append(part + base)
        base = base + part[:, Q - 1 : Q]
    for q in range(NQ):
        span = slice(q * Q, (q + 1) * Q)
        cum = cums[q]
        step_q = step[:, span]
        pos = first + q * Q + lax.broadcasted_iota(jnp.int32, (1, Q), 1)
        doc = doc_of(pos, starts_ref)
        tail = jnp.where(doc == doc_last, jnp.exp(base - cum) * step_q, 0.0)
        entry = jnp.where(doc == doc_before, jnp.exp(cum), 0.0)
        rest = jnp.zeros((D - 2 * heads, Q), F32)
        packed = split(tail, 2) + [rest]
        scale_ref[span, :] = jnp.transpose(jnp.concatenate(packed, axis=0), (1, 0)).astype(BF16)
        packed = [cum * LOG2E, entry, rest]
        cols_ref[span, :] = jnp.transpose(jnp.concatenate(packed, axis=0), (1, 0))
        terms = (cum - jnp.log(step_q)) * LOG2E
        for c in range(heads // HC):
            rows_ref[c, :, span] = terms[c * HC : (c + 1) * HC]
    decay = jnp.exp(base) * jnp.where(doc_last == doc_before, 1.0, 0.0)
    skip = column_of(skip_ref)
    for c in range(heads // HC):
        for i in range(HC):
            h = c * HC + i
            lanes = slice(i * D, (i + 1) * D)
            fade_ref[c, 0:1, lanes] = jnp.broadcast_to(skip[h : h + 1], (1, D))
            fade_ref[c, 1:2, lanes] = jnp.broadcast_to(decay[h : h + 1], (1, D))
    for q in range(NQ):
        row = lax.broadcasted_iota(jnp.int32, (Q, 2 * Q), 0)
        col = lax.broadcasted_iota(jnp.int32, (Q, 2 * Q), 1) - Q
        at = first + q * Q
        same = doc_of(at + row, starts_ref) == doc_of(at + col, starts_ref)
        for k in range(3):
            hit = same & (col == row - (3 - k))
            shift_ref[q, k * Q : (k + 1) * Q, :] = jnp.where(hit, 1.0, 0.0).astype(BF16)
        doc_row = doc_of(at + lax.broadcasted_iota(jnp.int32, (Q, BLK), 0), starts_ref)
        col = lax.broadcasted_iota(jnp.int32, (Q, BLK), 1)
        row = q * Q + lax.broadcasted_iota(jnp.int32, (Q, BLK), 0)
        keep = (row >= col) & (doc_row == doc_of(first + col, starts_ref))
        keep_ref[q * Q : (q + 1) * Q, :] = jnp.where(keep, 1.0, 0.0)
    for copy in copies:
        copy.wait()


def chooser(heads, chunk, lo, hi, width):
    k = lax.broadcasted_iota(jnp.int32, (D, width), 0)
    head = HC * chunk + lax.broadcasted_iota(jnp.int32, (D, width), 1) // D
    hit = ((k & (heads - 1)) == head) & (k >= lo * heads) & (k < hi * heads)
    return jnp.where(hit, 1.0, 0.0).astype(BF16)


def convolved(q, window, now, shift_ref, taps, bias):
    moved = jnp.dot(shift_ref[q], window, preferred_element_type=F32)
    total = (0.5 * taps[3]) * now.astype(F32) + 0.5 * bias
    for k in range(3):
        total = total + (0.5 * taps[k]) * moved[k * Q : (k + 1) * Q]
    return silu_half(total)


def window_of(q, edge_ref, x_ref):
    return edge_ref[...] if q == 0 else x_ref[(q - 1) * Q : (q + 1) * Q, :]


def edge(edge_ref, rim, x):
    width = x.shape[1]
    if rim is None:
        rim = jnp.zeros((Q, width), F32)
    else:
        rim = jnp.concatenate([jnp.zeros((Q - RIM, width), F32), rim.astype(F32)], axis=0)
    edge_ref[0:Q, 0:width] = rim.astype(BF16)
    edge_ref[Q : 2 * Q, 0:width] = x


def state_of(
    chunk, heads, x_ref, rim, wx_ref, bx_ref, shift_ref, scale_ref, bt, edge_ref, tail_ref, mx_ref=None
):
    wide = slice(chunk * CW, (chunk + 1) * CW)
    edge(edge_ref, rim, x_ref[0:Q, :])
    pick = chooser(heads, chunk, 0, 2, CW)
    taps = [wx_ref[k : k + 1, wide] for k in range(4)]
    for q in range(NQ):
        span = slice(q * Q, (q + 1) * Q)
        window = x_ref[(q - 1) * Q : (q + 1) * Q, :] if q else edge_ref[:, 0:CW]
        mixed = convolved(q, window, x_ref[span, :], shift_ref, taps, bx_ref[:, wide])
        if mx_ref is not None:
            mx_ref[chunk, span, :] = mixed.astype(BF16)
        scale = jnp.dot(scale_ref[span, :], pick, preferred_element_type=F32)
        tail_ref[span, :] = (mixed * scale).astype(BF16)
    return jnp.dot(bt, tail_ref[...], preferred_element_type=F32)


def chunk_of(x_ref, chunk):
    return x_ref.at[:, pl.ds(chunk * CW, CW)]


def mixed_of(q, part, edge_ref, bc_ref, shift_ref, wbc_ref, bbc_ref, wide):
    half = slice(part * wide, (part + 1) * wide)
    window = bc_ref[(q - 1) * Q : (q + 1) * Q, half] if q else edge_ref[:, 0:wide]
    taps = [wbc_ref[k, part : part + 1, :] for k in range(4)]
    return convolved(q, window, bc_ref[q * Q : (q + 1) * Q, half], shift_ref, taps, bbc_ref[part : part + 1, :])


def first_kernel(
    x_ref, rim_ref, wx_ref, bx_ref, shift_ref, scale_ref, bc_ref, wbc_ref, bbc_ref,
    mx_ref, end_ref, send_ref, bt_ref, edge_ref, tail_ref, *, heads,
):
    groups = bt_ref.shape[0]
    wide = groups * D
    start = x_ref.shape[1]
    edge(edge_ref, rim_ref[:, start : start + wide], bc_ref[0:Q, 0:wide])
    for q in range(NQ):
        mixed = mixed_of(q, 0, edge_ref, bc_ref, shift_ref, wbc_ref, bbc_ref, wide)
        for g in range(groups):
            bt_ref[g, :, q * Q : (q + 1) * Q] = jnp.transpose(mixed[:, g * D : (g + 1) * D], (1, 0)).astype(BF16)
    state = state_of(
        0, heads, chunk_of(x_ref, 0), rim_ref[:, 0:CW], wx_ref, bx_ref, shift_ref, scale_ref, bt_ref[0],
        edge_ref, tail_ref, mx_ref,
    )
    end_ref[0] = state
    send_ref[...] = state.astype(BF16)


def score_kernel(
    rim_ref, shift_ref, keep_ref, bc_ref, wbc_ref, bbc_ref, bt_ref, after_ref, c_ref, score_ref, edge_ref
):
    groups = bt_ref.shape[0]
    wide = groups * D
    start = rim_ref.shape[1] - wide
    edge(edge_ref, rim_ref[:, start:], bc_ref[0:Q, wide:])
    for q in range(NQ):
        span = slice(q * Q, (q + 1) * Q)
        upto = (q + 1) * Q
        mixed = mixed_of(q, 1, edge_ref, bc_ref, shift_ref, wbc_ref, bbc_ref, wide)
        for g in range(groups):
            c = mixed[:, g * D : (g + 1) * D].astype(BF16)
            c_ref[g, span, :] = c
            score = jnp.dot(c, bt_ref[g, :, 0:upto], preferred_element_type=F32)
            score_ref[g, span, 0:upto] = keep_ref[span, 0:upto] * score


def more_kernel(
    x_ref, rim_ref, wx_ref, bx_ref, shift_ref, scale_ref, bt_ref, old1, old2,
    mx_ref, end_ref, *rest, heads, per_group, some,
):
    edge_ref, tail_ref = rest[-2:]
    for chunk in some:
        wide = slice(chunk * CW, (chunk + 1) * CW)
        state = state_of(
            chunk, heads, chunk_of(x_ref, chunk), rim_ref[:, wide], wx_ref, bx_ref, shift_ref, scale_ref,
            bt_ref[chunk // per_group], edge_ref, tail_ref, mx_ref,
        )
        end_ref[chunk] = state
        for send_ref in rest[:-2]:
            send_ref[...] = state.astype(BF16)


def join_kernel(fade_ref, recv_ref, end_ref, token_ref, send_ref, *, turn, stream, per_stream):
    chunk = stream * per_stream + jnp.clip(turn - lax.axis_index("seq"), 0, per_stream - 1)
    send_ref[...] = (fade_ref[chunk, 1:2, :] * recv_ref[...].astype(F32) + end_ref[chunk]).astype(BF16)


def out_kernel(
    fade_ref, mx_ref, c_ref, score_ref, cols_ref, rows_ref, recv_ref,
    *rest, turn, stream, before, final, per_stream, per_group, heads,
):
    out_ref, block_ref, sem = rest[-3:]
    place = lax.axis_index("seq")

    def spot(when, which):
        chunk = which * per_stream + jnp.clip(when - place, 0, per_stream - 1)
        return pl.ds(pl.multiple_of(chunk * CW, CW), CW)

    def is_valid(when):
        return (when - place >= 0) & (when - place < per_stream)

    def half_copy(ref, when, which, half):
        rows = pl.ds(half * 2 * Q, 2 * Q)
        return pltpu.make_async_copy(ref.at[rows, :], out_ref.at[rows, spot(when, which)], sem.at[half])

    if before:
        @pl.when(is_valid(before[0]))
        def send():
            for half in range(2):
                half_copy(rest[0], *before, half).start()

    @pl.when(is_valid(turn))
    def compute():
        chunk = stream * per_stream + turn - place
        g = lax.div(chunk, per_group)
        cols = pltpu.roll(cols_ref[...], lax.rem(D - HC * chunk, D), 1)
        far = jnp.dot(c_ref[g], recv_ref[...], preferred_element_type=F32)
        zero = jnp.zeros((Q, Q), BF16)
        last = []
        for i in range(HC):
            lanes = slice(i * D, (i + 1) * D)
            cum = jnp.broadcast_to(cols[:, i : i + 1], (BLK, Q))
            entry = jnp.broadcast_to(cols[:, heads + i : heads + i + 1], (BLK, Q))
            tiles = []
            for q in range(NQ):
                span = slice(q * Q, (q + 1) * Q)
                line = []
                for j in range(q + 1):
                    there = slice(j * Q, (j + 1) * Q)
                    gap = cum[span] - rows_ref[chunk, i : i + 1, there]
                    if j == q:
                        gap = jnp.minimum(gap, 100.0)
                    line.append((score_ref[g, span, there] * jnp.exp2(gap)).astype(BF16))
                tiles.append(line + [zero] * (NQ - 1 - q))

            def weights(lines, halves):
                return jnp.concatenate([jnp.concatenate([tiles[q][j] for j in halves], axis=1) for q in lines], axis=0)

            left = jnp.dot(weights(range(NQ), (0, 1)), mx_ref[chunk, 0 : 2 * Q, lanes], preferred_element_type=F32)
            right = jnp.dot(weights((2, 3), (2, 3)), mx_ref[chunk, 2 * Q :, lanes], preferred_element_type=F32)
            for half in range(2):
                span = slice(half * 2 * Q, (half + 1) * 2 * Q)
                y = left[span] + right if half else left[span]
                x = mx_ref[chunk, span, lanes].astype(F32)
                y = y + entry[span] * far[span, lanes] + fade_ref[chunk, 0:1, lanes] * x
                block_ref[span, lanes] = y.astype(BF16)
            if final:
                there = pl.ds(pl.multiple_of(chunk * CW + i * D, D), D)
                last.append(
                    pltpu.make_async_copy(block_ref.at[:, pl.ds(i * D, D)], out_ref.at[:, there], sem.at[2 + i])
                )
                last[-1].start()
        for copy in last:
            copy.wait()

    if before:
        @pl.when(is_valid(before[0]))
        def wait():
            for half in range(2):
                half_copy(rest[0], *before, half).wait()


SMEM = pl.BlockSpec(memory_space=pltpu.SMEM)
ROOM = pltpu.CompilerParams(vmem_limit_bytes=16 * 2**20)
ANY = pl.BlockSpec(memory_space=pl.ANY)
VMEM = pl.BlockSpec(memory_space=pltpu.VMEM)


def whole(shape):
    return pl.BlockSpec(shape, lambda *_: (0,) * len(shape))


def shape_of(shape, dtype):
    return jax.ShapeDtypeStruct(shape, dtype)


def per_device(
    x_raw, bc_raw, dt_raw, dt_bias, a_log, d_skip, conv_x, conv_x_bias, conv_bc, conv_bc_bias, doc_starts
):
    rows, width = x_raw.shape
    held = [x_raw, dt_raw, dt_bias, a_log, d_skip, conv_bc, conv_bc_bias, doc_starts]
    held = [pltpu.with_memory_space_constraint(a, pltpu.HBM) for a in held]
    x_far, dt_raw, dt_bias, a_log, d_skip, conv_bc, conv_bc_bias, doc_starts = held
    bias_x = conv_x_bias[None]
    groups = bc_raw.shape[2] // D
    heads = dt_raw.shape[0]
    chunks = heads // HC
    per_group = chunks // groups
    seq = lax.axis_size("seq")
    ring = [(i, (i + 1) % seq) for i in range(seq)]
    cores = lax.axis_size("sub")

    def hop(slot, send):
        low, high = max(0, slot - per_stream + 1), min(slot, seq - 2)
        pairs = []
        for place in range(seq):
            for core in range(cores):
                if low <= place <= high + 1:
                    to = (place + 1 if place <= high else low) * cores + core
                else:
                    to = place * cores + (core + 1) % cores
                pairs.append((place * cores + core, to))
        return lax.ppermute(send, ("seq", "sub"), pairs)

    streams = 2
    per_stream = chunks // streams
    slots = per_stream + seq - 2

    tail = jnp.concatenate([x_raw[rows - RIM :], bc_raw[rows - RIM :].reshape(RIM, -1)], axis=1)
    rim = lax.ppermute(tail, "seq", ring)
    bc = bc_raw.reshape(rows, -1)

    scale, cols, row_terms, fade, shift, keep, x_near = pl.pallas_call(
        params_kernel,
        in_specs=[SMEM] * 4 + [VMEM, ANY],
        out_specs=[VMEM] * 7,
        out_shape=[
            shape_of((BLK, D), BF16),
            shape_of((BLK, D), F32),
            shape_of((chunks, HC, BLK), F32),
            shape_of((chunks, 2, CW), F32),
            shape_of((NQ, 3 * Q, 2 * Q), BF16),
            shape_of((BLK, BLK), F32),
            pltpu.VMEM((rows, width), BF16),
        ],
        scratch_shapes=[pltpu.SemaphoreType.DMA((4,))],
        compiler_params=ROOM,
        name="params",
    )(doc_starts, dt_bias, a_log, d_skip, dt_raw, x_far)

    big = [pltpu.VMEM((chunks, BLK, CW), BF16), pltpu.VMEM((chunks, D, CW), F32)]
    chunk_shape = shape_of((D, CW), BF16)
    bt_shape = shape_of((groups, D, BLK), BF16)
    scratch = [pltpu.VMEM((2 * Q, max(CW, 2 * groups * D)), BF16), pltpu.VMEM((BLK, CW), BF16)]

    mixed_x, end, send, bt = pl.pallas_call(
        functools.partial(first_kernel, heads=heads),
        in_specs=[VMEM] * 9,
        out_specs=[VMEM] * 4,
        out_shape=[*big, chunk_shape, bt_shape],
        scratch_shapes=scratch,
        compiler_params=ROOM,
        name="first",
    )(x_near, rim, conv_x, bias_x, shift, scale, bc, conv_bc, conv_bc_bias)

    def near(array):
        return pltpu.with_memory_space_constraint(array, pltpu.VMEM)

    def more(some, sends, mixed_x, end):
        return pl.pallas_call(
            functools.partial(more_kernel, heads=heads, per_group=per_group, some=some),
            in_specs=[VMEM] * 9,
            out_specs=[VMEM] * (2 + sends),
            out_shape=big + [chunk_shape] * sends,
            input_output_aliases={7: 0, 8: 1},
            scratch_shapes=scratch,
            compiler_params=ROOM,
            cost_estimate=pl.CostEstimate(
                flops=4 * len(some) * BLK * D * CW, bytes_accessed=4 * len(some) * BLK * CW, transcendentals=0
            ),
            name="more",
        )(x_near, rim, conv_x, bias_x, shift, scale, bt, near(mixed_x), near(end))

    begun = [send]
    flying = [hop(0, send)]
    for s in range(1, streams):
        mixed_x, end, send = more([s * per_stream], 1, mixed_x, end)
        begun.append(send)
        flying.append(hop(0, send))

    def scores(after):
        return pl.pallas_call(
            score_kernel,
            in_specs=[VMEM] * 7 + [ANY],
            out_specs=[VMEM] * 2,
            out_shape=[shape_of((groups, BLK, D), BF16), shape_of((groups, BLK, BLK), F32)],
            scratch_shapes=scratch[:1],
            compiler_params=ROOM,
            name="score",
        )(rim, shift, keep, bc, conv_bc, conv_bc_bias, bt, after)

    def join(turn, s, recv, token):
        return pl.pallas_call(
            functools.partial(join_kernel, turn=turn, stream=s, per_stream=per_stream),
            in_specs=[VMEM, VMEM, VMEM, ANY],
            out_specs=VMEM,
            out_shape=chunk_shape,
            compiler_params=ROOM,
            name="join",
        )(fade, recv, end, token)

    def output(turn, s, recv, before, block, out, mixed_c, score):
        old = [] if out is None else [block, out]
        return pl.pallas_call(
            functools.partial(
                out_kernel, turn=turn, stream=s, before=before, final=turn == slots and s == streams - 1,
                per_stream=per_stream, per_group=per_group, heads=heads,
            ),
            in_specs=[VMEM] * 7 + [VMEM, ANY][: len(old)],
            out_specs=[ANY, VMEM],
            out_shape=[pltpu.HBM((BLK, width), BF16), shape_of((BLK, CW), BF16)],
            input_output_aliases={8: 0} if old else {},
            scratch_shapes=[pltpu.SemaphoreType.DMA((2 + HC,))],
            compiler_params=ROOM,
            cost_estimate=pl.CostEstimate(
                flops=8 * BLK * Q * CW, bytes_accessed=6 * BLK * CW, transcendentals=0
            ),
            name="out",
        )(fade, mixed_x, mixed_c, score, cols, row_terms, recv, *old)

    out, block, before = None, None, None
    waiting = [(0, s, begun[s]) for s in range(streams)]
    token = bt
    for turn in range(1, slots + 1):
        if turn < per_stream:
            mixed_x, end = more([turn + i * per_stream for i in range(streams)], 0, mixed_x, end)
        for s in range(streams):
            recv = flying[s]
            if turn < slots:
                send = join(turn, s, recv, token)
                flying[s] = hop(turn, send)
            if turn == 1 and s == 0:
                mixed_c, score = scores(send)
            todo = [(turn, s, recv)]
            if waiting and turn >= min(per_stream, slots):
                todo.insert(0, waiting.pop(0))
            for when, which, got in todo:
                out, token = output(when, which, got, before, token, out, mixed_c, score)
                before = (when, which)
    return out


def solution(mesh):
    return jax.shard_map(
        per_device,
        mesh=mesh,
        in_specs=(
            P(("groups", "seq"), ("head", "sub")),
            P(("groups", "seq"), None, ("head", "sub")),
            P(("head", "sub"), ("groups", "seq")),
            P(("head", "sub")),
            P(("head", "sub")),
            P(("head", "sub")),
            P(None, ("head", "sub")),
            P(("head", "sub")),
            P(None, None, ("head", "sub")),
            P(None, ("head", "sub")),
            P("groups"),
        ),
        out_specs=P(("groups", "seq"), ("head", "sub")),
        check_vma=False,
    )
```

```python
import functools
import math

import jax
import jax.numpy as jnp
from jax import lax
from jax.experimental import pallas as pl
from jax.experimental.pallas import tpu as pltpu
from jax.sharding import PartitionSpec as P

D = 128
Q = 128
BLK = 512
NQ = BLK // Q
HC = 4
CW = HC * D
PARTS = 2
PW = CW // PARTS
RIM = 8
LOG2E = math.log2(math.e)
F32 = jnp.float32
BF16 = jnp.bfloat16


def doc_of(pos, starts_ref):
    count = jnp.zeros_like(pos)
    for j in range(starts_ref.shape[0]):
        count = count + (pos >= starts_ref[j]).astype(jnp.int32)
    return count - 1


def silu_half(u):
    return u + u * jnp.tanh(u)


def doc_at(pos, starts_ref):
    count = jnp.int32(-1)
    for j in range(starts_ref.shape[0]):
        count = count + (pos >= starts_ref[j]).astype(jnp.int32)
    return count


def column_of(ref):
    heads = ref.shape[0]
    index = lax.broadcasted_iota(jnp.int32, (heads, 1), 0)
    column = jnp.zeros((heads, 1), F32)
    for h in range(heads):
        column = jnp.where(index == h, ref[h], column)
    return column


def split(value, parts):
    pieces = []
    for _ in range(parts - 1):
        piece = value.astype(BF16).astype(F32)
        pieces.append(piece)
        value = value - piece
    return pieces + [value]


def doc_at(pos, starts_ref):
    count = jnp.int32(-1)
    for j in range(starts_ref.shape[0]):
        count = count + (pos >= starts_ref[j]).astype(jnp.int32)
    return count


def column_of(ref):
    heads = ref.shape[0]
    index = lax.broadcasted_iota(jnp.int32, (heads, 1), 0)
    column = jnp.zeros((heads, 1), F32)
    for h in range(heads):
        column = jnp.where(index == h, ref[h], column)
    return column


def split(value, parts):
    pieces = []
    for _ in range(parts - 1):
        piece = value.astype(BF16).astype(F32)
        pieces.append(piece)
        value = value - piece
    return pieces + [value]


def doc_at(pos, starts_ref):
    count = jnp.int32(-1)
    for j in range(starts_ref.shape[0]):
        count = count + (pos >= starts_ref[j]).astype(jnp.int32)
    return count


def column_of(ref):
    heads = ref.shape[0]
    index = lax.broadcasted_iota(jnp.int32, (heads, 1), 0)
    column = jnp.zeros((heads, 1), F32)
    for h in range(heads):
        column = jnp.where(index == h, ref[h], column)
    return column


def split(value, parts):
    pieces = []
    for _ in range(parts - 1):
        piece = value.astype(BF16).astype(F32)
        pieces.append(piece)
        value = value - piece
    return pieces + [value]


def doc_at(pos, starts_ref):
    count = jnp.int32(-1)
    for j in range(starts_ref.shape[0]):
        count = count + (pos >= starts_ref[j]).astype(jnp.int32)
    return count


def column_of(ref):
    heads = ref.shape[0]
    index = lax.broadcasted_iota(jnp.int32, (heads, 1), 0)
    column = jnp.zeros((heads, 1), F32)
    for h in range(heads):
        column = jnp.where(index == h, ref[h], column)
    return column


def split(value, parts):
    pieces = []
    for _ in range(parts - 1):
        piece = value.astype(BF16).astype(F32)
        pieces.append(piece)
        value = value - piece
    return pieces + [value]


def doc_at(pos, starts_ref):
    count = jnp.int32(-1)
    for j in range(starts_ref.shape[0]):
        count = count + (pos >= starts_ref[j]).astype(jnp.int32)
    return count


def column_of(ref):
    heads = ref.shape[0]
    index = lax.broadcasted_iota(jnp.int32, (heads, 1), 0)
    column = jnp.zeros((heads, 1), F32)
    for h in range(heads):
        column = jnp.where(index == h, ref[h], column)
    return column


def split(value, parts):
    pieces = []
    for _ in range(parts - 1):
        piece = value.astype(BF16).astype(F32)
        pieces.append(piece)
        value = value - piece
    return pieces + [value]


def doc_at(pos, starts_ref):
    count = jnp.int32(-1)
    for j in range(starts_ref.shape[0]):
        count = count + (pos >= starts_ref[j]).astype(jnp.int32)
    return count


def column_of(ref):
    heads = ref.shape[0]
    index = lax.broadcasted_iota(jnp.int32, (heads, 1), 0)
    column = jnp.zeros((heads, 1), F32)
    for h in range(heads):
        column = jnp.where(index == h, ref[h], column)
    return column


def split(value, parts):
    pieces = []
    for _ in range(parts - 1):
        piece = value.astype(BF16).astype(F32)
        pieces.append(piece)
        value = value - piece
    return pieces + [value]


def doc_at(pos, starts_ref):
    count = jnp.int32(-1)
    for j in range(starts_ref.shape[0]):
        count = count + (pos >= starts_ref[j]).astype(jnp.int32)
    return count


def column_of(ref):
    heads = ref.shape[0]
    index = lax.broadcasted_iota(jnp.int32, (heads, 1), 0)
    column = jnp.zeros((heads, 1), F32)
    for h in range(heads):
        column = jnp.where(index == h, ref[h], column)
    return column


def split(value, parts):
    pieces = []
    for _ in range(parts - 1):
        piece = value.astype(BF16).astype(F32)
        pieces.append(piece)
        value = value - piece
    return pieces + [value]


def doc_at(pos, starts_ref):
    count = jnp.int32(-1)
    for j in range(starts_ref.shape[0]):
        count = count + (pos >= starts_ref[j]).astype(jnp.int32)
    return count


def column_of(ref):
    heads = ref.shape[0]
    index = lax.broadcasted_iota(jnp.int32, (heads, 1), 0)
    column = jnp.zeros((heads, 1), F32)
    for h in range(heads):
        column = jnp.where(index == h, ref[h], column)
    return column


def split(value, parts):
    pieces = []
    for _ in range(parts - 1):
        piece = value.astype(BF16).astype(F32)
        pieces.append(piece)
        value = value - piece
    return pieces + [value]


def doc_at(pos, starts_ref):
    count = jnp.int32(-1)
    for j in range(starts_ref.shape[0]):
        count = count + (pos >= starts_ref[j]).astype(jnp.int32)
    return count


def column_of(ref):
    heads = ref.shape[0]
    index = lax.broadcasted_iota(jnp.int32, (heads, 1), 0)
    column = jnp.zeros((heads, 1), F32)
    for h in range(heads):
        column = jnp.where(index == h, ref[h], column)
    return column


def split(value, parts):
    pieces = []
    for _ in range(parts - 1):
        piece = value.astype(BF16).astype(F32)
        pieces.append(piece)
        value = value - piece
    return pieces + [value]


def doc_at(pos, starts_ref):
    count = jnp.int32(-1)
    for j in range(starts_ref.shape[0]):
        count = count + (pos >= starts_ref[j]).astype(jnp.int32)
    return count


def column_of(ref):
    heads = ref.shape[0]
    index = lax.broadcasted_iota(jnp.int32, (heads, 1), 0)
    column = jnp.zeros((heads, 1), F32)
    for h in range(heads):
        column = jnp.where(index == h, ref[h], column)
    return column


def split(value, parts):
    pieces = []
    for _ in range(parts - 1):
        piece = value.astype(BF16).astype(F32)
        pieces.append(piece)
        value = value - piece
    return pieces + [value]


def doc_at(pos, starts_ref):
    count = jnp.int32(-1)
    for j in range(starts_ref.shape[0]):
        count = count + (pos >= starts_ref[j]).astype(jnp.int32)
    return count


def column_of(ref):
    heads = ref.shape[0]
    index = lax.broadcasted_iota(jnp.int32, (heads, 1), 0)
    column = jnp.zeros((heads, 1), F32)
    for h in range(heads):
        column = jnp.where(index == h, ref[h], column)
    return column


def split(value, parts):
    pieces = []
    for _ in range(parts - 1):
        piece = value.astype(BF16).astype(F32)
        pieces.append(piece)
        value = value - piece
    return pieces + [value]


def doc_at(pos, starts_ref):
    count = jnp.int32(-1)
    for j in range(starts_ref.shape[0]):
        count = count + (pos >= starts_ref[j]).astype(jnp.int32)
    return count


def column_of(ref):
    heads = ref.shape[0]
    index = lax.broadcasted_iota(jnp.int32, (heads, 1), 0)
    column = jnp.zeros((heads, 1), F32)
    for h in range(heads):
        column = jnp.where(index == h, ref[h], column)
    return column


def split(value, parts):
    pieces = []
    for _ in range(parts - 1):
        piece = value.astype(BF16).astype(F32)
        pieces.append(piece)
        value = value - piece
    return pieces + [value]


def doc_at(pos, starts_ref):
    count = jnp.int32(-1)
    for j in range(starts_ref.shape[0]):
        count = count + (pos >= starts_ref[j]).astype(jnp.int32)
    return count


def column_of(ref):
    heads = ref.shape[0]
    index = lax.broadcasted_iota(jnp.int32, (heads, 1), 0)
    column = jnp.zeros((heads, 1), F32)
    for h in range(heads):
        column = jnp.where(index == h, ref[h], column)
    return column


def split(value, parts):
    pieces = []
    for _ in range(parts - 1):
        piece = value.astype(BF16).astype(F32)
        pieces.append(piece)
        value = value - piece
    return pieces + [value]


def doc_at(pos, starts_ref):
    count = jnp.int32(-1)
    for j in range(starts_ref.shape[0]):
        count = count + (pos >= starts_ref[j]).astype(jnp.int32)
    return count


def column_of(ref):
    heads = ref.shape[0]
    index = lax.broadcasted_iota(jnp.int32, (heads, 1), 0)
    column = jnp.zeros((heads, 1), F32)
    for h in range(heads):
        column = jnp.where(index == h, ref[h], column)
    return column


def split(value, parts):
    pieces = []
    for _ in range(parts - 1):
        piece = value.astype(BF16).astype(F32)
        pieces.append(piece)
        value = value - piece
    return pieces + [value]


def doc_at(pos, starts_ref):
    count = jnp.int32(-1)
    for j in range(starts_ref.shape[0]):
        count = count + (pos >= starts_ref[j]).astype(jnp.int32)
    return count


def column_of(ref):
    heads = ref.shape[0]
    index = lax.broadcasted_iota(jnp.int32, (heads, 1), 0)
    column = jnp.zeros((heads, 1), F32)
    for h in range(heads):
        column = jnp.where(index == h, ref[h], column)
    return column


def split(value, parts):
    pieces = []
    for _ in range(parts - 1):
        piece = value.astype(BF16).astype(F32)
        pieces.append(piece)
        value = value - piece
    return pieces + [value]


def doc_at(pos, starts_ref):
    count = jnp.int32(-1)
    for j in range(starts_ref.shape[0]):
        count = count + (pos >= starts_ref[j]).astype(jnp.int32)
    return count


def column_of(ref):
    heads = ref.shape[0]
    index = lax.broadcasted_iota(jnp.int32, (heads, 1), 0)
    column = jnp.zeros((heads, 1), F32)
    for h in range(heads):
        column = jnp.where(index == h, ref[h], column)
    return column


def split(value, parts):
    pieces = []
    for _ in range(parts - 1):
        piece = value.astype(BF16).astype(F32)
        pieces.append(piece)
        value = value - piece
    return pieces + [value]


def doc_at(pos, starts_ref):
    count = jnp.int32(-1)
    for j in range(starts_ref.shape[0]):
        count = count + (pos >= starts_ref[j]).astype(jnp.int32)
    return count


def column_of(ref):
    heads = ref.shape[0]
    index = lax.broadcasted_iota(jnp.int32, (heads, 1), 0)
    column = jnp.zeros((heads, 1), F32)
    for h in range(heads):
        column = jnp.where(index == h, ref[h], column)
    return column


def split(value, parts):
    pieces = []
    for _ in range(parts - 1):
        piece = value.astype(BF16).astype(F32)
        pieces.append(piece)
        value = value - piece
    return pieces + [value]


def doc_at(pos, starts_ref):
    count = jnp.int32(-1)
    for j in range(starts_ref.shape[0]):
        count = count + (pos >= starts_ref[j]).astype(jnp.int32)
    return count


def column_of(ref):
    heads = ref.shape[0]
    index = lax.broadcasted_iota(jnp.int32, (heads, 1), 0)
    column = jnp.zeros((heads, 1), F32)
    for h in range(heads):
        column = jnp.where(index == h, ref[h], column)
    return column


def split(value, parts):
    pieces = []
    for _ in range(parts - 1):
        piece = value.astype(BF16).astype(F32)
        pieces.append(piece)
        value = value - piece
    return pieces + [value]


def doc_at(pos, starts_ref):
    count = jnp.int32(-1)
    for j in range(starts_ref.shape[0]):
        count = count + (pos >= starts_ref[j]).astype(jnp.int32)
    return count


def column_of(ref):
    heads = ref.shape[0]
    index = lax.broadcasted_iota(jnp.int32, (heads, 1), 0)
    column = jnp.zeros((heads, 1), F32)
    for h in range(heads):
        column = jnp.where(index == h, ref[h], column)
    return column


def split(value, parts):
    pieces = []
    for _ in range(parts - 1):
        piece = value.astype(BF16).astype(F32)
        pieces.append(piece)
        value = value - piece
    return pieces + [value]


def doc_at(pos, starts_ref):
    count = jnp.int32(-1)
    for j in range(starts_ref.shape[0]):
        count = count + (pos >= starts_ref[j]).astype(jnp.int32)
    return count


def column_of(ref):
    heads = ref.shape[0]
    index = lax.broadcasted_iota(jnp.int32, (heads, 1), 0)
    column = jnp.zeros((heads, 1), F32)
    for h in range(heads):
        column = jnp.where(index == h, ref[h], column)
    return column


def split(value, parts):
    pieces = []
    for _ in range(parts - 1):
        piece = value.astype(BF16).astype(F32)
        pieces.append(piece)
        value = value - piece
    return pieces + [value]


def doc_at(pos, starts_ref):
    count = jnp.int32(-1)
    for j in range(starts_ref.shape[0]):
        count = count + (pos >= starts_ref[j]).astype(jnp.int32)
    return count


def column_of(ref):
    heads = ref.shape[0]
    index = lax.broadcasted_iota(jnp.int32, (heads, 1), 0)
    column = jnp.zeros((heads, 1), F32)
    for h in range(heads):
        column = jnp.where(index == h, ref[h], column)
    return column


def split(value, parts):
    pieces = []
    for _ in range(parts - 1):
        piece = value.astype(BF16).astype(F32)
        pieces.append(piece)
        value = value - piece
    return pieces + [value]


def params_kernel(
    starts_ref, bias_ref, alog_ref, skip_ref, dt_ref, far_x_ref,
    scale_ref, cols_ref, rows_ref, fade_ref, shift_ref, keep_ref, x_ref, sem,
):
    copies = []
    width = x_ref.shape[1]
    for part in range(4):
        lanes = pl.ds(part * (width // 4), width // 4)
        copies.append(pltpu.make_async_copy(far_x_ref.at[:, lanes], x_ref.at[:, lanes], sem.at[part]))
        copies[-1].start()
    first = lax.axis_index("seq") * BLK
    heads = dt_ref.shape[0]
    v = dt_ref[...] + column_of(bias_ref)
    step = jnp.maximum(v, 0.0) + jnp.log(1.0 + jnp.exp(-jnp.abs(v)))
    rate = -jnp.exp(column_of(alog_ref)) * step
    tri = (
        lax.broadcasted_iota(jnp.int32, (Q, Q), 0) <= lax.broadcasted_iota(jnp.int32, (Q, Q), 1)
    ).astype(F32)
    doc_before = doc_at(first - 1, starts_ref)
    doc_last = doc_at(first + BLK - 1, starts_ref)
    cums = []
    base = jnp.zeros((heads, 1), F32)
    for q in range(NQ):
        part = jnp.dot(
            rate[:, q * Q : (q + 1) * Q], tri, precision=lax.Precision.HIGHEST, preferred_element_type=F32
        )
        cums.append(part + base)
        base = base + part[:, Q - 1 : Q]
    for q in range(NQ):
        span = slice(q * Q, (q + 1) * Q)
        cum = cums[q]
        step_q = step[:, span]
        pos = first + q * Q + lax.broadcasted_iota(jnp.int32, (1, Q), 1)
        doc = doc_of(pos, starts_ref)
        tail = jnp.where(doc == doc_last, jnp.exp(base - cum) * step_q, 0.0)
        entry = jnp.where(doc == doc_before, jnp.exp(cum), 0.0)
        rest = jnp.zeros((D - 2 * heads, Q), F32)
        packed = split(tail, 2) + [rest]
        scale_ref[span, :] = jnp.transpose(jnp.concatenate(packed, axis=0), (1, 0)).astype(BF16)
        packed = [cum * LOG2E, entry, rest]
        cols_ref[span, :] = jnp.transpose(jnp.concatenate(packed, axis=0), (1, 0))
        terms = (cum - jnp.log(step_q)) * LOG2E
        for c in range(heads // HC):
            rows_ref[c, :, span] = terms[c * HC : (c + 1) * HC]
    decay = jnp.exp(base) * jnp.where(doc_last == doc_before, 1.0, 0.0)
    skip = column_of(skip_ref)
    for c in range(heads // HC):
        for i in range(HC):
            h = c * HC + i
            lanes = slice(i * D, (i + 1) * D)
            fade_ref[c, 0:1, lanes] = jnp.broadcast_to(skip[h : h + 1], (1, D))
            fade_ref[c, 1:2, lanes] = jnp.broadcast_to(decay[h : h + 1], (1, D))
    for q in range(NQ):
        row = lax.broadcasted_iota(jnp.int32, (Q, 2 * Q), 0)
        col = lax.broadcasted_iota(jnp.int32, (Q, 2 * Q), 1) - Q
        at = first + q * Q
        same = doc_of(at + row, starts_ref) == doc_of(at + col, starts_ref)
        for k in range(3):
            hit = same & (col == row - (3 - k))
            shift_ref[q, k * Q : (k + 1) * Q, :] = jnp.where(hit, 1.0, 0.0).astype(BF16)
        doc_row = doc_of(at + lax.broadcasted_iota(jnp.int32, (Q, BLK), 0), starts_ref)
        col = lax.broadcasted_iota(jnp.int32, (Q, BLK), 1)
        row = q * Q + lax.broadcasted_iota(jnp.int32, (Q, BLK), 0)
        keep = (row >= col) & (doc_row == doc_of(first + col, starts_ref))
        keep_ref[q * Q : (q + 1) * Q, :] = jnp.where(keep, 1.0, 0.0)
    for copy in copies:
        copy.wait()


def chooser(heads, chunk, lo, hi, width):
    k = lax.broadcasted_iota(jnp.int32, (D, width), 0)
    head = HC * chunk + lax.broadcasted_iota(jnp.int32, (D, width), 1) // D
    hit = ((k & (heads - 1)) == head) & (k >= lo * heads) & (k < hi * heads)
    return jnp.where(hit, 1.0, 0.0).astype(BF16)


def convolved(q, window, now, shift_ref, taps, bias):
    moved = jnp.dot(shift_ref[q], window, preferred_element_type=F32)
    total = (0.5 * taps[3]) * now.astype(F32) + 0.5 * bias
    for k in range(3):
        total = total + (0.5 * taps[k]) * moved[k * Q : (k + 1) * Q]
    return silu_half(total)


def window_of(q, edge_ref, x_ref):
    return edge_ref[...] if q == 0 else x_ref[(q - 1) * Q : (q + 1) * Q, :]


def edge(edge_ref, rim, x):
    width = x.shape[1]
    if rim is None:
        rim = jnp.zeros((Q, width), F32)
    else:
        rim = jnp.concatenate([jnp.zeros((Q - RIM, width), F32), rim.astype(F32)], axis=0)
    edge_ref[0:Q, 0:width] = rim.astype(BF16)
    edge_ref[Q : 2 * Q, 0:width] = x


def state_of(
    chunk, heads, x_ref, rim, wx_ref, bx_ref, shift_ref, scale_ref, bt, edge_ref, tail_ref, mx_ref=None
):
    wide = slice(chunk * CW, (chunk + 1) * CW)
    edge(edge_ref, rim, x_ref[0:Q, :])
    pick = chooser(heads, chunk, 0, 2, CW)
    taps = [wx_ref[k : k + 1, wide] for k in range(4)]
    for q in range(NQ):
        span = slice(q * Q, (q + 1) * Q)
        window = x_ref[(q - 1) * Q : (q + 1) * Q, :] if q else edge_ref[:, 0:CW]
        mixed = convolved(q, window, x_ref[span, :], shift_ref, taps, bx_ref[:, wide])
        if mx_ref is not None:
            mx_ref[chunk, span, :] = mixed.astype(BF16)
        scale = jnp.dot(scale_ref[span, :], pick, preferred_element_type=F32)
        tail_ref[span, :] = (mixed * scale).astype(BF16)
    return jnp.dot(bt, tail_ref[...], preferred_element_type=F32)


def chunk_of(x_ref, chunk):
    return x_ref.at[:, pl.ds(chunk * CW, CW)]


def mixed_of(q, part, edge_ref, bc_ref, shift_ref, wbc_ref, bbc_ref, wide):
    half = slice(part * wide, (part + 1) * wide)
    window = bc_ref[(q - 1) * Q : (q + 1) * Q, half] if q else edge_ref[:, 0:wide]
    taps = [wbc_ref[k, part : part + 1, :] for k in range(4)]
    return convolved(q, window, bc_ref[q * Q : (q + 1) * Q, half], shift_ref, taps, bbc_ref[part : part + 1, :])


def first_kernel(
    x_ref, rim_ref, wx_ref, bx_ref, shift_ref, scale_ref, bc_ref, wbc_ref, bbc_ref,
    mx_ref, end_ref, send_ref, bt_ref, edge_ref, tail_ref, *, heads,
):
    groups = bt_ref.shape[0]
    wide = groups * D
    start = x_ref.shape[1]
    edge(edge_ref, rim_ref[:, start : start + wide], bc_ref[0:Q, 0:wide])
    for q in range(NQ):
        mixed = mixed_of(q, 0, edge_ref, bc_ref, shift_ref, wbc_ref, bbc_ref, wide)
        for g in range(groups):
            bt_ref[g, :, q * Q : (q + 1) * Q] = jnp.transpose(mixed[:, g * D : (g + 1) * D], (1, 0)).astype(BF16)
    state = state_of(
        0, heads, chunk_of(x_ref, 0), rim_ref[:, 0:CW], wx_ref, bx_ref, shift_ref, scale_ref, bt_ref[0],
        edge_ref, tail_ref, mx_ref,
    )
    end_ref[0] = state
    send_ref[...] = state.astype(BF16)


def score_kernel(
    rim_ref, shift_ref, keep_ref, bc_ref, wbc_ref, bbc_ref, bt_ref, after_ref, c_ref, score_ref, edge_ref
):
    groups = bt_ref.shape[0]
    wide = groups * D
    start = rim_ref.shape[1] - wide
    edge(edge_ref, rim_ref[:, start:], bc_ref[0:Q, wide:])
    for q in range(NQ):
        span = slice(q * Q, (q + 1) * Q)
        upto = (q + 1) * Q
        mixed = mixed_of(q, 1, edge_ref, bc_ref, shift_ref, wbc_ref, bbc_ref, wide)
        for g in range(groups):
            c = mixed[:, g * D : (g + 1) * D].astype(BF16)
            c_ref[g, span, :] = c
            score = jnp.dot(c, bt_ref[g, :, 0:upto], preferred_element_type=F32)
            score_ref[g, span, 0:upto] = keep_ref[span, 0:upto] * score


def more_kernel(
    x_ref, rim_ref, wx_ref, bx_ref, shift_ref, scale_ref, bt_ref, old1, old2,
    mx_ref, end_ref, *rest, heads, per_group, some,
):
    edge_ref, tail_ref = rest[-2:]
    for chunk in some:
        wide = slice(chunk * CW, (chunk + 1) * CW)
        state = state_of(
            chunk, heads, chunk_of(x_ref, chunk), rim_ref[:, wide], wx_ref, bx_ref, shift_ref, scale_ref,
            bt_ref[chunk // per_group], edge_ref, tail_ref, mx_ref,
        )
        end_ref[chunk] = state
        for send_ref in rest[:-2]:
            send_ref[...] = state.astype(BF16)


def join_kernel(fade_ref, recv_ref, end_ref, token_ref, send_ref, *, turn, stream, per_stream):
    chunk = stream * per_stream + jnp.clip(turn - lax.axis_index("seq"), 0, per_stream - 1)
    send_ref[...] = (fade_ref[chunk, 1:2, :] * recv_ref[...].astype(F32) + end_ref[chunk]).astype(BF16)


def out_kernel(
    fade_ref, mx_ref, c_ref, score_ref, cols_ref, rows_ref, recv_ref,
    *rest, turn, stream, before, final, per_stream, per_group, heads,
):
    out_ref, block_ref, sem = rest[-3:]
    place = lax.axis_index("seq")

    def spot(when, which):
        chunk = which * per_stream + jnp.clip(when - place, 0, per_stream - 1)
        return pl.ds(pl.multiple_of(chunk * CW, CW), CW)

    def is_valid(when):
        return (when - place >= 0) & (when - place < per_stream)

    def half_copy(ref, when, which, half):
        rows = pl.ds(half * 2 * Q, 2 * Q)
        return pltpu.make_async_copy(ref.at[rows, :], out_ref.at[rows, spot(when, which)], sem.at[half])

    if before:
        @pl.when(is_valid(before[0]))
        def send():
            for half in range(2):
                half_copy(rest[0], *before, half).start()

    @pl.when(is_valid(turn))
    def compute():
        chunk = stream * per_stream + turn - place
        g = lax.div(chunk, per_group)
        cols = pltpu.roll(cols_ref[...], lax.rem(D - HC * chunk, D), 1)
        far = jnp.dot(c_ref[g], recv_ref[...], preferred_element_type=F32)
        zero = jnp.zeros((Q, Q), BF16)
        last = []
        for i in range(HC):
            lanes = slice(i * D, (i + 1) * D)
            cum = jnp.broadcast_to(cols[:, i : i + 1], (BLK, Q))
            entry = jnp.broadcast_to(cols[:, heads + i : heads + i + 1], (BLK, Q))
            tiles = []
            for q in range(NQ):
                span = slice(q * Q, (q + 1) * Q)
                line = []
                for j in range(q + 1):
                    there = slice(j * Q, (j + 1) * Q)
                    gap = cum[span] - rows_ref[chunk, i : i + 1, there]
                    if j == q:
                        gap = jnp.minimum(gap, 100.0)
                    line.append((score_ref[g, span, there] * jnp.exp2(gap)).astype(BF16))
                tiles.append(line + [zero] * (NQ - 1 - q))

            def weights(lines, halves):
                return jnp.concatenate([jnp.concatenate([tiles[q][j] for j in halves], axis=1) for q in lines], axis=0)

            left = jnp.dot(weights(range(NQ), (0, 1)), mx_ref[chunk, 0 : 2 * Q, lanes], preferred_element_type=F32)
            right = jnp.dot(weights((2, 3), (2, 3)), mx_ref[chunk, 2 * Q :, lanes], preferred_element_type=F32)
            for half in range(2):
                span = slice(half * 2 * Q, (half + 1) * 2 * Q)
                y = left[span] + right if half else left[span]
                x = mx_ref[chunk, span, lanes].astype(F32)
                y = y + entry[span] * far[span, lanes] + fade_ref[chunk, 0:1, lanes] * x
                block_ref[span, lanes] = y.astype(BF16)
            if final:
                there = pl.ds(pl.multiple_of(chunk * CW + i * D, D), D)
                last.append(
                    pltpu.make_async_copy(block_ref.at[:, pl.ds(i * D, D)], out_ref.at[:, there], sem.at[2 + i])
                )
                last[-1].start()
        for copy in last:
            copy.wait()

    if before:
        @pl.when(is_valid(before[0]))
        def wait():
            for half in range(2):
                half_copy(rest[0], *before, half).wait()


SMEM = pl.BlockSpec(memory_space=pltpu.SMEM)
ROOM = pltpu.CompilerParams(vmem_limit_bytes=16 * 2**20)
ANY = pl.BlockSpec(memory_space=pl.ANY)
VMEM = pl.BlockSpec(memory_space=pltpu.VMEM)


def whole(shape):
    return pl.BlockSpec(shape, lambda *_: (0,) * len(shape))


def shape_of(shape, dtype):
    return jax.ShapeDtypeStruct(shape, dtype)


def per_device(
    x_raw, bc_raw, dt_raw, dt_bias, a_log, d_skip, conv_x, conv_x_bias, conv_bc, conv_bc_bias, doc_starts
):
    rows, width = x_raw.shape
    held = [x_raw, dt_raw, dt_bias, a_log, d_skip, conv_bc, conv_bc_bias, doc_starts]
    held = [pltpu.with_memory_space_constraint(a, pltpu.HBM) for a in held]
    x_far, dt_raw, dt_bias, a_log, d_skip, conv_bc, conv_bc_bias, doc_starts = held
    bias_x = conv_x_bias[None]
    groups = bc_raw.shape[2] // D
    heads = dt_raw.shape[0]
    chunks = heads // HC
    per_group = chunks // groups
    seq = lax.axis_size("seq")
    ring = [(i, (i + 1) % seq) for i in range(seq)]
    cores = lax.axis_size("sub")

    def hop(slot, send):
        low, high = max(0, slot - per_stream + 1), min(slot, seq - 2)
        pairs = []
        for place in range(seq):
            for core in range(cores):
                if low <= place <= high + 1:
                    to = (place + 1 if place <= high else low) * cores + core
                else:
                    to = place * cores + (core + 1) % cores
                pairs.append((place * cores + core, to))
        return lax.ppermute(send, ("seq", "sub"), pairs)

    streams = 2
    per_stream = chunks // streams
    slots = per_stream + seq - 2

    tail = jnp.concatenate([x_raw[rows - RIM :], bc_raw[rows - RIM :].reshape(RIM, -1)], axis=1)
    rim = lax.ppermute(tail, "seq", ring)
    bc = bc_raw.reshape(rows, -1)

    scale, cols, row_terms, fade, shift, keep, x_near = pl.pallas_call(
        params_kernel,
        in_specs=[SMEM] * 4 + [VMEM, ANY],
        out_specs=[VMEM] * 7,
        out_shape=[
            shape_of((BLK, D), BF16),
            shape_of((BLK, D), F32),
            shape_of((chunks, HC, BLK), F32),
            shape_of((chunks, 2, CW), F32),
            shape_of((NQ, 3 * Q, 2 * Q), BF16),
            shape_of((BLK, BLK), F32),
            pltpu.VMEM((rows, width), BF16),
        ],
        scratch_shapes=[pltpu.SemaphoreType.DMA((4,))],
        compiler_params=ROOM,
        name="params",
    )(doc_starts, dt_bias, a_log, d_skip, dt_raw, x_far)

    big = [pltpu.VMEM((chunks, BLK, CW), BF16), pltpu.VMEM((chunks, D, CW), F32)]
    chunk_shape = shape_of((D, CW), BF16)
    bt_shape = shape_of((groups, D, BLK), BF16)
    scratch = [pltpu.VMEM((2 * Q, max(CW, 2 * groups * D)), BF16), pltpu.VMEM((BLK, CW), BF16)]

    mixed_x, end, send, bt = pl.pallas_call(
        functools.partial(first_kernel, heads=heads),
        in_specs=[VMEM] * 9,
        out_specs=[VMEM] * 4,
        out_shape=[*big, chunk_shape, bt_shape],
        scratch_shapes=scratch,
        compiler_params=ROOM,
        name="first",
    )(x_near, rim, conv_x, bias_x, shift, scale, bc, conv_bc, conv_bc_bias)

    def near(array):
        return pltpu.with_memory_space_constraint(array, pltpu.VMEM)

    def more(some, sends, mixed_x, end):
        return pl.pallas_call(
            functools.partial(more_kernel, heads=heads, per_group=per_group, some=some),
            in_specs=[VMEM] * 9,
            out_specs=[VMEM] * (2 + sends),
            out_shape=big + [chunk_shape] * sends,
            input_output_aliases={7: 0, 8: 1},
            scratch_shapes=scratch,
            compiler_params=ROOM,
            cost_estimate=pl.CostEstimate(
                flops=4 * len(some) * BLK * D * CW, bytes_accessed=4 * len(some) * BLK * CW, transcendentals=0
            ),
            name="more",
        )(x_near, rim, conv_x, bias_x, shift, scale, bt, near(mixed_x), near(end))

    begun = [send]
    flying = [hop(0, send)]
    for s in range(1, streams):
        mixed_x, end, send = more([s * per_stream], 1, mixed_x, end)
        begun.append(send)
        flying.append(hop(0, send))

    def scores(after):
        return pl.pallas_call(
            score_kernel,
            in_specs=[VMEM] * 7 + [ANY],
            out_specs=[VMEM] * 2,
            out_shape=[shape_of((groups, BLK, D), BF16), shape_of((groups, BLK, BLK), F32)],
            scratch_shapes=scratch[:1],
            compiler_params=ROOM,
            name="score",
        )(rim, shift, keep, bc, conv_bc, conv_bc_bias, bt, after)

    def join(turn, s, recv, token):
        return pl.pallas_call(
            functools.partial(join_kernel, turn=turn, stream=s, per_stream=per_stream),
            in_specs=[VMEM, VMEM, VMEM, ANY],
            out_specs=VMEM,
            out_shape=chunk_shape,
            compiler_params=ROOM,
            name="join",
        )(fade, recv, end, token)

    def output(turn, s, recv, before, block, out, mixed_c, score):
        old = [] if out is None else [last_block[-1], out, block]
        return pl.pallas_call(
            functools.partial(
                out_kernel, turn=turn, stream=s, before=before, final=turn == slots and s == streams - 1,
                per_stream=per_stream, per_group=per_group, heads=heads,
            ),
            in_specs=[VMEM] * 7 + [VMEM, ANY, ANY][: len(old)],
            out_specs=[ANY, VMEM],
            out_shape=[pltpu.HBM((BLK, width), BF16), shape_of((BLK, CW), BF16)],
            input_output_aliases={8: 0} if old else {},
            scratch_shapes=[pltpu.SemaphoreType.DMA((2 + HC,))],
            compiler_params=ROOM,
            cost_estimate=pl.CostEstimate(
                flops=8 * BLK * Q * CW, bytes_accessed=6 * BLK * CW, transcendentals=0
            ),
            name="out",
        )(fade, mixed_x, mixed_c, score, cols, row_terms, recv, *old)

    out, before = None, None
    last_block = []
    waiting = [(0, s, begun[s]) for s in range(streams)]
    token = bt
    ready = []

    def flush(ready, before, token, out):
        for when, which, got in ready:
            out, token = output(when, which, got, before, token, out, mixed_c, score)
            last_block.append(token)
            before = (when, which)
        return before, token, out

    for turn in range(1, slots + 1):
        for s in range(streams):
            if turn < per_stream:
                mixed_x, end = more([turn + s * per_stream], 0, mixed_x, end)
            got = flying[s]
            if turn < slots:
                send = join(turn, s, got, token)
                flying[s] = hop(turn, send)
                token = send
            elif s == 0:
                ready = waiting + ready
                waiting = []
            if turn == slots - 1 and turn > per_stream and s == 0:
                before, token, out = flush(ready, before, token, out)
                ready = []
            ready.append((turn, s, got))
            if (turn > per_stream and turn != slots - 1) or turn == slots:
                before, token, out = flush(ready, before, token, out)
                ready = []
        if turn == 1:
            mixed_c, score = scores(send)
            token = score
        if turn == per_stream - 1:
            ready, waiting = waiting + ready, []
        if (turn <= per_stream or turn == slots - 1) and ready:
            keep = 0 if turn == slots - 1 else 1 if turn == per_stream else streams
            before, token, out = flush(ready[: len(ready) - keep], before, token, out)
            ready = ready[len(ready) - keep :]
    return out


def solution(mesh):
    return jax.shard_map(
        per_device,
        mesh=mesh,
        in_specs=(
            P(("groups", "seq"), ("head", "sub")),
            P(("groups", "seq"), None, ("head", "sub")),
            P(("head", "sub"), ("groups", "seq")),
            P(("head", "sub")),
            P(("head", "sub")),
            P(("head", "sub")),
            P(None, ("head", "sub")),
            P(("head", "sub")),
            P(None, None, ("head", "sub")),
            P(None, ("head", "sub")),
            P("groups"),
        ),
        out_specs=P(("groups", "seq"), ("head", "sub")),
        check_vma=False,
    )
```

```python
import functools
import math

import jax
import jax.numpy as jnp
from jax import lax
from jax.experimental import pallas as pl
from jax.experimental.pallas import tpu as pltpu
from jax.sharding import PartitionSpec as P

D = 128
Q = 128
BLK = 512
NQ = BLK // Q
HC = 4
CW = HC * D
PARTS = 2
PW = CW // PARTS
RIM = 8
LOG2E = math.log2(math.e)
F32 = jnp.float32
BF16 = jnp.bfloat16


def doc_of(pos, starts_ref):
    count = jnp.zeros_like(pos)
    for j in range(starts_ref.shape[0]):
        count = count + (pos >= starts_ref[j]).astype(jnp.int32)
    return count - 1


def silu_half(u):
    return u + u * jnp.tanh(u)


def doc_at(pos, starts_ref):
    count = jnp.int32(-1)
    for j in range(starts_ref.shape[0]):
        count = count + (pos >= starts_ref[j]).astype(jnp.int32)
    return count


def column_of(ref):
    heads = ref.shape[0]
    index = lax.broadcasted_iota(jnp.int32, (heads, 1), 0)
    column = jnp.zeros((heads, 1), F32)
    for h in range(heads):
        column = jnp.where(index == h, ref[h], column)
    return column


def split(value, parts):
    pieces = []
    for _ in range(parts - 1):
        piece = value.astype(BF16).astype(F32)
        pieces.append(piece)
        value = value - piece
    return pieces + [value]


def doc_at(pos, starts_ref):
    count = jnp.int32(-1)
    for j in range(starts_ref.shape[0]):
        count = count + (pos >= starts_ref[j]).astype(jnp.int32)
    return count


def column_of(ref):
    heads = ref.shape[0]
    index = lax.broadcasted_iota(jnp.int32, (heads, 1), 0)
    column = jnp.zeros((heads, 1), F32)
    for h in range(heads):
        column = jnp.where(index == h, ref[h], column)
    return column


def split(value, parts):
    pieces = []
    for _ in range(parts - 1):
        piece = value.astype(BF16).astype(F32)
        pieces.append(piece)
        value = value - piece
    return pieces + [value]


def doc_at(pos, starts_ref):
    count = jnp.int32(-1)
    for j in range(starts_ref.shape[0]):
        count = count + (pos >= starts_ref[j]).astype(jnp.int32)
    return count


def column_of(ref):
    heads = ref.shape[0]
    index = lax.broadcasted_iota(jnp.int32, (heads, 1), 0)
    column = jnp.zeros((heads, 1), F32)
    for h in range(heads):
        column = jnp.where(index == h, ref[h], column)
    return column


def split(value, parts):
    pieces = []
    for _ in range(parts - 1):
        piece = value.astype(BF16).astype(F32)
        pieces.append(piece)
        value = value - piece
    return pieces + [value]


def doc_at(pos, starts_ref):
    count = jnp.int32(-1)
    for j in range(starts_ref.shape[0]):
        count = count + (pos >= starts_ref[j]).astype(jnp.int32)
    return count


def column_of(ref):
    heads = ref.shape[0]
    index = lax.broadcasted_iota(jnp.int32, (heads, 1), 0)
    column = jnp.zeros((heads, 1), F32)
    for h in range(heads):
        column = jnp.where(index == h, ref[h], column)
    return column


def split(value, parts):
    pieces = []
    for _ in range(parts - 1):
        piece = value.astype(BF16).astype(F32)
        pieces.append(piece)
        value = value - piece
    return pieces + [value]


def doc_at(pos, starts_ref):
    count = jnp.int32(-1)
    for j in range(starts_ref.shape[0]):
        count = count + (pos >= starts_ref[j]).astype(jnp.int32)
    return count


def column_of(ref):
    heads = ref.shape[0]
    index = lax.broadcasted_iota(jnp.int32, (heads, 1), 0)
    column = jnp.zeros((heads, 1), F32)
    for h in range(heads):
        column = jnp.where(index == h, ref[h], column)
    return column


def split(value, parts):
    pieces = []
    for _ in range(parts - 1):
        piece = value.astype(BF16).astype(F32)
        pieces.append(piece)
        value = value - piece
    return pieces + [value]


def doc_at(pos, starts_ref):
    count = jnp.int32(-1)
    for j in range(starts_ref.shape[0]):
        count = count + (pos >= starts_ref[j]).astype(jnp.int32)
    return count


def column_of(ref):
    heads = ref.shape[0]
    index = lax.broadcasted_iota(jnp.int32, (heads, 1), 0)
    column = jnp.zeros((heads, 1), F32)
    for h in range(heads):
        column = jnp.where(index == h, ref[h], column)
    return column


def split(value, parts):
    pieces = []
    for _ in range(parts - 1):
        piece = value.astype(BF16).astype(F32)
        pieces.append(piece)
        value = value - piece
    return pieces + [value]


def doc_at(pos, starts_ref):
    count = jnp.int32(-1)
    for j in range(starts_ref.shape[0]):
        count = count + (pos >= starts_ref[j]).astype(jnp.int32)
    return count


def column_of(ref):
    heads = ref.shape[0]
    index = lax.broadcasted_iota(jnp.int32, (heads, 1), 0)
    column = jnp.zeros((heads, 1), F32)
    for h in range(heads):
        column = jnp.where(index == h, ref[h], column)
    return column


def split(value, parts):
    pieces = []
    for _ in range(parts - 1):
        piece = value.astype(BF16).astype(F32)
        pieces.append(piece)
        value = value - piece
    return pieces + [value]


def doc_at(pos, starts_ref):
    count = jnp.int32(-1)
    for j in range(starts_ref.shape[0]):
        count = count + (pos >= starts_ref[j]).astype(jnp.int32)
    return count


def column_of(ref):
    heads = ref.shape[0]
    index = lax.broadcasted_iota(jnp.int32, (heads, 1), 0)
    column = jnp.zeros((heads, 1), F32)
    for h in range(heads):
        column = jnp.where(index == h, ref[h], column)
    return column


def split(value, parts):
    pieces = []
    for _ in range(parts - 1):
        piece = value.astype(BF16).astype(F32)
        pieces.append(piece)
        value = value - piece
    return pieces + [value]


def doc_at(pos, starts_ref):
    count = jnp.int32(-1)
    for j in range(starts_ref.shape[0]):
        count = count + (pos >= starts_ref[j]).astype(jnp.int32)
    return count


def column_of(ref):
    heads = ref.shape[0]
    index = lax.broadcasted_iota(jnp.int32, (heads, 1), 0)
    column = jnp.zeros((heads, 1), F32)
    for h in range(heads):
        column = jnp.where(index == h, ref[h], column)
    return column


def split(value, parts):
    pieces = []
    for _ in range(parts - 1):
        piece = value.astype(BF16).astype(F32)
        pieces.append(piece)
        value = value - piece
    return pieces + [value]


def doc_at(pos, starts_ref):
    count = jnp.int32(-1)
    for j in range(starts_ref.shape[0]):
        count = count + (pos >= starts_ref[j]).astype(jnp.int32)
    return count


def column_of(ref):
    heads = ref.shape[0]
    index = lax.broadcasted_iota(jnp.int32, (heads, 1), 0)
    column = jnp.zeros((heads, 1), F32)
    for h in range(heads):
        column = jnp.where(index == h, ref[h], column)
    return column


def split(value, parts):
    pieces = []
    for _ in range(parts - 1):
        piece = value.astype(BF16).astype(F32)
        pieces.append(piece)
        value = value - piece
    return pieces + [value]


def doc_at(pos, starts_ref):
    count = jnp.int32(-1)
    for j in range(starts_ref.shape[0]):
        count = count + (pos >= starts_ref[j]).astype(jnp.int32)
    return count


def column_of(ref):
    heads = ref.shape[0]
    index = lax.broadcasted_iota(jnp.int32, (heads, 1), 0)
    column = jnp.zeros((heads, 1), F32)
    for h in range(heads):
        column = jnp.where(index == h, ref[h], column)
    return column


def split(value, parts):
    pieces = []
    for _ in range(parts - 1):
        piece = value.astype(BF16).astype(F32)
        pieces.append(piece)
        value = value - piece
    return pieces + [value]


def doc_at(pos, starts_ref):
    count = jnp.int32(-1)
    for j in range(starts_ref.shape[0]):
        count = count + (pos >= starts_ref[j]).astype(jnp.int32)
    return count


def column_of(ref):
    heads = ref.shape[0]
    index = lax.broadcasted_iota(jnp.int32, (heads, 1), 0)
    column = jnp.zeros((heads, 1), F32)
    for h in range(heads):
        column = jnp.where(index == h, ref[h], column)
    return column


def split(value, parts):
    pieces = []
    for _ in range(parts - 1):
        piece = value.astype(BF16).astype(F32)
        pieces.append(piece)
        value = value - piece
    return pieces + [value]


def doc_at(pos, starts_ref):
    count = jnp.int32(-1)
    for j in range(starts_ref.shape[0]):
        count = count + (pos >= starts_ref[j]).astype(jnp.int32)
    return count


def column_of(ref):
    heads = ref.shape[0]
    index = lax.broadcasted_iota(jnp.int32, (heads, 1), 0)
    column = jnp.zeros((heads, 1), F32)
    for h in range(heads):
        column = jnp.where(index == h, ref[h], column)
    return column


def split(value, parts):
    pieces = []
    for _ in range(parts - 1):
        piece = value.astype(BF16).astype(F32)
        pieces.append(piece)
        value = value - piece
    return pieces + [value]


def doc_at(pos, starts_ref):
    count = jnp.int32(-1)
    for j in range(starts_ref.shape[0]):
        count = count + (pos >= starts_ref[j]).astype(jnp.int32)
    return count


def column_of(ref):
    heads = ref.shape[0]
    index = lax.broadcasted_iota(jnp.int32, (heads, 1), 0)
    column = jnp.zeros((heads, 1), F32)
    for h in range(heads):
        column = jnp.where(index == h, ref[h], column)
    return column


def split(value, parts):
    pieces = []
    for _ in range(parts - 1):
        piece = value.astype(BF16).astype(F32)
        pieces.append(piece)
        value = value - piece
    return pieces + [value]


def doc_at(pos, starts_ref):
    count = jnp.int32(-1)
    for j in range(starts_ref.shape[0]):
        count = count + (pos >= starts_ref[j]).astype(jnp.int32)
    return count


def column_of(ref):
    heads = ref.shape[0]
    index = lax.broadcasted_iota(jnp.int32, (heads, 1), 0)
    column = jnp.zeros((heads, 1), F32)
    for h in range(heads):
        column = jnp.where(index == h, ref[h], column)
    return column


def split(value, parts):
    pieces = []
    for _ in range(parts - 1):
        piece = value.astype(BF16).astype(F32)
        pieces.append(piece)
        value = value - piece
    return pieces + [value]


def doc_at(pos, starts_ref):
    count = jnp.int32(-1)
    for j in range(starts_ref.shape[0]):
        count = count + (pos >= starts_ref[j]).astype(jnp.int32)
    return count


def column_of(ref):
    heads = ref.shape[0]
    index = lax.broadcasted_iota(jnp.int32, (heads, 1), 0)
    column = jnp.zeros((heads, 1), F32)
    for h in range(heads):
        column = jnp.where(index == h, ref[h], column)
    return column


def split(value, parts):
    pieces = []
    for _ in range(parts - 1):
        piece = value.astype(BF16).astype(F32)
        pieces.append(piece)
        value = value - piece
    return pieces + [value]


def doc_at(pos, starts_ref):
    count = jnp.int32(-1)
    for j in range(starts_ref.shape[0]):
        count = count + (pos >= starts_ref[j]).astype(jnp.int32)
    return count


def column_of(ref):
    heads = ref.shape[0]
    index = lax.broadcasted_iota(jnp.int32, (heads, 1), 0)
    column = jnp.zeros((heads, 1), F32)
    for h in range(heads):
        column = jnp.where(index == h, ref[h], column)
    return column


def split(value, parts):
    pieces = []
    for _ in range(parts - 1):
        piece = value.astype(BF16).astype(F32)
        pieces.append(piece)
        value = value - piece
    return pieces + [value]


def doc_at(pos, starts_ref):
    count = jnp.int32(-1)
    for j in range(starts_ref.shape[0]):
        count = count + (pos >= starts_ref[j]).astype(jnp.int32)
    return count


def column_of(ref):
    heads = ref.shape[0]
    index = lax.broadcasted_iota(jnp.int32, (heads, 1), 0)
    column = jnp.zeros((heads, 1), F32)
    for h in range(heads):
        column = jnp.where(index == h, ref[h], column)
    return column


def split(value, parts):
    pieces = []
    for _ in range(parts - 1):
        piece = value.astype(BF16).astype(F32)
        pieces.append(piece)
        value = value - piece
    return pieces + [value]


def doc_at(pos, starts_ref):
    count = jnp.int32(-1)
    for j in range(starts_ref.shape[0]):
        count = count + (pos >= starts_ref[j]).astype(jnp.int32)
    return count


def column_of(ref):
    heads = ref.shape[0]
    index = lax.broadcasted_iota(jnp.int32, (heads, 1), 0)
    column = jnp.zeros((heads, 1), F32)
    for h in range(heads):
        column = jnp.where(index == h, ref[h], column)
    return column


def split(value, parts):
    pieces = []
    for _ in range(parts - 1):
        piece = value.astype(BF16).astype(F32)
        pieces.append(piece)
        value = value - piece
    return pieces + [value]


def doc_at(pos, starts_ref):
    count = jnp.int32(-1)
    for j in range(starts_ref.shape[0]):
        count = count + (pos >= starts_ref[j]).astype(jnp.int32)
    return count


def column_of(ref):
    heads = ref.shape[0]
    index = lax.broadcasted_iota(jnp.int32, (heads, 1), 0)
    column = jnp.zeros((heads, 1), F32)
    for h in range(heads):
        column = jnp.where(index == h, ref[h], column)
    return column


def split(value, parts):
    pieces = []
    for _ in range(parts - 1):
        piece = value.astype(BF16).astype(F32)
        pieces.append(piece)
        value = value - piece
    return pieces + [value]


def doc_at(pos, starts_ref):
    count = jnp.int32(-1)
    for j in range(starts_ref.shape[0]):
        count = count + (pos >= starts_ref[j]).astype(jnp.int32)
    return count


def column_of(ref):
    heads = ref.shape[0]
    index = lax.broadcasted_iota(jnp.int32, (heads, 1), 0)
    column = jnp.zeros((heads, 1), F32)
    for h in range(heads):
        column = jnp.where(index == h, ref[h], column)
    return column


def split(value, parts):
    pieces = []
    for _ in range(parts - 1):
        piece = value.astype(BF16).astype(F32)
        pieces.append(piece)
        value = value - piece
    return pieces + [value]


def doc_at(pos, starts_ref):
    count = jnp.int32(-1)
    for j in range(starts_ref.shape[0]):
        count = count + (pos >= starts_ref[j]).astype(jnp.int32)
    return count


def column_of(ref):
    heads = ref.shape[0]
    index = lax.broadcasted_iota(jnp.int32, (heads, 1), 0)
    column = jnp.zeros((heads, 1), F32)
    for h in range(heads):
        column = jnp.where(index == h, ref[h], column)
    return column


def split(value, parts):
    pieces = []
    for _ in range(parts - 1):
        piece = value.astype(BF16).astype(F32)
        pieces.append(piece)
        value = value - piece
    return pieces + [value]


def params_kernel(
    starts_ref, bias_ref, alog_ref, skip_ref, dt_ref, far_x_ref,
    scale_ref, cols_ref, rows_ref, fade_ref, shift_ref, keep_ref, x_ref, sem,
):
    copies = []
    width = x_ref.shape[1]
    for part in range(4):
        lanes = pl.ds(part * (width // 4), width // 4)
        copies.append(pltpu.make_async_copy(far_x_ref.at[:, lanes], x_ref.at[:, lanes], sem.at[part]))
        copies[-1].start()
    first = lax.axis_index("seq") * BLK
    heads = dt_ref.shape[0]
    v = dt_ref[...] + column_of(bias_ref)
    step = jnp.maximum(v, 0.0) + jnp.log(1.0 + jnp.exp(-jnp.abs(v)))
    rate = -jnp.exp(column_of(alog_ref)) * step
    tri = (
        lax.broadcasted_iota(jnp.int32, (Q, Q), 0) <= lax.broadcasted_iota(jnp.int32, (Q, Q), 1)
    ).astype(F32)
    doc_before = doc_at(first - 1, starts_ref)
    doc_last = doc_at(first + BLK - 1, starts_ref)
    cums = []
    base = jnp.zeros((heads, 1), F32)
    for q in range(NQ):
        part = jnp.dot(
            rate[:, q * Q : (q + 1) * Q], tri, precision=lax.Precision.HIGHEST, preferred_element_type=F32
        )
        cums.append(part + base)
        base = base + part[:, Q - 1 : Q]
    for q in range(NQ):
        span = slice(q * Q, (q + 1) * Q)
        cum = cums[q]
        step_q = step[:, span]
        pos = first + q * Q + lax.broadcasted_iota(jnp.int32, (1, Q), 1)
        doc = doc_of(pos, starts_ref)
        tail = jnp.where(doc == doc_last, jnp.exp(base - cum) * step_q, 0.0)
        entry = jnp.where(doc == doc_before, jnp.exp(cum), 0.0)
        rest = jnp.zeros((D - 2 * heads, Q), F32)
        packed = split(tail, 2) + [rest]
        scale_ref[span, :] = jnp.transpose(jnp.concatenate(packed, axis=0), (1, 0)).astype(BF16)
        packed = [cum * LOG2E, entry, rest]
        cols_ref[span, :] = jnp.transpose(jnp.concatenate(packed, axis=0), (1, 0))
        terms = (cum - jnp.log(step_q)) * LOG2E
        for c in range(heads // HC):
            rows_ref[c, :, span] = terms[c * HC : (c + 1) * HC]
    decay = jnp.exp(base) * jnp.where(doc_last == doc_before, 1.0, 0.0)
    skip = column_of(skip_ref)
    for c in range(heads // HC):
        for i in range(HC):
            h = c * HC + i
            lanes = slice(i * D, (i + 1) * D)
            fade_ref[c, 0:1, lanes] = jnp.broadcast_to(skip[h : h + 1], (1, D))
            fade_ref[c, 1:2, lanes] = jnp.broadcast_to(decay[h : h + 1], (1, D))
    for q in range(NQ):
        row = lax.broadcasted_iota(jnp.int32, (Q, 2 * Q), 0)
        col = lax.broadcasted_iota(jnp.int32, (Q, 2 * Q), 1) - Q
        at = first + q * Q
        same = doc_of(at + row, starts_ref) == doc_of(at + col, starts_ref)
        for k in range(3):
            hit = same & (col == row - (3 - k))
            shift_ref[q, k * Q : (k + 1) * Q, :] = jnp.where(hit, 1.0, 0.0).astype(BF16)
        doc_row = doc_of(at + lax.broadcasted_iota(jnp.int32, (Q, BLK), 0), starts_ref)
        col = lax.broadcasted_iota(jnp.int32, (Q, BLK), 1)
        row = q * Q + lax.broadcasted_iota(jnp.int32, (Q, BLK), 0)
        keep = (row >= col) & (doc_row == doc_of(first + col, starts_ref))
        keep_ref[q * Q : (q + 1) * Q, :] = jnp.where(keep, 1.0, 0.0)
    for copy in copies:
        copy.wait()


def chooser(heads, chunk, lo, hi, width):
    k = lax.broadcasted_iota(jnp.int32, (D, width), 0)
    head = HC * chunk + lax.broadcasted_iota(jnp.int32, (D, width), 1) // D
    hit = ((k & (heads - 1)) == head) & (k >= lo * heads) & (k < hi * heads)
    return jnp.where(hit, 1.0, 0.0).astype(BF16)


def convolved(q, window, now, shift_ref, taps, bias):
    moved = jnp.dot(shift_ref[q], window, preferred_element_type=F32)
    total = (0.5 * taps[3]) * now.astype(F32) + 0.5 * bias
    for k in range(3):
        total = total + (0.5 * taps[k]) * moved[k * Q : (k + 1) * Q]
    return silu_half(total)


def window_of(q, edge_ref, x_ref):
    return edge_ref[...] if q == 0 else x_ref[(q - 1) * Q : (q + 1) * Q, :]


def edge(edge_ref, rim, x):
    width = x.shape[1]
    if rim is None:
        rim = jnp.zeros((Q, width), F32)
    else:
        rim = jnp.concatenate([jnp.zeros((Q - RIM, width), F32), rim.astype(F32)], axis=0)
    edge_ref[0:Q, 0:width] = rim.astype(BF16)
    edge_ref[Q : 2 * Q, 0:width] = x


def state_of(
    chunk, heads, x_ref, rim, wx_ref, bx_ref, shift_ref, scale_ref, bt, edge_ref, tail_ref, mx_ref=None
):
    wide = slice(chunk * CW, (chunk + 1) * CW)
    edge(edge_ref, rim, x_ref[0:Q, :])
    pick = chooser(heads, chunk, 0, 2, CW)
    taps = [wx_ref[k : k + 1, wide] for k in range(4)]
    for q in range(NQ):
        span = slice(q * Q, (q + 1) * Q)
        window = x_ref[(q - 1) * Q : (q + 1) * Q, :] if q else edge_ref[:, 0:CW]
        mixed = convolved(q, window, x_ref[span, :], shift_ref, taps, bx_ref[:, wide])
        if mx_ref is not None:
            mx_ref[chunk, span, :] = mixed.astype(BF16)
        scale = jnp.dot(scale_ref[span, :], pick, preferred_element_type=F32)
        tail_ref[span, :] = (mixed * scale).astype(BF16)
    return jnp.dot(bt, tail_ref[...], preferred_element_type=F32)


def chunk_of(x_ref, chunk):
    return x_ref.at[:, pl.ds(chunk * CW, CW)]


def mixed_of(q, part, edge_ref, bc_ref, shift_ref, wbc_ref, bbc_ref, wide):
    half = slice(part * wide, (part + 1) * wide)
    window = bc_ref[(q - 1) * Q : (q + 1) * Q, half] if q else edge_ref[:, 0:wide]
    taps = [wbc_ref[k, part : part + 1, :] for k in range(4)]
    return convolved(q, window, bc_ref[q * Q : (q + 1) * Q, half], shift_ref, taps, bbc_ref[part : part + 1, :])


def first_kernel(
    x_ref, rim_ref, wx_ref, bx_ref, shift_ref, scale_ref, bc_ref, wbc_ref, bbc_ref,
    mx_ref, end_ref, send_ref, bt_ref, edge_ref, tail_ref, *, heads,
):
    groups = bt_ref.shape[0]
    wide = groups * D
    start = x_ref.shape[1]
    edge(edge_ref, rim_ref[:, start : start + wide], bc_ref[0:Q, 0:wide])
    for q in range(NQ):
        mixed = mixed_of(q, 0, edge_ref, bc_ref, shift_ref, wbc_ref, bbc_ref, wide)
        for g in range(groups):
            bt_ref[g, :, q * Q : (q + 1) * Q] = jnp.transpose(mixed[:, g * D : (g + 1) * D], (1, 0)).astype(BF16)
    state = state_of(
        0, heads, chunk_of(x_ref, 0), rim_ref[:, 0:CW], wx_ref, bx_ref, shift_ref, scale_ref, bt_ref[0],
        edge_ref, tail_ref, mx_ref,
    )
    end_ref[0] = state
    send_ref[...] = state.astype(BF16)


def score_kernel(
    rim_ref, shift_ref, keep_ref, bc_ref, wbc_ref, bbc_ref, bt_ref, after_ref, c_ref, score_ref, edge_ref
):
    groups = bt_ref.shape[0]
    wide = groups * D
    start = rim_ref.shape[1] - wide
    edge(edge_ref, rim_ref[:, start:], bc_ref[0:Q, wide:])
    for q in range(NQ):
        span = slice(q * Q, (q + 1) * Q)
        upto = (q + 1) * Q
        mixed = mixed_of(q, 1, edge_ref, bc_ref, shift_ref, wbc_ref, bbc_ref, wide)
        for g in range(groups):
            c = mixed[:, g * D : (g + 1) * D].astype(BF16)
            c_ref[g, span, :] = c
            score = jnp.dot(c, bt_ref[g, :, 0:upto], preferred_element_type=F32)
            score_ref[g, span, 0:upto] = keep_ref[span, 0:upto] * score


def more_kernel(
    x_ref, rim_ref, wx_ref, bx_ref, shift_ref, scale_ref, bt_ref, old1, old2,
    mx_ref, end_ref, *rest, heads, per_group, some,
):
    edge_ref, tail_ref = rest[-2:]
    for chunk in some:
        wide = slice(chunk * CW, (chunk + 1) * CW)
        state = state_of(
            chunk, heads, chunk_of(x_ref, chunk), rim_ref[:, wide], wx_ref, bx_ref, shift_ref, scale_ref,
            bt_ref[chunk // per_group], edge_ref, tail_ref, mx_ref,
        )
        end_ref[chunk] = state
        for send_ref in rest[:-2]:
            send_ref[...] = state.astype(BF16)


def join_kernel(fade_ref, recv_ref, end_ref, token_ref, send_ref, *, turn, stream, per_stream):
    chunk = stream * per_stream + jnp.clip(turn - lax.axis_index("seq"), 0, per_stream - 1)
    send_ref[...] = (fade_ref[chunk, 1:2, :] * recv_ref[...].astype(F32) + end_ref[chunk]).astype(BF16)


def out_kernel(
    fade_ref, mx_ref, c_ref, score_ref, cols_ref, rows_ref, recv_ref,
    *rest, turn, stream, before, final, per_stream, per_group, heads,
):
    out_ref, block_ref, sem = rest[-3:]
    place = lax.axis_index("seq")

    def spot(when, which):
        chunk = which * per_stream + jnp.clip(when - place, 0, per_stream - 1)
        return pl.ds(pl.multiple_of(chunk * CW, CW), CW)

    def is_valid(when):
        return (when - place >= 0) & (when - place < per_stream)

    def half_copy(ref, when, which, half):
        rows = pl.ds(half * 2 * Q, 2 * Q)
        return pltpu.make_async_copy(ref.at[rows, :], out_ref.at[rows, spot(when, which)], sem.at[half])

    if before:
        @pl.when(is_valid(before[0]))
        def send():
            for half in range(2):
                half_copy(rest[0], *before, half).start()

    @pl.when(is_valid(turn))
    def compute():
        chunk = stream * per_stream + turn - place
        g = lax.div(chunk, per_group)
        cols = pltpu.roll(cols_ref[...], lax.rem(D - HC * chunk, D), 1)
        far = jnp.dot(c_ref[g], recv_ref[...], preferred_element_type=F32)
        zero = jnp.zeros((Q, Q), BF16)
        last = []
        for i in range(HC):
            lanes = slice(i * D, (i + 1) * D)
            cum = jnp.broadcast_to(cols[:, i : i + 1], (BLK, Q))
            entry = jnp.broadcast_to(cols[:, heads + i : heads + i + 1], (BLK, Q))
            tiles = []
            for q in range(NQ):
                span = slice(q * Q, (q + 1) * Q)
                line = []
                for j in range(q + 1):
                    there = slice(j * Q, (j + 1) * Q)
                    gap = cum[span] - rows_ref[chunk, i : i + 1, there]
                    if j == q:
                        gap = jnp.minimum(gap, 100.0)
                    line.append((score_ref[g, span, there] * jnp.exp2(gap)).astype(BF16))
                tiles.append(line + [zero] * (NQ - 1 - q))

            def weights(lines, halves):
                return jnp.concatenate([jnp.concatenate([tiles[q][j] for j in halves], axis=1) for q in lines], axis=0)

            left = jnp.dot(weights(range(NQ), (0, 1)), mx_ref[chunk, 0 : 2 * Q, lanes], preferred_element_type=F32)
            right = jnp.dot(weights((2, 3), (2, 3)), mx_ref[chunk, 2 * Q :, lanes], preferred_element_type=F32)
            for half in range(2):
                span = slice(half * 2 * Q, (half + 1) * 2 * Q)
                y = left[span] + right if half else left[span]
                x = mx_ref[chunk, span, lanes].astype(F32)
                y = y + entry[span] * far[span, lanes] + fade_ref[chunk, 0:1, lanes] * x
                block_ref[span, lanes] = y.astype(BF16)
            if final:
                there = pl.ds(pl.multiple_of(chunk * CW + i * D, D), D)
                last.append(
                    pltpu.make_async_copy(block_ref.at[:, pl.ds(i * D, D)], out_ref.at[:, there], sem.at[2 + i])
                )
                last[-1].start()
        for copy in last:
            copy.wait()

    if before:
        @pl.when(is_valid(before[0]))
        def wait():
            for half in range(2):
                half_copy(rest[0], *before, half).wait()


SMEM = pl.BlockSpec(memory_space=pltpu.SMEM)
ROOM = pltpu.CompilerParams(vmem_limit_bytes=16 * 2**20)
ANY = pl.BlockSpec(memory_space=pl.ANY)
VMEM = pl.BlockSpec(memory_space=pltpu.VMEM)


def whole(shape):
    return pl.BlockSpec(shape, lambda *_: (0,) * len(shape))


def shape_of(shape, dtype):
    return jax.ShapeDtypeStruct(shape, dtype)


def per_device(
    x_raw, bc_raw, dt_raw, dt_bias, a_log, d_skip, conv_x, conv_x_bias, conv_bc, conv_bc_bias, doc_starts
):
    rows, width = x_raw.shape
    held = [x_raw, dt_raw, dt_bias, a_log, d_skip, conv_bc, conv_bc_bias, doc_starts]
    held = [pltpu.with_memory_space_constraint(a, pltpu.HBM) for a in held]
    x_far, dt_raw, dt_bias, a_log, d_skip, conv_bc, conv_bc_bias, doc_starts = held
    bias_x = conv_x_bias[None]
    groups = bc_raw.shape[2] // D
    heads = dt_raw.shape[0]
    chunks = heads // HC
    per_group = chunks // groups
    seq = lax.axis_size("seq")
    ring = [(i, (i + 1) % seq) for i in range(seq)]
    cores = lax.axis_size("sub")

    def hop(slot, send):
        low, high = max(0, slot - per_stream + 1), min(slot, seq - 2)
        pairs = []
        for place in range(seq):
            for core in range(cores):
                if low <= place <= high + 1:
                    to = (place + 1 if place <= high else low) * cores + core
                else:
                    to = place * cores + (core + 1) % cores
                pairs.append((place * cores + core, to))
        return lax.ppermute(send, ("seq", "sub"), pairs)

    streams = 2
    per_stream = chunks // streams
    slots = per_stream + seq - 2

    tail = jnp.concatenate([x_raw[rows - RIM :], bc_raw[rows - RIM :].reshape(RIM, -1)], axis=1)
    rim = lax.ppermute(tail, "seq", ring)
    bc = bc_raw.reshape(rows, -1)

    scale, cols, row_terms, fade, shift, keep, x_near = pl.pallas_call(
        params_kernel,
        in_specs=[SMEM] * 4 + [VMEM, ANY],
        out_specs=[VMEM] * 7,
        out_shape=[
            shape_of((BLK, D), BF16),
            shape_of((BLK, D), F32),
            shape_of((chunks, HC, BLK), F32),
            shape_of((chunks, 2, CW), F32),
            shape_of((NQ, 3 * Q, 2 * Q), BF16),
            shape_of((BLK, BLK), F32),
            pltpu.VMEM((rows, width), BF16),
        ],
        scratch_shapes=[pltpu.SemaphoreType.DMA((4,))],
        compiler_params=ROOM,
        name="params",
    )(doc_starts, dt_bias, a_log, d_skip, dt_raw, x_far)

    big = [pltpu.VMEM((chunks, BLK, CW), BF16), pltpu.VMEM((chunks, D, CW), F32)]
    chunk_shape = shape_of((D, CW), BF16)
    bt_shape = shape_of((groups, D, BLK), BF16)
    scratch = [pltpu.VMEM((2 * Q, max(CW, 2 * groups * D)), BF16), pltpu.VMEM((BLK, CW), BF16)]

    mixed_x, end, send, bt = pl.pallas_call(
        functools.partial(first_kernel, heads=heads),
        in_specs=[VMEM] * 9,
        out_specs=[VMEM] * 4,
        out_shape=[*big, chunk_shape, bt_shape],
        scratch_shapes=scratch,
        compiler_params=ROOM,
        name="first",
    )(x_near, rim, conv_x, bias_x, shift, scale, bc, conv_bc, conv_bc_bias)

    def near(array):
        return pltpu.with_memory_space_constraint(array, pltpu.VMEM)

    def more(some, sends, mixed_x, end):
        return pl.pallas_call(
            functools.partial(more_kernel, heads=heads, per_group=per_group, some=some),
            in_specs=[VMEM] * 9,
            out_specs=[VMEM] * (2 + sends),
            out_shape=big + [chunk_shape] * sends,
            input_output_aliases={7: 0, 8: 1},
            scratch_shapes=scratch,
            compiler_params=ROOM,
            cost_estimate=pl.CostEstimate(
                flops=4 * len(some) * BLK * D * CW, bytes_accessed=4 * len(some) * BLK * CW, transcendentals=0
            ),
            name="more",
        )(x_near, rim, conv_x, bias_x, shift, scale, bt, near(mixed_x), near(end))

    begun = [send]
    flying = [hop(0, send)]
    for s in range(1, streams):
        mixed_x, end, send = more([s * per_stream], 1, mixed_x, end)
        begun.append(send)
        flying.append(hop(0, send))

    def scores(after):
        return pl.pallas_call(
            score_kernel,
            in_specs=[VMEM] * 7 + [ANY],
            out_specs=[VMEM] * 2,
            out_shape=[shape_of((groups, BLK, D), BF16), shape_of((groups, BLK, BLK), F32)],
            scratch_shapes=scratch[:1],
            compiler_params=ROOM,
            name="score",
        )(rim, shift, keep, bc, conv_bc, conv_bc_bias, bt, after)

    def join(turn, s, recv, token):
        return pl.pallas_call(
            functools.partial(join_kernel, turn=turn, stream=s, per_stream=per_stream),
            in_specs=[VMEM, VMEM, VMEM, ANY],
            out_specs=VMEM,
            out_shape=chunk_shape,
            compiler_params=ROOM,
            name="join",
        )(fade, recv, end, token)

    def output(turn, s, recv, before, block, out, mixed_c, score):
        old = [] if out is None else [last_block[-1], out, block]
        return pl.pallas_call(
            functools.partial(
                out_kernel, turn=turn, stream=s, before=before, final=turn == slots and s == streams - 1,
                per_stream=per_stream, per_group=per_group, heads=heads,
            ),
            in_specs=[VMEM] * 7 + [VMEM, ANY, ANY][: len(old)],
            out_specs=[ANY, VMEM],
            out_shape=[pltpu.HBM((BLK, width), BF16), shape_of((BLK, CW), BF16)],
            input_output_aliases={8: 0} if old else {},
            scratch_shapes=[pltpu.SemaphoreType.DMA((2 + HC,))],
            compiler_params=ROOM,
            cost_estimate=pl.CostEstimate(
                flops=8 * BLK * Q * CW, bytes_accessed=6 * BLK * CW, transcendentals=0
            ),
            name="out",
        )(fade, mixed_x, mixed_c, score, cols, row_terms, recv, *old)

    out, before = None, None
    last_block = []
    waiting = [(0, s, begun[s]) for s in range(streams)]
    token = bt
    ready = []

    def flush(ready, before, token, out):
        for when, which, got in ready:
            out, token = output(when, which, got, before, token, out, mixed_c, score)
            last_block.append(token)
            before = (when, which)
        return before, token, out

    for turn in range(1, slots + 1):
        for s in range(streams):
            if turn < per_stream:
                mixed_x, end = more([turn + s * per_stream], 0, mixed_x, end)
            got = flying[s]
            if turn < slots:
                send = join(turn, s, got, token)
                flying[s] = hop(turn, send)
                token = send
            elif s == 0:
                ready = waiting + ready
                waiting = []
            ready.append((turn, s, got))
            if (turn > per_stream and turn != slots - 1) or turn == slots:
                before, token, out = flush(ready, before, token, out)
                ready = []
        if turn == 1:
            mixed_c, score = scores(send)
            token = score
        if turn == per_stream - 1:
            ready, waiting = waiting + ready, []
        if (turn <= per_stream or turn == slots - 1) and ready:
            keep = 0 if turn == slots - 1 else 1 if turn == per_stream else streams
            before, token, out = flush(ready[: len(ready) - keep], before, token, out)
            ready = ready[len(ready) - keep :]
    return out


def solution(mesh):
    return jax.shard_map(
        per_device,
        mesh=mesh,
        in_specs=(
            P(("groups", "seq"), ("head", "sub")),
            P(("groups", "seq"), None, ("head", "sub")),
            P(("head", "sub"), ("groups", "seq")),
            P(("head", "sub")),
            P(("head", "sub")),
            P(("head", "sub")),
            P(None, ("head", "sub")),
            P(("head", "sub")),
            P(None, None, ("head", "sub")),
            P(None, ("head", "sub")),
            P("groups"),
        ),
        out_specs=P(("groups", "seq"), ("head", "sub")),
        check_vma=False,
    )
```
